32 devices in a mesh: dp: 8 (over z, y), seq: 4 (over x, core).
Axes of the slice: x: 2, y: 2, z: 4, core: 2. Of those that a mesh axis runs over, the one named last changes fastest.
Arguments:
- tokens: bfloat16 [16, 1024, 1536], P(None, ('dp', 'seq')), may hold values from -6 to 6
- cotangent: bfloat16 [16, 1024, 1536], P(None, ('dp', 'seq')), may hold values from -6 to 6
- routes: int32 [16, 1024, 8], P(None, ('dp', 'seq')), may hold values from 0 to 11, as said below
- lengths: int32 [16], replicated, may hold values from 128 to 1024, as said below
- deal_order: int32 [16], replicated, may hold values from 0 to 15, as said below
- attn_gain: float32 [1536], P('dp'), may hold values from 0.5 to 1.5
- query_weight: float32 [1536, 1536], P('dp'), may hold values from -0.15625 to 0.15625
- key_matrix: float32 [1536, 512], P('dp'), may hold values from -0.15625 to 0.15625
- value_matrix: float32 [1536, 512], P('dp'), may hold values from -0.15625 to 0.15625
- out_weight: float32 [1536, 1536], P('dp'), may hold values from -1.75 to 1.75
- moe_gain: float32 [1536], P('dp'), may hold values from 0.5 to 1.5
- router_weight: float32 [1536, 12], P('dp'), may hold values from -0.078125 to 0.078125
- expert_weight: float32 [1536, 12, 1536], P('dp'), may hold values from -0.3125 to 0.3125
Outputs:
- output: float32 [16, 1024, 1536], P(None, ('dp', 'seq'))
- grad_tokens: float32 [16, 1024, 1536], P(None, ('dp', 'seq'))
- grad_attn_gain: float32 [1536], P('dp')
- grad_query: float32 [1536, 1536], P('dp')
- grad_key: float32 [1536, 512], P('dp')
- grad_value: float32 [1536, 512], P('dp')
- grad_out: float32 [1536, 1536], P('dp')
- grad_moe_gain: float32 [1536], P('dp')
- grad_router: float32 [1536, 12], P('dp')
- grad_experts: float32 [1536, 12, 1536], P('dp')
The draws below stay inside these ranges and needn't reach their ends.
Inputs may be any that keep to these rules, and one draw needn't show every extreme that they name: Every length is a multiple of 128; lengths[deal_order[2k]] + lengths[deal_order[2k+1]] = 1152 for every k; some length equals 1024. `deal_order`: A permutation of the sequences. `routes`: each row names 8 different experts. For each g < 8 and s < 4, take the slots p < length of the sequences deal_order[2g] and deal_order[2g + 1] with (p // 32) % 4 == s: among these rows each expert is named at most 216 times, and some expert exactly 216 times.
All inputs are finite; a program needn't handle non-finite values.
Results may differ from the reference program's by a relative error of at most 0.023.
Values may be sent and summed in bfloat16 or wider, within the bound.
No kernel may reach another device: no remote copies, remote signals or barrier semaphores. Data moves between devices by JAX's collectives and lax.ppermute only.
A program may use at most 640 MiB of HBM per device.

```python
import jax
import jax.numpy as jnp
from jax import lax

MODEL_WIDTH = 1536
QUERY_HEADS = 24
KEY_VALUE_HEADS = 8
HEAD_SIZE = 64
F = 512
TOPK = 8
EXPERTS = 12
LMAX = 1024
PAIR_TOK = 1152
PAIRS = 1
SEQS = 16
BLK = 32
UNIT = 128


def pair_plan(key):
    lowest = (PAIR_TOK - LMAX) // UNIT
    highest = LMAX // UNIT
    item_count = SEQS // 2
    first_units = jax.random.randint(jax.random.fold_in(key, 11), (item_count,), lowest, highest + 1)
    first_units = first_units.at[0].set(highest)
    swapped = jax.random.randint(jax.random.fold_in(key, 12), (item_count,), 0, 2)
    first_len = first_units * UNIT
    lead_len = jnp.where(swapped > 0, PAIR_TOK - first_len, first_len)
    dealt_len = jnp.stack([lead_len, PAIR_TOK - lead_len], axis=1).reshape(SEQS)
    order = jax.random.permutation(jax.random.fold_in(key, 13), SEQS).astype(jnp.int32)
    seq_lengths = jnp.zeros((SEQS,), jnp.int32).at[order].set(dealt_len.astype(jnp.int32))
    return (seq_lengths, order)


def draw_lengths(key, part):
    return pair_plan(key)[0]


def draw_deal_order(key, part):
    return pair_plan(key)[1]


def draw_routes(key, part):
    seq_lengths, order = pair_plan(key)
    groups = SEQS // (2 * PAIRS)
    members = LMAX // (BLK * groups)
    quarter_tok = PAIR_TOK // members
    grid_shape = (groups, members, PAIRS, quarter_tok)
    group_idx = jnp.arange(groups, dtype=jnp.int32)[:, None, None, None]
    member_idx = jnp.arange(members, dtype=jnp.int32)[None, :, None, None]
    pair_idx = jnp.arange(PAIRS, dtype=jnp.int32)[None, None, :, None]
    row_idx = jnp.arange(quarter_tok, dtype=jnp.int32)[None, None, None, :]
    first_slot = group_idx * 2 * PAIRS + 2 * pair_idx
    first_count = seq_lengths[order[first_slot]] // members
    second_half = (row_idx >= first_count).astype(jnp.int32)
    slot_index = first_slot + second_half
    local_row = row_idx - first_count * second_half
    token_position = local_row // BLK * members * BLK + member_idx * BLK + local_row % BLK
    token_position = jnp.broadcast_to(token_position, grid_shape)
    sequence = jnp.broadcast_to(order[slot_index], grid_shape)
    rank_scores = jax.random.randint(jax.random.fold_in(key, 21), grid_shape, 0, 2 ** 20) * quarter_tok + row_idx
    rank_value = jnp.argsort(rank_scores, axis=-1).astype(jnp.int32)
    quarter = rank_value % 4
    expert_ids = jnp.arange(EXPERTS, dtype=jnp.int32)
    expert_scores = jax.random.randint(jax.random.fold_in(key, 22), (groups, members, EXPERTS), 0, 2 ** 20) * EXPERTS + expert_ids
    expert_order = jnp.argsort(expert_scores, axis=-1).astype(jnp.int32)
    place = jnp.argsort(expert_order, axis=-1).astype(jnp.int32)
    expert_quarter = place // (EXPERTS // 4)
    forced = expert_order[:, :, 0]
    base_score = jax.random.randint(jax.random.fold_in(key, 23), grid_shape + (EXPERTS,), 0, 2 ** 16)
    excluded = expert_quarter[:, :, None, None, :] == quarter[..., None]
    pushed = (expert_ids == forced[:, :, None, None, None]) & (quarter[..., None] != 0)
    choice_score = jnp.where(excluded, -1, jnp.where(pushed, 2 ** 17, base_score)) * EXPERTS + expert_ids
    picked = lax.top_k(choice_score, TOPK)[1].astype(jnp.int32)
    filler_scores = jax.random.randint(jax.random.fold_in(key, 24), (SEQS, LMAX, EXPERTS), 0, 2 ** 16) * EXPERTS + expert_ids
    filler = lax.top_k(filler_scores, TOPK)[1].astype(jnp.int32)
    filled = filler.at[sequence.reshape(-1), token_position.reshape(-1)].set(picked.reshape(-1, TOPK))
    return filled.astype(jnp.int32)


def block_levels(own_key, extent, pieces, low, top_value):
    level = 1.0
    for axis_at, blocks in pieces:
        draws = jax.random.uniform(jax.random.fold_in(jax.random.fold_in(own_key, 6), axis_at), (blocks,), jnp.float32, low / len(pieces), top_value / len(pieces))
        level = level * jnp.repeat(jnp.exp(draws), extent[axis_at] // blocks).reshape((-1,) + (1,) * (len(extent) - 1 - axis_at))
    return level


def normal_values(rng, shape, spread, limit, pieces=(), kind=jnp.bfloat16):
    factor_of = block_levels(rng, shape, pieces, -0.22, 0.18) if pieces else 1.0
    values = jax.random.normal(rng, shape, jnp.float32) * spread * factor_of
    return jnp.minimum(jnp.maximum(values, -limit), limit).astype(kind)


def setup_inputs(seed: int = 0) -> dict:
    key_of = jax.random.split(jax.random.key(seed), 14)
    tokens = normal_values(key_of[0], (SEQS, LMAX, MODEL_WIDTH), 1.0, 6.0, ((1, 32),))
    cotangent = normal_values(key_of[1], (SEQS, LMAX, MODEL_WIDTH), 1.0, 6.0, ((1, 32),))
    routes = draw_routes(jax.random.fold_in(key_of[13], 71), 0)
    lengths = draw_lengths(jax.random.fold_in(key_of[13], 71), 0)
    deal_order = draw_deal_order(jax.random.fold_in(key_of[13], 71), 0)
    attn_gain = jnp.clip(1.0 + 0.1 * jax.random.normal(key_of[5], (MODEL_WIDTH,), jnp.float32), 0.5, 1.5)
    query_weight = normal_values(key_of[6], (MODEL_WIDTH, QUERY_HEADS * HEAD_SIZE), MODEL_WIDTH ** -0.5, 0.15625, ((0, 8),), jnp.float32)
    key_matrix = normal_values(key_of[7], (MODEL_WIDTH, KEY_VALUE_HEADS * HEAD_SIZE), MODEL_WIDTH ** -0.5, 0.15625, ((0, 8),), jnp.float32)
    value_matrix = normal_values(key_of[8], (MODEL_WIDTH, KEY_VALUE_HEADS * HEAD_SIZE), MODEL_WIDTH ** -0.5, 0.15625, ((0, 8),), jnp.float32)
    out_weight = normal_values(key_of[9], (QUERY_HEADS * HEAD_SIZE, MODEL_WIDTH), (max(MODEL_WIDTH // 128, 1)) ** -0.5, 1.75, ((0, 8),), jnp.float32)
    moe_gain = jnp.clip(1.0 + 0.1 * jax.random.normal(key_of[10], (MODEL_WIDTH,), jnp.float32), 0.5, 1.5)
    router_weight = normal_values(key_of[11], (MODEL_WIDTH, EXPERTS), (4 * MODEL_WIDTH) ** -0.5, 0.078125, ((0, 8),), jnp.float32)
    expert_weight = normal_values(key_of[12], (MODEL_WIDTH, EXPERTS, 3 * F), (MODEL_WIDTH // 4) ** -0.5, 0.3125, ((0, 8),), jnp.float32)
    return {"tokens": tokens, "cotangent": cotangent, "routes": routes, "lengths": lengths, "deal_order": deal_order, "attn_gain": attn_gain, "query_weight": query_weight, "key_matrix": key_matrix, "value_matrix": value_matrix, "out_weight": out_weight, "moe_gain": moe_gain, "router_weight": router_weight, "expert_weight": expert_weight}


@jax.custom_vjp
def low(v):
    return lax.optimization_barrier(v.astype(jnp.bfloat16)).astype(jnp.float32)

@jax.custom_vjp
def low_back(v):
    return v

def low_keep(v):
    return (low(v), None)

def low_pass(kept, grad):
    return (grad,)

def back_keep(v):
    return (v, None)

def back_low(kept, grad):
    return (low(grad),)
low.defvjp(low_keep, low_pass)
low_back.defvjp(back_keep, back_low)
exact_precision = lax.Precision.HIGHEST
eps_norm = 1e-06
rope_base = 10000.0

def rms_scale(values, gain):
    return values * lax.rsqrt(lax.optimization_barrier(jnp.mean(values * values, axis=-1, keepdims=True)) + eps_norm) * gain

def rotary_embedding(values, token_position):
    middle = values.shape[-1] // 2
    freq = rope_base ** (-(jnp.arange(middle, dtype=jnp.float32) * 2.0 / values.shape[-1]))
    angle = token_position.astype(jnp.float32)[:, None] * freq[None, :]
    cosine = jnp.cos(angle)[:, None, :]
    sine = jnp.sin(angle)[:, None, :]
    first = values[..., :middle]
    second = values[..., middle:]
    return jnp.concatenate([first * cosine - second * sine, second * cosine + first * sine], axis=-1)

def pair_layer(params, xrow, route_row, token_position, segment):
    gain_a, w_query, key_projection, value_projection, w_out, gain_m, w_router, w_expert = params
    item_count = xrow.shape[0]
    attention_normed = low(rms_scale(xrow, gain_a))
    query_linear = low_back(jnp.dot(attention_normed, w_query, precision=exact_precision)).reshape(item_count, QUERY_HEADS, HEAD_SIZE)
    key_linear = low_back(jnp.dot(attention_normed, key_projection, precision=exact_precision)).reshape(item_count, KEY_VALUE_HEADS, HEAD_SIZE)
    value_row_set = low_back(low(jnp.dot(attention_normed, value_projection, precision=exact_precision))).reshape(item_count, KEY_VALUE_HEADS, HEAD_SIZE)
    query_rotated = low_back(low(rotary_embedding(query_linear, token_position))).reshape(item_count, KEY_VALUE_HEADS, QUERY_HEADS // KEY_VALUE_HEADS, HEAD_SIZE)
    key_rotated = low_back(low(rotary_embedding(key_linear, token_position)))
    scores = low_back(jnp.einsum('tgjd,ugd->gjtu', query_rotated, key_rotated, precision=exact_precision) * 0.125)
    allowed = (segment[:, None] == segment[None, :]) & (token_position[None, :] <= token_position[:, None])
    scores = jnp.where(allowed[None, None], scores, -jnp.inf)
    probability = low(jax.nn.softmax(scores, axis=-1))
    heads = low_back(low(jnp.einsum('gjtu,ugd->tgjd', probability, value_row_set, precision=exact_precision)))
    heads = heads.reshape(item_count, QUERY_HEADS * HEAD_SIZE)
    middle = xrow + low_back(jnp.dot(heads, w_out, precision=exact_precision))
    normed_m = low(rms_scale(middle, gain_m))
    logits = low_back(jnp.dot(normed_m, w_router, precision=exact_precision))
    chosen = lax.optimization_barrier(jnp.sum((route_row[:, :, None] == jnp.arange(EXPERTS)[None, None, :]).astype(jnp.float32), axis=1))
    gates = jax.nn.softmax(jnp.where(chosen > 0, logits, -jnp.inf), axis=-1)
    gate_up = low_back(jnp.einsum('td,def->tef', normed_m, w_expert[:, :, :2 * F], precision=exact_precision))
    hidden = low(jax.nn.silu(gate_up[..., :F]) * gate_up[..., F:])
    branch = low_back(jnp.einsum('tef,def->ted', hidden, w_expert[:, :, 2 * F:], precision=exact_precision))
    return middle + jnp.einsum('te,ted->td', gates, branch, precision=exact_precision)

def reference(tokens, cotangent, routes, lengths, deal_order, attn_gain, query_weight, key_matrix, value_matrix, out_weight, moe_gain, router_weight, expert_weight):
    first_seq = deal_order[0::2]
    second_seq = deal_order[1::2]
    first_len = lengths[first_seq]
    row_ids = jnp.arange(PAIR_TOK, dtype=jnp.int32)
    is_later = row_ids[None, :] >= first_len[:, None]
    seq_index = jnp.where(is_later, second_seq[:, None], first_seq[:, None]).astype(jnp.int32)
    token_position = (row_ids[None, :] - jnp.where(is_later, first_len[:, None], 0)).astype(jnp.int32)
    segment = is_later.astype(jnp.int32)
    x_rows = tokens[seq_index, token_position].astype(jnp.float32)
    cot_rows = cotangent[seq_index, token_position].astype(jnp.float32)
    route_rows = routes[seq_index, token_position]
    params = (attn_gain, query_weight, key_matrix, value_matrix, out_weight, moe_gain, router_weight, expert_weight)

    def whole(param_set, inputs):
        rounded = tuple((low(item) for item in param_set))
        layer = jax.checkpoint(pair_layer)

        def one_pair(item):
            return layer(rounded, item[0], item[1], item[2], item[3])
        return lax.map(one_pair, (inputs, route_rows, token_position, segment))
    results, pullback = jax.vjp(whole, params, x_rows)
    grads, grad_rows = pullback(cot_rows)
    output = jnp.zeros((SEQS, LMAX, MODEL_WIDTH), jnp.float32).at[seq_index, token_position].set(results)
    grad_tokens = jnp.zeros((SEQS, LMAX, MODEL_WIDTH), jnp.float32).at[seq_index, token_position].set(grad_rows)
    return (output, grad_tokens, grads[0], grads[1], grads[2], grads[3], grads[4], grads[5], grads[6], grads[7])
```

```python
import jax
import jax.numpy as jnp
from jax import lax
from jax.experimental import pallas as pl
from jax.experimental.pallas import tpu as pltpu
from jax.sharding import PartitionSpec as P

QUERY_HEADS = 24
KEY_VALUE_HEADS = 8
HEAD = 64
PAIR_TOK = 1152
MEMBERS = 4
LANE = 128
TILE = 384
KEYROWS = 128
UNIT = PAIR_TOK // KEYROWS // 1
eps_norm = 1e-06
rope_base = 10000.0
NEG = -1e30
BF = jnp.bfloat16
F32 = jnp.float32

Q_LOC = QUERY_HEADS // MEMBERS * HEAD
KV_LOC = KEY_VALUE_HEADS // MEMBERS * HEAD
KVH = KEY_VALUE_HEADS // MEMBERS
GROUP = QUERY_HEADS // KEY_VALUE_HEADS
QKV = Q_LOC + 2 * KV_LOC
OUT_F = LANE
OUT_B = Q_LOC - OUT_F

ANY = pl.BlockSpec(memory_space=pl.ANY)
SMEM = pl.BlockSpec(memory_space=pltpu.SMEM)
VM = pl.BlockSpec(memory_space=pltpu.VMEM)


def params(megabytes):
    return pltpu.CompilerParams(vmem_limit_bytes=megabytes << 20)


def cost(flops, moved, trans=0):
    return pl.CostEstimate(flops=flops, bytes_accessed=moved, transcendentals=trans)


def dot(a, b):
    return lax.dot_general(a, b, (((1,), (0,)), ((), ())), preferred_element_type=F32)


def dot_nt(a, b):
    return lax.dot_general(a, b, (((1,), (1,)), ((), ())), preferred_element_type=F32)


def dot_tn(a, b):
    return lax.dot_general(a, b, (((0,), (0,)), ((), ())), preferred_element_type=F32)


def pick_rows(values, order):
    count, block, width = values.shape

    def kernel(order_ref, in_ref, out_ref):
        out_ref[...] = in_ref[...]

    return pl.pallas_call(
        kernel,
        out_shape=jax.ShapeDtypeStruct(values.shape, values.dtype),
        grid_spec=pltpu.PrefetchScalarGridSpec(
            num_scalar_prefetch=1,
            grid=(count,),
            in_specs=[pl.BlockSpec((1, block, width), lambda i, o: (o[i], 0, 0))],
            out_specs=pl.BlockSpec((1, block, width), lambda i, o: (i, 0, 0)),
        ),
        cost_estimate=cost(0, 4 * values.size),
        name="pick",
    )(order, values)


def pick_marked(values, routes, order):
    count, block, width = values.shape
    topk = routes.shape[2]

    def kernel(order_ref, in_ref, route_ref, out_ref):
        out_ref[0, :, :width] = in_ref[0]
        lanes = lax.broadcasted_iota(jnp.int32, (block, LANE), 1)
        mark = jnp.zeros((block, LANE), F32)
        for k in range(topk):
            mark = mark + jnp.where(route_ref[0, :, k : k + 1] == lanes, 1.0, 0.0)
        out_ref[0, :, width:] = mark.astype(BF)

    return pl.pallas_call(
        kernel,
        out_shape=jax.ShapeDtypeStruct((count, block, width + LANE), values.dtype),
        grid_spec=pltpu.PrefetchScalarGridSpec(
            num_scalar_prefetch=1,
            grid=(count,),
            in_specs=[
                pl.BlockSpec((1, block, width), lambda i, o: (o[i], 0, 0)),
                pl.BlockSpec((1, block, topk), lambda i, o: (o[i], 0, 0)),
            ],
            out_specs=pl.BlockSpec((1, block, width + LANE), lambda i, o: (i, 0, 0)),
        ),
        cost_estimate=cost(0, 4 * values.size),
        name="pick_marked",
    )(order, values, routes)


def dealt_index(t, first):
    return jnp.where(t < first, 2 * t, 2 * (t - first) + 1)


def norm_rows(dealt, gain, first, units):
    _, block, width = dealt.shape

    def kernel(first_ref, in_ref, gain_ref, x_ref, a_ref):
        x = in_ref[0].astype(F32)
        scale = lax.rsqrt(jnp.mean(x * x, axis=-1, keepdims=True) + eps_norm)
        x_ref[0] = in_ref[0]
        a_ref[0] = (x * scale * gain_ref[...].astype(F32)).astype(BF)

    shape = jax.ShapeDtypeStruct((units, block, width), BF)
    spec = pl.BlockSpec((1, block, width), lambda t, f: (t, 0, 0))
    return pl.pallas_call(
        kernel,
        out_shape=(shape, shape),
        grid_spec=pltpu.PrefetchScalarGridSpec(
            num_scalar_prefetch=1,
            grid=(units,),
            in_specs=[
                pl.BlockSpec((1, block, width), lambda t, f: (dealt_index(t, f[0]), 0, 0)),
                pl.BlockSpec((1, width), lambda t, f: (0, 0)),
            ],
            out_specs=(spec, spec),
        ),
        cost_estimate=cost(0, 6 * units * block * width),
        name="norm_rows",
    )(first, dealt, gain)


def take_rows(dealt, first, units):
    _, block, width = dealt.shape

    def kernel(first_ref, in_ref, out_ref):
        out_ref[...] = in_ref[...]

    return pl.pallas_call(
        kernel,
        out_shape=jax.ShapeDtypeStruct((units, block, width), BF),
        grid_spec=pltpu.PrefetchScalarGridSpec(
            num_scalar_prefetch=1,
            grid=(units,),
            in_specs=[pl.BlockSpec((1, block, width), lambda t, f: (dealt_index(t, f[0]), 0, 0))],
            out_specs=pl.BlockSpec((1, block, width), lambda t, f: (t, 0, 0)),
        ),
        cost_estimate=cost(0, 4 * units * block * width),
        name="take_rows",
    )(first, dealt)


def spread_rows(rows, first, slots):
    units, block, width = rows.shape

    def source(i, f):
        u = jnp.where(i % 2 == 0, i // 2, f[0] + i // 2)
        return jnp.minimum(u, units - 1)

    def kernel(first_ref, in_ref, out_ref):
        i = pl.program_id(0)
        limit = jnp.where(i % 2 == 0, first_ref[0], units - first_ref[0])
        keep = i // 2 < limit
        out_ref[...] = jnp.where(keep, in_ref[...].astype(F32), 0.0).astype(BF)

    return pl.pallas_call(
        kernel,
        out_shape=jax.ShapeDtypeStruct((slots, block, width), BF),
        grid_spec=pltpu.PrefetchScalarGridSpec(
            num_scalar_prefetch=1,
            grid=(slots,),
            in_specs=[pl.BlockSpec((1, block, width), lambda i, f: (source(i, f), 0, 0))],
            out_specs=pl.BlockSpec((1, block, width), lambda i, f: (i, 0, 0)),
        ),
        cost_estimate=cost(0, 4 * slots * block * width),
        name="spread_rows",
    )(first, rows)


def place_rows(values, order):
    count, block, width = values.shape

    def kernel(order_ref, in_ref, out_ref):
        out_ref[...] = in_ref[...].astype(F32)

    return pl.pallas_call(
        kernel,
        out_shape=jax.ShapeDtypeStruct(values.shape, F32),
        grid_spec=pltpu.PrefetchScalarGridSpec(
            num_scalar_prefetch=1,
            grid=(count,),
            in_specs=[pl.BlockSpec((1, block, width), lambda i, o: (i, 0, 0))],
            out_specs=pl.BlockSpec((1, block, width), lambda i, o: (o[i], 0, 0)),
        ),
        cost_estimate=cost(0, 6 * values.size),
        name="place_rows",
    )(order, values)


def cut_experts(weight, base, per):
    rows, count, width = weight.shape
    step = 16
    half = width // 2

    def kernel(base_ref, in_ref, *out_refs):
        for e in range(per):
            for j in range(MEMBERS):

                @pl.when(base_ref[0] == j * per)
                def _():
                    value = in_ref[:, j * per + e, :].astype(BF)
                    out_refs[2 * e][...] = value[:, :half]
                    out_refs[2 * e + 1][...] = value[:, half:]

    return pl.pallas_call(
        kernel,
        out_shape=tuple(jax.ShapeDtypeStruct((rows, half), BF) for _ in range(2 * per)),
        grid_spec=pltpu.PrefetchScalarGridSpec(
            num_scalar_prefetch=1,
            grid=(rows // step,),
            in_specs=[pl.BlockSpec((step, count, width), lambda i, b: (i, 0, 0))],
            out_specs=tuple(pl.BlockSpec((step, half), lambda i, b: (i, 0)) for _ in range(2 * per)),
        ),
        cost_estimate=cost(0, 6 * weight.size),
        name="cut_experts",
    )(base, weight)


def start_rows(refs, scratch, table, at, sems):
    copies = []
    for k in range(MEMBERS):
        place = pl.multiple_of(table[at + k] * 32, 32)
        copies.append(
            pltpu.make_async_copy(refs[k], scratch.at[:, pl.ds(place, 32), :], sems.at[k])
        )
        copies[-1].start()
    return copies


def start_weights(refs_f, refs_b, wf, wb, scratch, table, sems):
    copies = []
    n = len(refs_f)
    for s in range(n):
        rows = refs_f[s].shape[0]
        row_f = pl.multiple_of(table[s], 16)
        row_b = pl.multiple_of(table[n + s], 16)
        copies.append(
            pltpu.make_async_copy(
                refs_f[s].at[:, pl.ds(0, wf)],
                scratch.at[pl.ds(row_f, rows), pl.ds(0, wf)],
                sems.at[s],
            )
        )
        copies.append(
            pltpu.make_async_copy(
                refs_b[s].at[:, pl.ds(0, wb)],
                scratch.at[pl.ds(row_b, rows), pl.ds(wf, wb)],
                sems.at[n + s],
            )
        )
    for c in copies:
        c.start()
    return copies


def start_out(refs, scratch, table, at, sems):
    copies = []
    for k in range(MEMBERS):
        copies.append(pltpu.make_async_copy(refs[k], scratch.at[table[at + k]], sems.at[k]))
        copies[-1].start()
    return copies


def wait_all(copies):
    for c in copies:
        c.wait()


def turn(values, cosine, sine):
    width = values.shape[1]
    lanes = lax.broadcasted_iota(jnp.int32, values.shape, 1)
    low = pltpu.roll(values, width - HEAD // 2, 1)
    high = pltpu.roll(values, HEAD // 2, 1)
    swapped = jnp.where(lanes % HEAD < HEAD // 2, low, high)
    reps = width // LANE
    return values * jnp.concatenate([cosine] * reps, 1) + swapped * jnp.concatenate([sine] * reps, 1)


def bias_for(t, extent, first_len):
    gi = lax.broadcasted_iota(jnp.int32, (KEYROWS, extent), 0) + t * KEYROWS
    gj = lax.broadcasted_iota(jnp.int32, (KEYROWS, extent), 1)
    allowed = (gj <= gi) & ((gi < first_len) | (gj >= first_len))
    return jnp.concatenate([jnp.where(allowed, 0.0, NEG)] * GROUP, 0)


def attention_forward(table, base, af, ab, rows_a, wout, cosine, sine, width):
    n = len(af)
    tiles = PAIR_TOK // TILE
    per = TILE // KEYROWS

    def kernel(*refs):
        tab = refs[0]
        f_refs = refs[1 : 1 + n]
        b_refs = refs[1 + n : 1 + 2 * n]
        a_refs = refs[1 + 2 * n : 5 + 2 * n]
        o_refs = refs[5 + 2 * n : 9 + 2 * n]
        cos_ref, sin_ref = refs[9 + 2 * n : 11 + 2 * n]
        part, q_out, k_out, v_out, heads = refs[11 + 2 * n : 16 + 2 * n]
        a_v, w_v, o_v, sem_a, sem_w, sem_o = refs[16 + 2 * n :]
        ca = start_rows(a_refs, a_v, tab, base, sem_a)
        cw = start_weights(f_refs, b_refs, Q_LOC, 2 * KV_LOC, w_v, tab, sem_w)
        co = start_out(o_refs, o_v, tab, base + 4, sem_o)
        wait_all(cw)
        wait_all(ca)
        first_len = tab[base + 8]

        def project(i, carry):
            block = a_v[pl.ds(i * per, per)].reshape(TILE, width)
            y = dot(block, w_v[...])
            rows = pl.ds(pl.multiple_of(i * TILE, TILE), TILE)
            turned = turn(y[:, : Q_LOC + KV_LOC], cos_ref[rows, :], sin_ref[rows, :])
            q = (turned[:, :Q_LOC] * 0.125).astype(BF)
            k = turned[:, Q_LOC:].astype(BF)
            v = y[:, Q_LOC + KV_LOC :].astype(BF)
            for j in range(KVH):
                k_out[j, rows, :] = k[:, j * HEAD : (j + 1) * HEAD]
                v_out[j, rows, :] = v[:, j * HEAD : (j + 1) * HEAD]
                for h in range(GROUP):
                    c = (j * GROUP + h) * HEAD
                    for r in range(per):
                        q_out[j, i * per + r, h * KEYROWS : (h + 1) * KEYROWS, :] = q[
                            r * KEYROWS : (r + 1) * KEYROWS, c : c + HEAD
                        ]
            return carry

        lax.fori_loop(0, tiles, project, 0)
        for c in range(tiles):
            extent = (c + 1) * TILE

            def attend(i, carry, c=c, extent=extent):
                t = c * per + i
                bias = bias_for(t, extent, first_len)
                mixed = []
                for j in range(KVH):
                    s = dot_nt(q_out[j, t], k_out[j, :extent, :]) + bias
                    top = jnp.max(s, axis=1, keepdims=True)
                    p = jnp.exp(s - top)
                    total = jnp.sum(p, axis=1, keepdims=True)
                    o = dot(p.astype(BF), v_out[j, :extent, :]) / total
                    mixed += [o[h * KEYROWS : (h + 1) * KEYROWS] for h in range(GROUP)]
                rows = pl.ds(pl.multiple_of(t * KEYROWS, KEYROWS), KEYROWS)
                heads[rows, :] = jnp.concatenate(mixed, 1).astype(BF)
                return carry

            lax.fori_loop(0, per, attend, 0)
        wait_all(co)

        def project_out(i, carry):
            rows = pl.ds(pl.multiple_of(i * TILE, TILE), TILE)
            h = heads[rows, :]
            for j in range(MEMBERS):
                y = dot(h, o_v[j]).astype(BF)
                part[pl.ds(i * per, per), :, j * Q_LOC : (j + 1) * Q_LOC] = y.reshape(
                    per, KEYROWS, Q_LOC
                )
            return carry

        lax.fori_loop(0, tiles, project_out, 0)

    nt = PAIR_TOK // KEYROWS
    return pl.pallas_call(
        kernel,
        out_shape=(
            jax.ShapeDtypeStruct((nt, KEYROWS, width), BF),
            jax.ShapeDtypeStruct((KVH, nt, GROUP * KEYROWS, HEAD), BF),
            jax.ShapeDtypeStruct((KVH, PAIR_TOK, HEAD), BF),
            jax.ShapeDtypeStruct((KVH, PAIR_TOK, HEAD), BF),
            jax.ShapeDtypeStruct((PAIR_TOK, Q_LOC), BF),
        ),
        in_specs=[SMEM] + [ANY] * (2 * n + 8) + [VM, VM],
        out_specs=(VM,) * 5,
        scratch_shapes=[
            pltpu.VMEM((nt, KEYROWS, width), BF),
            pltpu.VMEM((width, QKV), BF),
            pltpu.VMEM((MEMBERS, Q_LOC, Q_LOC), BF),
            pltpu.SemaphoreType.DMA((4,)),
            pltpu.SemaphoreType.DMA((2 * n,)),
            pltpu.SemaphoreType.DMA((4,)),
        ],
        compiler_params=params(48),
        cost_estimate=cost(15 * 10**9, 14 << 20, 5 * 10**6),
        name="attention_forward",
    )(table, *af, *ab, *rows_a, *wout, cosine, sine)


def attention_backward(table, base, af, ab, rows_m, wout, q, k, v, cosine, sine, width):
    n = len(af)
    tiles = PAIR_TOK // TILE
    per = TILE // KEYROWS
    nt = PAIR_TOK // KEYROWS
    wide = rows_m[0].shape[2]

    def kernel(*refs):
        tab = refs[0]
        f_refs = refs[1 : 1 + n]
        b_refs = refs[1 + n : 1 + 2 * n]
        m_refs = refs[1 + 2 * n : 5 + 2 * n]
        o_refs = refs[5 + 2 * n : 9 + 2 * n]
        q_ref, k_ref, v_ref, cos_ref, sin_ref = refs[9 + 2 * n : 14 + 2 * n]
        da, dqkv = refs[14 + 2 * n : 16 + 2 * n]
        m_v, w_v, o_v, dh_s, dq_s, dk_s, dv_s, sem_m, sem_w, sem_o = refs[16 + 2 * n :]
        cm = start_rows(m_refs, m_v, tab, base, sem_m)
        co = start_out(o_refs, o_v, tab, base + 4, sem_o)
        cw = start_weights(f_refs, b_refs, Q_LOC, 2 * KV_LOC, w_v, tab, sem_w)
        dk_s[...] = jnp.zeros_like(dk_s)
        dv_s[...] = jnp.zeros_like(dv_s)
        wait_all(co)
        wait_all(cm)
        first_len = tab[base + 8]

        def heads_back(i, carry):
            total = None
            for j in range(MEMBERS):
                block = m_v[pl.ds(i * per, per), :, j * Q_LOC : (j + 1) * Q_LOC]
                y = dot_nt(block.reshape(TILE, Q_LOC), o_v[j])
                total = y if total is None else total + y
            total = total.astype(BF)
            for j in range(KVH):
                for h in range(GROUP):
                    c = (j * GROUP + h) * HEAD
                    for r in range(per):
                        dh_s[j, i * per + r, h * KEYROWS : (h + 1) * KEYROWS, :] = total[
                            r * KEYROWS : (r + 1) * KEYROWS, c : c + HEAD
                        ]
            return carry

        lax.fori_loop(0, tiles, heads_back, 0)
        for c in range(tiles):
            extent = (c + 1) * TILE

            def attend(i, carry, c=c, extent=extent):
                t = c * per + i
                bias = bias_for(t, extent, first_len)
                for j in range(KVH):
                    qb = q_ref[j, t]
                    db = dh_s[j, t]
                    kb = k_ref[j, :extent, :]
                    s = dot_nt(qb, kb) + bias
                    top = jnp.max(s, axis=1, keepdims=True)
                    p = jnp.exp(s - top)
                    p = p * (1.0 / jnp.sum(p, axis=1, keepdims=True))
                    dp = dot_nt(db, v_ref[j, :extent, :])
                    prod = p * dp
                    delta = jnp.sum(prod, axis=1, keepdims=True)
                    ds = (prod - p * delta).astype(BF)
                    dq_s[j, t] = dot(ds, kb) * 0.125
                    dk_s[j, :extent, :] += dot_tn(ds, qb)
                    dv_s[j, :extent, :] += dot_tn(p.astype(BF), db)
                return carry

            lax.fori_loop(0, per, attend, 0)
        wait_all(cw)

        def inputs_back(i, carry):
            rows = pl.ds(pl.multiple_of(i * TILE, TILE), TILE)
            cols = []
            for j in range(KVH):
                for h in range(GROUP):
                    cols.append(
                        jnp.concatenate(
                            [
                                dq_s[j, i * per + r, h * KEYROWS : (h + 1) * KEYROWS, :]
                                for r in range(per)
                            ],
                            0,
                        )
                    )
            cols += [dk_s[j, rows, :] for j in range(KVH)]
            joined = jnp.concatenate(cols, 1).astype(BF).astype(F32)
            turned = turn(joined, cos_ref[rows, :], -sin_ref[rows, :])
            value = jnp.concatenate([dv_s[j, rows, :] for j in range(KVH)], 1)
            out = jnp.concatenate([turned, value], 1).astype(BF)
            dqkv[rows, :] = out
            y = dot_nt(out, w_v[...]).astype(BF)
            da[pl.ds(i * per, per)] = y.reshape(per, KEYROWS, width)
            return carry

        lax.fori_loop(0, tiles, inputs_back, 0)

    return pl.pallas_call(
        kernel,
        out_shape=(
            jax.ShapeDtypeStruct((nt, KEYROWS, width), BF),
            jax.ShapeDtypeStruct((PAIR_TOK, QKV), BF),
        ),
        in_specs=[SMEM] + [ANY] * (2 * n + 8) + [VM] * 5,
        out_specs=(VM,) * 2,
        scratch_shapes=[
            pltpu.VMEM((nt, KEYROWS, wide), BF),
            pltpu.VMEM((width, QKV), BF),
            pltpu.VMEM((MEMBERS, Q_LOC, Q_LOC), BF),
            pltpu.VMEM((KVH, nt, GROUP * KEYROWS, HEAD), BF),
            pltpu.VMEM((KVH, nt, GROUP * KEYROWS, HEAD), F32),
            pltpu.VMEM((KVH, PAIR_TOK, HEAD), F32),
            pltpu.VMEM((KVH, PAIR_TOK, HEAD), F32),
            pltpu.SemaphoreType.DMA((4,)),
            pltpu.SemaphoreType.DMA((2 * n,)),
            pltpu.SemaphoreType.DMA((4,)),
        ],
        compiler_params=params(56),
        cost_estimate=cost(20 * 10**9, 16 << 20, 5 * 10**6),
        name="attention_backward",
    )(table, *af, *ab, *rows_m, *wout, q, k, v, cosine, sine)


def attention_grads(table, base, rows_a, rows_b, rows_m, heads, dqkv, width):
    nt = PAIR_TOK // KEYROWS
    step = 256
    wide = rows_m[0].shape[2]

    def kernel(*refs):
        tab = refs[0]
        a_refs, b_refs, m_refs = refs[1:5], refs[5:9], refs[9:13]
        heads_ref, d_ref = refs[13:15]
        gq, go, gr = refs[15:18]
        a_v, b_v, m_v, sem_a, sem_b, sem_m = refs[18:]
        j = pl.program_id(0)

        @pl.when(j == 0)
        def _():
            ca = start_rows(a_refs, a_v, tab, base, sem_a)
            cb = start_rows(b_refs, b_v, tab, base, sem_b)
            cm = start_rows(m_refs, m_v, tab, base, sem_m)
            wait_all(ca)
            wait_all(cb)
            wait_all(cm)

        cols = pl.ds(pl.multiple_of(j * step, step), step)
        a = a_v[:, :, cols].reshape(PAIR_TOK, step)
        gq[...] = dot_tn(a, d_ref[...]).astype(BF)
        b = b_v[:, :, cols].reshape(PAIR_TOK, step)
        gr[...] = dot_tn(b, m_v[:, :, width:].reshape(PAIR_TOK, LANE)).astype(BF)
        m = m_v[:, :, cols].reshape(PAIR_TOK, step)
        go[...] = dot_tn(heads_ref[...], m).astype(BF)

    return pl.pallas_call(
        kernel,
        grid=(width // step,),
        out_shape=(
            jax.ShapeDtypeStruct((width, QKV), BF),
            jax.ShapeDtypeStruct((Q_LOC, width), BF),
            jax.ShapeDtypeStruct((width, LANE), BF),
        ),
        in_specs=[SMEM]
        + [ANY] * 12
        + [
            pl.BlockSpec((PAIR_TOK, Q_LOC), lambda j: (0, 0)),
            pl.BlockSpec((PAIR_TOK, QKV), lambda j: (0, 0)),
        ],
        out_specs=(
            pl.BlockSpec((step, QKV), lambda j: (j, 0)),
            pl.BlockSpec((Q_LOC, step), lambda j: (0, j)),
            pl.BlockSpec((step, LANE), lambda j: (j, 0)),
        ),
        scratch_shapes=[
            pltpu.VMEM((nt, KEYROWS, width), BF),
            pltpu.VMEM((nt, KEYROWS, width), BF),
            pltpu.VMEM((nt, KEYROWS, wide), BF),
            pltpu.SemaphoreType.DMA((4,)),
            pltpu.SemaphoreType.DMA((4,)),
            pltpu.SemaphoreType.DMA((4,)),
        ],
        compiler_params=params(40),
        cost_estimate=cost(4 * 10**9, 16 << 20),
        name="attention_grads",
    )(table, *rows_a, *rows_b, *rows_m, heads, dqkv)


def expert_kernel(table, base, slot, wf, wb, rows_b, rows_d, router, width, hidden):
    n = len(wf)
    nt = PAIR_TOK // KEYROWS
    tiles = PAIR_TOK // TILE
    per = TILE // KEYROWS
    step = 256
    cuts = width // step
    wide = width + LANE
    half = wf[0].shape[1]

    def kernel(*refs):
        tab = refs[0]
        f_refs = refs[1 : 1 + n]
        w_refs = refs[1 + n : 1 + 2 * n]
        b_refs = refs[1 + 2 * n : 5 + 2 * n]
        d_refs = refs[5 + 2 * n : 9 + 2 * n]
        r_ref = refs[9 + 2 * n]
        db, out, grad = refs[10 + 2 * n : 13 + 2 * n]
        w_v, b_v, d_v, dgu_v, gh_v, sem_w, sem_b, sem_d = refs[13 + 2 * n :]
        i = pl.program_id(0)

        @pl.when(i == 0)
        def _():
            cw = start_weights(f_refs, w_refs, half, half, w_v, tab, sem_w)
            cb = start_rows(b_refs, b_v, tab, base, sem_b)
            cd = start_rows(d_refs, d_v, tab, base, sem_d)
            wait_all(cw)
            wait_all(cb)
            wait_all(cd)

        @pl.when(i < tiles)
        def _():
            at = pl.ds(i * per, per)
            b = b_v[at].reshape(TILE, width)
            dy = d_v[at, :, :width].reshape(TILE, width)
            mark = d_v[at, :, width:].reshape(TILE, LANE).astype(F32)
            expert = tab[base + 9] + slot
            lanes = lax.broadcasted_iota(jnp.int32, (TILE, LANE), 1)
            logits = jnp.where(mark > 0.0, dot_nt(b, r_ref[...]), NEG)
            top = jnp.max(logits, axis=1, keepdims=True)
            weight = jnp.where(mark > 0.0, jnp.exp(logits - top), 0.0)
            gates = weight / jnp.sum(weight, axis=1, keepdims=True)
            gate = jnp.sum(jnp.where(lanes == expert, gates, 0.0), axis=1, keepdims=True)
            gu = dot(b, w_v[:, : 2 * hidden])
            back = dot(dy, w_v[:, 2 * hidden :])
            g = gu[:, :hidden]
            u = gu[:, hidden:]
            sig = 1.0 / (1.0 + jnp.exp(-g))
            act = g * sig
            hb = (act * u).astype(BF)
            hf = hb.astype(F32)
            dgate = jnp.sum(hf * back, axis=1, keepdims=True)
            gh = (hf * gate).astype(BF)
            dh = back * gate
            dg = dh * u * (sig * (1.0 + g * (1.0 - sig)))
            dgu = jnp.concatenate([dg, dh * act], 1).astype(BF)
            rows = pl.ds(pl.multiple_of(i * TILE, TILE), TILE)
            dgu_v[rows, :] = dgu
            gh_v[rows, :] = gh
            db[:, :, :width] = (
                dot_nt(dgu, w_v[:, : 2 * hidden]).astype(BF).reshape(per, KEYROWS, width)
            )
            high = dgate.astype(BF).astype(F32)
            low = dgate - high
            extra = jnp.where(
                lanes == expert, high, jnp.where(lanes == expert + LANE // 2, low, 0.0)
            )
            db[:, :, width:] = extra.astype(BF).reshape(per, KEYROWS, LANE)
            out[...] = dot_nt(gh, w_v[:, 2 * hidden :]).astype(BF).reshape(per, KEYROWS, width)

        @pl.when(i >= tiles)
        def _():
            cols = pl.ds(pl.multiple_of((i - tiles) * step, step), step)
            b = b_v[:, :, cols].reshape(PAIR_TOK, step)
            grad[:, : 2 * hidden] = dot_tn(b, dgu_v[...]).astype(BF)
            dy = d_v[:, :, cols].reshape(PAIR_TOK, step)
            grad[:, 2 * hidden :] = dot_tn(dy, gh_v[...]).astype(BF)

    return pl.pallas_call(
        kernel,
        grid=(tiles + cuts,),
        out_shape=(
            jax.ShapeDtypeStruct((nt, KEYROWS, wide), BF),
            jax.ShapeDtypeStruct((nt, KEYROWS, width), BF),
            jax.ShapeDtypeStruct((width, 3 * hidden), BF),
        ),
        in_specs=[SMEM] + [ANY] * (2 * n + 8) + [pl.BlockSpec((LANE, width), lambda i: (0, 0))],
        out_specs=(
            pl.BlockSpec((per, KEYROWS, wide), lambda i: (jnp.minimum(i, tiles - 1), 0, 0)),
            pl.BlockSpec((per, KEYROWS, width), lambda i: (jnp.minimum(i, tiles - 1), 0, 0)),
            pl.BlockSpec((step, 3 * hidden), lambda i: (jnp.maximum(i - tiles, 0), 0)),
        ),
        scratch_shapes=[
            pltpu.VMEM((width, 3 * hidden), BF),
            pltpu.VMEM((nt, KEYROWS, width), BF),
            pltpu.VMEM((nt, KEYROWS, wide), BF),
            pltpu.VMEM((PAIR_TOK, 2 * hidden), BF),
            pltpu.VMEM((PAIR_TOK, hidden), BF),
            pltpu.SemaphoreType.DMA((2 * n,)),
            pltpu.SemaphoreType.DMA((4,)),
            pltpu.SemaphoreType.DMA((4,)),
        ],
        compiler_params=params(48),
        cost_estimate=cost(17 * 10**9, 26 << 20, 10**6),
        name="expert",
    )(table, *wf, *wb, *rows_b, *rows_d, router)


def turn_out_weight(places, af, ab):
    n = len(af)
    rows = af[0].shape[0]

    def kernel(*refs):
        tab = refs[0]
        f_refs = refs[1 : 1 + n]
        b_refs = refs[1 + n : 1 + 2 * n]
        out, sems = refs[1 + 2 * n :]
        copies = []
        for s in range(n):
            at = pl.ds(pl.multiple_of(tab[n + s], 16), rows)
            copies.append(
                pltpu.make_async_copy(
                    f_refs[s].at[:, pl.ds(Q_LOC, OUT_F)],
                    out.at[tab[s], at, pl.ds(0, OUT_F)],
                    sems.at[s],
                )
            )
            at = pl.ds(pl.multiple_of(tab[3 * n + s], 16), rows)
            copies.append(
                pltpu.make_async_copy(
                    b_refs[s].at[:, pl.ds(2 * KV_LOC, OUT_B)],
                    out.at[tab[2 * n + s], at, pl.ds(OUT_F, OUT_B)],
                    sems.at[n + s],
                )
            )
        for c in copies:
            c.start()
        wait_all(copies)

    return pl.pallas_call(
        kernel,
        out_shape=jax.ShapeDtypeStruct((MEMBERS, Q_LOC, Q_LOC), BF),
        in_specs=[SMEM] + [ANY] * (2 * n),
        out_specs=ANY,
        scratch_shapes=[pltpu.SemaphoreType.DMA((2 * n,))],
        cost_estimate=cost(0, 3 << 20),
        name="turn_out_weight",
    )(places, *af, *ab)


def join_experts(places, shares, per):
    rows, half = shares[0][0].shape
    width = 2 * half
    count = MEMBERS * per
    step = 16

    def kernel(*refs):
        tab = refs[0]
        ins = refs[1 : 1 + 2 * count]
        out, hold = refs[1 + 2 * count :]
        for k in range(MEMBERS):
            for e in range(per):
                for side in range(2):
                    value = ins[(k * per + e) * 2 + side][...].astype(F32)
                    hold[tab[k] * per + e, :, side * half : (side + 1) * half] = value
        for c in range(count):
            out[:, c, :] = hold[c]

    flat = [part for share in shares for part in share]
    return pl.pallas_call(
        kernel,
        out_shape=jax.ShapeDtypeStruct((rows, count, width), F32),
        grid=(rows // step,),
        in_specs=[SMEM] + [pl.BlockSpec((step, half), lambda i: (i, 0))] * (2 * count),
        out_specs=pl.BlockSpec((step, count, width), lambda i: (i, 0, 0)),
        scratch_shapes=[pltpu.VMEM((count, step, width), F32)],
        compiler_params=params(32),
        cost_estimate=cost(0, 6 * rows * count * width),
        name="join_experts",
    )(places, *flat)


def ring_place(index, n):
    return jnp.where(index % 2 == 0, index // 2, n - 1 - index // 2)


def ring_index(place, n):
    return jnp.where(place < n // 2, 2 * place, 2 * (n - 1 - place) + 1)


def ring_pairs(n):
    ring = list(range(0, n, 2)) + list(range(n - 1, 0, -2))
    ahead = [(ring[i], ring[(i + 1) % n]) for i in range(n)]
    back = [(b, a) for a, b in ahead]
    return ahead, back


def swap(values, bits):
    return lax.ppermute(values, "seq", [(i, i ^ bits) for i in range(MEMBERS)])


def share_rows(values):
    across = swap(values, 2)
    return [values, swap(values, 1), across, swap(across, 1)]


def body(
    tokens,
    cotangent,
    routes,
    lengths,
    deal_order,
    attn_gain,
    query_weight,
    key_matrix,
    value_matrix,
    out_weight,
    moe_gain,
    router_weight,
    expert_weight,
):
    n = lax.axis_size("dp")
    group = lax.axis_index("dp")
    member = lax.axis_index("seq")
    slots, block, width = tokens.shape
    units = PAIR_TOK // (MEMBERS * block)
    local_rows = query_weight.shape[0]
    n_expert = router_weight.shape[1]
    hidden = expert_weight.shape[2] // 3
    per = n_expert // MEMBERS
    ahead, back = ring_pairs(n)
    natural = block == 32

    place = ring_place(group, n)
    steps = jnp.arange(n, dtype=jnp.int32)
    from_f = ring_index((place - steps) % n, n).astype(jnp.int32)
    from_b = ring_index((place + steps) % n, n).astype(jnp.int32)
    xors = jnp.bitwise_xor(jnp.arange(MEMBERS, dtype=jnp.int32), member)
    row_place = xors if natural else jnp.arange(MEMBERS, dtype=jnp.int32)
    first_seq = deal_order[2 * group]
    first_len = lengths[first_seq]
    first = (first_len // (MEMBERS * block)).reshape(1)
    base = 2 * n
    table = jnp.concatenate(
        [
            from_f * local_rows,
            from_b * local_rows,
            row_place,
            xors,
            jnp.stack([first_len, per * member]),
        ]
    ).astype(jnp.int32)
    share = n // MEMBERS
    out_places = jnp.concatenate(
        [
            jnp.bitwise_xor(from_f // share, member),
            from_f % share * local_rows,
            jnp.bitwise_xor(from_b // share, member),
            from_b % share * local_rows,
        ]
    ).astype(jnp.int32)

    small = jnp.concatenate(
        [attn_gain[None], moe_gain[None], router_weight.T, jnp.zeros((2, local_rows), F32)], 0
    ).astype(BF)
    rows_small = small.shape[0]
    everywhere = jnp.zeros((n, rows_small, local_rows), BF)
    everywhere = lax.dynamic_update_slice(everywhere, small[None], (group, 0, 0))
    f, b = small, small
    for s in range(1, n // 2 + 1):
        f = lax.ppermute(f, "dp", ahead)
        everywhere = lax.dynamic_update_slice(everywhere, f[None], (from_f[s], 0, 0))
        if s < n // 2:
            b = lax.ppermute(b, "dp", back)
            everywhere = lax.dynamic_update_slice(everywhere, b[None], (from_b[s], 0, 0))
    everywhere = everywhere.transpose(1, 0, 2).reshape(rows_small, width)
    gain_a = everywhere[0:1]
    gain_m = everywhere[1:2].astype(F32)
    router = jnp.concatenate(
        [everywhere[2 : 2 + n_expert], jnp.zeros((LANE - n_expert, width), BF)], 0
    )

    sent_x = pick_rows(tokens, deal_order)
    sent_d = pick_marked(cotangent, routes, deal_order)
    dealt_x = lax.all_to_all(sent_x, "dp", split_axis=0, concat_axis=0, tiled=True)
    dealt_d = lax.all_to_all(sent_d, "dp", split_axis=0, concat_axis=0, tiled=True)
    x_rows, a_rows = norm_rows(dealt_x, gain_a, first, units)
    d_rows = take_rows(dealt_d, first, units)

    def cut(values, size):
        return lax.dynamic_slice_in_dim(values, member * size, size, axis=1).astype(BF)

    out_cols = cut(out_weight, Q_LOC)
    attn_f = jnp.concatenate([cut(query_weight, Q_LOC), out_cols[:, :OUT_F]], 1)
    attn_b = jnp.concatenate(
        [cut(key_matrix, KV_LOC), cut(value_matrix, KV_LOC), out_cols[:, OUT_F:]], 1
    )
    expert_parts = cut_experts(expert_weight, (per * member).reshape(1), per)

    def ring_gather(f, b):
        fs, bs = [f], [b]
        for _ in range(n - 1):
            fs.append(lax.ppermute(fs[-1], "dp", ahead))
            bs.append(lax.ppermute(bs[-1], "dp", back))
        return fs, bs

    def ring_scatter(part_f, part_b):
        f, b = part_f(1), part_b(1)
        for s in range(2, n + 1):
            f = lax.ppermute(f, "dp", ahead)
            b = lax.ppermute(b, "dp", back)
            f = (f.astype(F32) + part_f(s % n).astype(F32)).astype(BF)
            b = (b.astype(F32) + part_b(s % n).astype(F32)).astype(BF)
        return f, b

    def rows_of(chunks):
        if natural:
            return chunks
        w = chunks[0].shape[2]
        whole = jnp.zeros((units, MEMBERS, block, w), BF)
        for k in range(MEMBERS):
            whole = lax.dynamic_update_slice(whole, chunks[k][:, None], (0, xors[k], 0, 0))
        whole = whole.reshape(PAIR_TOK // KEYROWS, MEMBERS, 32, w)
        return [whole[:, j] for j in range(MEMBERS)]

    def gather_rows(values):
        return rows_of(share_rows(values))

    def scatter_rows(parts):
        shaped = [p.reshape(units, MEMBERS, block, p.shape[2]) for p in parts]

        def part(k):
            total = None
            for p in shaped:
                one = lax.dynamic_index_in_dim(p, xors[k], axis=1, keepdims=False).astype(F32)
                total = one if total is None else total + one
            return total

        far = swap(part(3).astype(BF), 1)
        near = swap(part(1).astype(BF), 1)
        cross = swap((part(2) + far.astype(F32)).astype(BF), 2)
        return part(0) + near.astype(F32) + cross.astype(F32)

    attn_fs, attn_bs = ring_gather(attn_f, attn_b)
    expert_fs, expert_bs = [], []
    for e in range(per):
        fs, bs = ring_gather(expert_parts[2 * e], expert_parts[2 * e + 1])
        expert_fs.append(fs)
        expert_bs.append(bs)

    turned = turn_out_weight(out_places, attn_fs, attn_bs)
    wout = [turned[0]] + [swap(turned[k], k) for k in range(1, MEMBERS)]

    row = jnp.arange(PAIR_TOK, dtype=jnp.int32)
    pos = row - jnp.where(row >= first_len, first_len, 0)
    freq = rope_base ** (-(jnp.arange(HEAD // 2, dtype=F32) * 2.0 / HEAD))
    angle = pos.astype(F32)[:, None] * freq[None, :]
    cosine = jnp.concatenate([jnp.cos(angle)] * 4, 1)
    sine = jnp.sin(angle)
    sine = jnp.concatenate([-sine, sine, -sine, sine], 1)

    rows_a = gather_rows(a_rows)
    rows_d = gather_rows(d_rows)
    part, q, k, v, heads = attention_forward(
        table, base, attn_fs, attn_bs, rows_a, wout, cosine, sine, width
    )
    middle = x_rows.astype(F32) + scatter_rows([part])

    inverse = lax.rsqrt(jnp.mean(middle * middle, axis=-1, keepdims=True) + eps_norm)
    b_rows = (middle * inverse * gain_m).astype(BF)
    rows_b = gather_rows(b_rows)

    dbs, outs, grads = [], [], []
    for e in range(per):
        db, out, grad = expert_kernel(
            table, base, e, expert_fs[e], expert_bs[e], rows_b, rows_d, router, width, hidden
        )
        dbs.append(db)
        outs.append(out)
        grads.append(grad)

    own_b = b_rows.reshape(units * block, width)
    mark = d_rows[:, :, width:].reshape(units * block, LANE).astype(F32)
    logits = dot_nt(own_b, router)
    gates = jax.nn.softmax(jnp.where(mark > 0.0, logits, -jnp.inf), axis=-1)

    back_sum = scatter_rows(dbs).reshape(units * block, width + LANE)
    extra = back_sum[:, width:]
    dgate = extra + jnp.roll(extra, -(LANE // 2), axis=1)
    dgate = jnp.where(mark > 0.0, dgate, 0.0)
    dlogits = (gates * (dgate - jnp.sum(gates * dgate, axis=-1, keepdims=True))).astype(BF)
    db_own = back_sum[:, :width] + dot(dlogits, router)
    mid_own = middle.reshape(units * block, width)
    inv_own = inverse.reshape(units * block, 1)
    d_own = d_rows[:, :, :width].reshape(units * block, width).astype(F32)
    normed = mid_own * inv_own
    scaled = db_own * gain_m
    dmiddle = d_own + inv_own * (
        scaled - normed * jnp.mean(scaled * normed, axis=-1, keepdims=True)
    )
    dmix = jnp.concatenate([dmiddle.astype(BF), dlogits], 1).reshape(units, block, width + LANE)
    rows_m = gather_rows(dmix)

    da, dqkv = attention_backward(
        table, base, attn_fs, attn_bs, rows_m, wout, q, k, v, cosine, sine, width
    )
    gqkv, gout, grouter = attention_grads(table, base, rows_a, rows_b, rows_m, heads, dqkv, width)

    da_own = scatter_rows([da]).reshape(units * block, width)
    x_own = x_rows.reshape(units * block, width).astype(F32)
    inv_x = lax.rsqrt(jnp.mean(x_own * x_own, axis=-1, keepdims=True) + eps_norm)
    normed_x = x_own * inv_x
    scaled_x = da_own * gain_a.astype(F32)
    grad_x = dmiddle + inv_x * (
        scaled_x - normed_x * jnp.mean(scaled_x * normed_x, axis=-1, keepdims=True)
    )
    result = middle + scatter_rows(outs)

    gout_cols = jnp.zeros((width, Q_LOC), BF)
    for kk in range(MEMBERS):
        piece = lax.dynamic_slice_in_dim(gout, xors[kk] * Q_LOC, Q_LOC, axis=1)
        if kk:
            piece = swap(piece, kk)
        gout_cols = lax.dynamic_update_slice(gout_cols, piece, (xors[kk] * Q_LOC, 0))
    full_f = jnp.concatenate([gqkv[:, :Q_LOC], gout_cols[:, :OUT_F]], 1)
    full_b = jnp.concatenate([gqkv[:, Q_LOC:], gout_cols[:, OUT_F:], grouter], 1)

    def piece_f(values, lo, size):
        return lambda s: lax.dynamic_slice(values, (table[s], lo), (local_rows, size))

    def piece_b(values, lo, size):
        return lambda s: lax.dynamic_slice(values, (table[n + s], lo), (local_rows, size))

    half = 3 * hidden // 2
    expert_shares = []
    for e in range(per):
        f, b = ring_scatter(piece_f(grads[e], 0, half), piece_b(grads[e], half, half))
        expert_shares.append((share_rows(f), share_rows(b)))
    share_f, share_b = ring_scatter(
        piece_f(full_f, 0, full_f.shape[1]), piece_b(full_b, 0, full_b.shape[1])
    )
    small_grad = share_b[:, full_b.shape[1] - LANE :]
    shares_f = share_rows(share_f)
    shares_b = share_rows(share_b[:, : full_b.shape[1] - LANE])

    def spread(chunks, lo, size):
        whole = jnp.zeros((local_rows, MEMBERS * size), F32)
        for kk in range(MEMBERS):
            whole = lax.dynamic_update_slice(
                whole, chunks[kk][:, lo : lo + size].astype(F32), (0, xors[kk] * size)
            )
        return whole

    grad_query = spread(shares_f, 0, Q_LOC)
    grad_key = spread(shares_b, 0, KV_LOC)
    grad_value = spread(shares_b, KV_LOC, KV_LOC)
    out_joined = [
        jnp.concatenate([cf[:, Q_LOC:], cb[:, 2 * KV_LOC :]], 1)
        for cf, cb in zip(shares_f, shares_b)
    ]
    grad_out = spread(out_joined, 0, Q_LOC)
    grad_router = small_grad[:, :n_expert].astype(F32)
    shares = [
        [expert_shares[e][side][kk] for e in range(per) for side in range(2)]
        for kk in range(MEMBERS)
    ]
    grad_experts = join_experts(xors, shares, per)

    def low(values):
        return values.astype(BF).astype(F32)

    grad_attn_gain = (
        jnp.sum(low(query_weight) * grad_query, axis=1)
        + jnp.sum(low(key_matrix) * grad_key, axis=1)
        + jnp.sum(low(value_matrix) * grad_value, axis=1)
    ) / low(attn_gain)
    grad_moe_gain = (
        jnp.sum(
            low(expert_weight[:, :, : 2 * hidden]) * grad_experts[:, :, : 2 * hidden], axis=(1, 2)
        )
        + jnp.sum(low(router_weight) * grad_router, axis=1)
    ) / low(moe_gain)

    back_out = lax.all_to_all(
        spread_rows(result.astype(BF), first, slots),
        "dp",
        split_axis=0,
        concat_axis=0,
        tiled=True,
    )
    back_grad = lax.all_to_all(
        spread_rows(grad_x.reshape(units, block, width).astype(BF), first, slots),
        "dp",
        split_axis=0,
        concat_axis=0,
        tiled=True,
    )
    output = place_rows(back_out, deal_order)
    grad_tokens = place_rows(back_grad, deal_order)
    return (
        output,
        grad_tokens,
        grad_attn_gain,
        grad_query,
        grad_key,
        grad_value,
        grad_out,
        grad_moe_gain,
        grad_router,
        grad_experts,
    )


def solution(mesh):
    rows = P(None, ("dp", "seq"), None)
    placed = (
        rows,
        rows,
        rows,
        P(),
        P(),
        P("dp"),
        P("dp", None),
        P("dp", None),
        P("dp", None),
        P("dp", None),
        P("dp"),
        P("dp", None),
        P("dp", None, None),
    )
    return jax.shard_map(
        body,
        mesh=mesh,
        in_specs=placed,
        out_specs=(
            rows,
            rows,
            P("dp"),
            P("dp", None),
            P("dp", None),
            P("dp", None),
            P("dp", None),
            P("dp"),
            P("dp", None),
            P("dp", None, None),
        ),
        check_vma=False,
    )
```

```python
import jax
import jax.numpy as jnp
from jax import lax
from jax.experimental import pallas as pl
from jax.experimental.pallas import tpu as pltpu
from jax.sharding import PartitionSpec as P

QUERY_HEADS = 24
KEY_VALUE_HEADS = 8
HEAD = 64
PAIR_TOK = 1152
MEMBERS = 4
LANE = 128
TILE = 384
KEYROWS = 128
UNIT = PAIR_TOK // KEYROWS // 1
eps_norm = 1e-06
rope_base = 10000.0
NEG = -1e30
BF = jnp.bfloat16
F32 = jnp.float32

Q_LOC = QUERY_HEADS // MEMBERS * HEAD
KV_LOC = KEY_VALUE_HEADS // MEMBERS * HEAD
KVH = KEY_VALUE_HEADS // MEMBERS
GROUP = QUERY_HEADS // KEY_VALUE_HEADS
QKV = Q_LOC + 2 * KV_LOC
OUT_F = LANE
OUT_B = Q_LOC - OUT_F
GAINS_AT = 64

ANY = pl.BlockSpec(memory_space=pl.ANY)
SMEM = pl.BlockSpec(memory_space=pltpu.SMEM)
VM = pl.BlockSpec(memory_space=pltpu.VMEM)


def params(megabytes):
    return pltpu.CompilerParams(vmem_limit_bytes=megabytes << 20)


def cost(flops, moved, trans=0):
    return pl.CostEstimate(flops=flops // 100, bytes_accessed=moved // 100, transcendentals=trans // 100)


def dot(a, b):
    return lax.dot_general(a, b, (((1,), (0,)), ((), ())), preferred_element_type=F32)


def dot_nt(a, b):
    return lax.dot_general(a, b, (((1,), (1,)), ((), ())), preferred_element_type=F32)


def dot_tn(a, b):
    return lax.dot_general(a, b, (((0,), (0,)), ((), ())), preferred_element_type=F32)


def pick_rows(values, order):
    count = values.shape[0]

    def kernel(order_ref, in_ref, out_ref, sems):
        copies = [
            pltpu.make_async_copy(in_ref.at[order_ref[i]], out_ref.at[i], sems.at[i])
            for i in range(count)
        ]
        for c in copies:
            c.start()
        wait_all(copies)

    return pl.pallas_call(
        kernel,
        out_shape=jax.ShapeDtypeStruct(values.shape, values.dtype),
        in_specs=[SMEM, ANY],
        out_specs=VM,
        scratch_shapes=[pltpu.SemaphoreType.DMA((count,))],
        cost_estimate=cost(0, 4 * values.size),
        name="pick",
    )(order, values)


def pick_marked(values, routes, order):
    count, block, width = values.shape
    topk = routes.shape[2]

    def kernel(order_ref, in_ref, route_ref, out_ref, sems):
        copies = [
            pltpu.make_async_copy(
                in_ref.at[order_ref[i]], out_ref.at[i, :, pl.ds(0, width)], sems.at[i]
            )
            for i in range(count)
        ]
        for c in copies:
            c.start()
        lanes = lax.broadcasted_iota(jnp.int32, (block, LANE), 1)

        def mark_one(i, carry):
            routed = route_ref[order_ref[i]]
            mark = jnp.zeros((block, LANE), F32)
            for k in range(topk):
                mark = mark + jnp.where(routed[:, k : k + 1] == lanes, 1.0, 0.0)
            out_ref[i, :, width:] = mark.astype(BF)
            return carry

        lax.fori_loop(0, count, mark_one, 0)
        wait_all(copies)

    return pl.pallas_call(
        kernel,
        out_shape=jax.ShapeDtypeStruct((count, block, width + LANE), values.dtype),
        in_specs=[SMEM, ANY, VM],
        out_specs=VM,
        scratch_shapes=[pltpu.SemaphoreType.DMA((count,))],
        cost_estimate=cost(0, 4 * values.size),
        name="pick_marked",
    )(order, values, routes)


def take_rows(dealt, first, units):
    _, block, width = dealt.shape

    def kernel(first_ref, in_ref, out_ref, sems):
        copies = []
        for t in range(units):
            source = jnp.where(t < first_ref[0], 2 * t, 2 * (t - first_ref[0]) + 1)
            copies.append(pltpu.make_async_copy(in_ref.at[source], out_ref.at[t], sems.at[t]))
            copies[-1].start()
        wait_all(copies)

    return pl.pallas_call(
        kernel,
        out_shape=jax.ShapeDtypeStruct((units, block, width), BF),
        in_specs=[SMEM, ANY],
        out_specs=VM,
        scratch_shapes=[pltpu.SemaphoreType.DMA((units,))],
        cost_estimate=cost(0, 4 * units * block * width),
        name="take_rows",
    )(first, dealt)


def spread_rows(rows, first, slots):
    units, block, width = rows.shape

    def kernel(first_ref, in_ref, out_ref):
        for i in range(slots):
            u = i // 2 if i % 2 == 0 else first_ref[0] + i // 2
            limit = first_ref[0] if i % 2 == 0 else units - first_ref[0]
            keep = i // 2 < limit

            @pl.when(keep)
            def _():
                out_ref[i] = in_ref[jnp.minimum(u, units - 1)]

            @pl.when(jnp.logical_not(keep))
            def _():
                out_ref[i] = jnp.zeros((block, width), BF)

    return pl.pallas_call(
        kernel,
        out_shape=jax.ShapeDtypeStruct((slots, block, width), BF),
        in_specs=[SMEM, VM],
        out_specs=VM,
        cost_estimate=cost(0, 4 * slots * block * width),
        name="spread_rows",
    )(first, rows)


def place_rows(values, order):
    count, block, width = values.shape

    def kernel(order_ref, in_ref, out_ref, hold, sems):
        copies = []
        for j in range(count):
            hold[j] = in_ref[j].astype(F32)
            copies.append(
                pltpu.make_async_copy(hold.at[j], out_ref.at[order_ref[j]], sems.at[j])
            )
            copies[-1].start()
        wait_all(copies)

    return pl.pallas_call(
        kernel,
        out_shape=jax.ShapeDtypeStruct(values.shape, F32),
        in_specs=[SMEM, VM],
        out_specs=ANY,
        scratch_shapes=[
            pltpu.VMEM(values.shape, F32),
            pltpu.SemaphoreType.DMA((count,)),
        ],
        cost_estimate=cost(0, 6 * values.size),
        name="place_rows",
    )(order, values)


def place_experts(places, shares, weight, lo, count, split, per, total):
    rows = shares[0].shape[0]
    width = shares[0].shape[1] // count
    half = width // 2
    used = 2 * width // 3

    def kernel(*refs):
        tab = refs[0]
        ins = refs[1 : 1 + MEMBERS]
        weight_ref = refs[1 + MEMBERS]
        out, gain, hold, w_v, sems, sem_w = refs[-6:]
        loads = []
        for k in range(MEMBERS):
            for e in range(count):
                at = k * count + e
                loads.append(
                    pltpu.make_async_copy(
                        weight_ref.at[tab[k] * per + lo + e, :, pl.ds(0, used)],
                        w_v.at[tab[k] * count + e],
                        sem_w.at[at],
                    )
                )
                loads[-1].start()
        copies = []
        for k in range(MEMBERS):
            for e in range(count):
                at = tab[k] * count + e
                for side in range(2):
                    col = (side * count + e) * half if split else e * width + side * half
                    hold[at, :, side * half : (side + 1) * half] = ins[k][
                        :, col : col + half
                    ].astype(F32)
                copies.append(
                    pltpu.make_async_copy(
                        hold.at[at], out.at[tab[k] * per + lo + e], sems.at[k * count + e]
                    )
                )
                copies[-1].start()
        wait_all(loads)
        gain[...] = jnp.zeros_like(gain)

        def add(at, carry):
            total = jnp.zeros((rows, LANE), F32)
            for c in range(used // LANE):
                cols = slice(c * LANE, (c + 1) * LANE)
                total = total + w_v[at, :, cols].astype(BF).astype(F32) * hold[at, :, cols]
            gain[...] += total
            return carry

        lax.fori_loop(0, MEMBERS * count, add, 0)
        wait_all(copies)

    before = [] if total is None else [total]
    return pl.pallas_call(
        kernel,
        out_shape=(
            jax.ShapeDtypeStruct((MEMBERS * per, rows, width), F32),
            jax.ShapeDtypeStruct((rows, LANE), F32),
        ),
        in_specs=[SMEM] + [VM] * MEMBERS + [ANY] * (1 + len(before)),
        out_specs=(ANY, VM),
        input_output_aliases={2 + MEMBERS: 0} if before else {},
        scratch_shapes=[
            pltpu.VMEM((MEMBERS * count, rows, width), F32),
            pltpu.VMEM((MEMBERS * count, rows, used), F32),
            pltpu.SemaphoreType.DMA((MEMBERS * count,)),
            pltpu.SemaphoreType.DMA((MEMBERS * count,)),
        ],
        compiler_params=params(40),
        cost_estimate=cost(0, 6 * MEMBERS * count * rows * width),
        name="place_experts",
    )(places, *shares, weight, *before)


def start_rows(refs, scratch, table, at, sems):
    copies = []
    for k in range(MEMBERS):
        place = pl.multiple_of(table[at + k] * 32, 32)
        copies.append(
            pltpu.make_async_copy(refs[k], scratch.at[:, pl.ds(place, 32), :], sems.at[k])
        )
        copies[-1].start()
    return copies


def start_weights(refs_f, refs_b, wf, wb, scratch, table, sems):
    copies = []
    n = len(refs_f)
    for s in range(n):
        rows = refs_f[s].shape[0]
        row_f = pl.multiple_of(table[s], 16)
        row_b = pl.multiple_of(table[n + s], 16)
        copies.append(
            pltpu.make_async_copy(
                refs_f[s].at[:, pl.ds(0, wf)],
                scratch.at[pl.ds(row_f, rows), pl.ds(0, wf)],
                sems.at[s],
            )
        )
        copies.append(
            pltpu.make_async_copy(
                refs_b[s].at[:, pl.ds(0, wb)],
                scratch.at[pl.ds(row_b, rows), pl.ds(wf, wb)],
                sems.at[n + s],
            )
        )
    for c in copies:
        c.start()
    return copies


def start_out(refs, scratch, table, at, sems):
    copies = []
    for k in range(MEMBERS):
        copies.append(pltpu.make_async_copy(refs[k], scratch.at[table[at + k]], sems.at[k]))
        copies[-1].start()
    return copies


def store_members(out, table, at, tiles, values, cols=None):
    per = values.shape[0] // KEYROWS
    shaped = values.reshape(per, KEYROWS, values.shape[1])
    for j in range(MEMBERS):
        piece = shaped[:, j * 32 : (j + 1) * 32]
        if cols is None:
            out[table[at + j], tiles] = piece
        else:
            out[table[at + j], tiles, :, cols] = piece


def wait_all(copies):
    for c in copies:
        c.wait()


def turn(values, cosine, sine):
    width = values.shape[1]
    lanes = lax.broadcasted_iota(jnp.int32, values.shape, 1)
    low = pltpu.roll(values, width - HEAD // 2, 1)
    high = pltpu.roll(values, HEAD // 2, 1)
    swapped = jnp.where(lanes % HEAD < HEAD // 2, low, high)
    reps = width // LANE
    return values * jnp.concatenate([cosine] * reps, 1) + swapped * jnp.concatenate([sine] * reps, 1)


def bias_for(t, extent, first_len):
    gi = lax.broadcasted_iota(jnp.int32, (KEYROWS, extent), 0) + t * KEYROWS
    gj = lax.broadcasted_iota(jnp.int32, (KEYROWS, extent), 1)
    allowed = (gj <= gi) & ((gi < first_len) | (gj >= first_len))
    return jnp.concatenate([jnp.where(allowed, 0.0, NEG)] * GROUP, 0)


def attention_forward(table, base, af, ab, rows_x, cosine, sine, width):
    n = len(af)
    tiles = PAIR_TOK // TILE
    per = TILE // KEYROWS
    nt = PAIR_TOK // KEYROWS
    chunk = af[0].shape[0]

    def kernel(*refs):
        tab = refs[0]
        f_refs = refs[1 : 1 + n]
        b_refs = refs[1 + n : 1 + 2 * n]
        x_refs = refs[1 + 2 * n : 5 + 2 * n]
        cos_ref, sin_ref = refs[5 + 2 * n : 7 + 2 * n]
        a_out, q_out, k_out, v_out, heads, small, gains = refs[7 + 2 * n : 14 + 2 * n]
        w_v, sem_x, sem_w, sem_s = refs[14 + 2 * n :]
        cs = []
        for s in range(n):
            row = pl.ds(pl.multiple_of(tab[s], 16), chunk)
            cs.append(
                pltpu.make_async_copy(
                    f_refs[s].at[:, pl.ds(Q_LOC + OUT_F, LANE)], small.at[row, :], sem_s.at[s]
                )
            )
            cs[-1].start()
        cw = start_weights(f_refs, b_refs, Q_LOC, 2 * KV_LOC, w_v, tab, sem_w)
        cx = start_rows(x_refs, a_out, tab, base, sem_x)
        wait_all(cs)
        pick = lax.broadcasted_iota(jnp.int32, (8, LANE), 1)
        pick = pick == lax.broadcasted_iota(jnp.int32, (8, LANE), 0) + GAINS_AT
        gains[...] = dot_nt(pick.astype(F32).astype(BF), small[...])
        wait_all(cw)
        wait_all(cx)
        first_len = tab[base + 8]

        def project(i, carry):
            at = pl.ds(i * per, per)
            x = a_out[at].reshape(TILE, width).astype(F32)
            scale = lax.rsqrt(jnp.mean(x * x, axis=-1, keepdims=True) + eps_norm)
            block = (x * scale * gains[0:1, :]).astype(BF)
            a_out[at] = block.reshape(per, KEYROWS, width)
            y = dot(block, w_v[...])
            rows = pl.ds(pl.multiple_of(i * TILE, TILE), TILE)
            turned = turn(y[:, : Q_LOC + KV_LOC], cos_ref[rows, :], sin_ref[rows, :])
            q = (turned[:, :Q_LOC] * 0.125).astype(BF)
            k = turned[:, Q_LOC:].astype(BF)
            v = y[:, Q_LOC + KV_LOC :].astype(BF)
            for j in range(KVH):
                k_out[j, rows, :] = k[:, j * HEAD : (j + 1) * HEAD]
                v_out[j, rows, :] = v[:, j * HEAD : (j + 1) * HEAD]
                for h in range(GROUP):
                    c = (j * GROUP + h) * HEAD
                    for r in range(per):
                        q_out[j, i * per + r, h * KEYROWS : (h + 1) * KEYROWS, :] = q[
                            r * KEYROWS : (r + 1) * KEYROWS, c : c + HEAD
                        ]
            return carry

        lax.fori_loop(0, tiles, project, 0)
        for c in range(tiles):
            extent = (c + 1) * TILE

            def attend(i, carry, c=c, extent=extent):
                t = c * per + i
                bias = bias_for(t, extent, first_len)
                mixed = []
                for j in range(KVH):
                    s = dot_nt(q_out[j, t], k_out[j, :extent, :]) + bias
                    top = jnp.max(s, axis=1, keepdims=True)
                    p = jnp.exp(s - top)
                    total = jnp.sum(p, axis=1, keepdims=True)
                    o = dot(p.astype(BF), v_out[j, :extent, :]) / total
                    mixed += [o[h * KEYROWS : (h + 1) * KEYROWS] for h in range(GROUP)]
                rows = pl.ds(pl.multiple_of(t * KEYROWS, KEYROWS), KEYROWS)
                heads[rows, :] = jnp.concatenate(mixed, 1).astype(BF)
                return carry

            lax.fori_loop(0, per, attend, 0)

    return pl.pallas_call(
        kernel,
        out_shape=(
            jax.ShapeDtypeStruct((nt, KEYROWS, width), BF),
            jax.ShapeDtypeStruct((KVH, nt, GROUP * KEYROWS, HEAD), BF),
            jax.ShapeDtypeStruct((KVH, PAIR_TOK, HEAD), BF),
            jax.ShapeDtypeStruct((KVH, PAIR_TOK, HEAD), BF),
            jax.ShapeDtypeStruct((PAIR_TOK, Q_LOC), BF),
            jax.ShapeDtypeStruct((width, LANE), BF),
            jax.ShapeDtypeStruct((8, width), F32),
        ),
        in_specs=[SMEM] + [ANY] * (2 * n + 4) + [VM, VM],
        out_specs=(VM,) * 7,
        scratch_shapes=[
            pltpu.VMEM((width, QKV), BF),
            pltpu.SemaphoreType.DMA((4,)),
            pltpu.SemaphoreType.DMA((2 * n,)),
            pltpu.SemaphoreType.DMA((n,)),
        ],
        compiler_params=params(48),
        cost_estimate=cost(12 * 10**9, 14 << 20, 5 * 10**6),
        name="attention_forward",
    )(table, *af, *ab, *rows_x, cosine, sine)


def project_out(table, base, heads, wout, width):
    tiles = PAIR_TOK // TILE
    per = TILE // KEYROWS
    nt = PAIR_TOK // KEYROWS

    def kernel(tab, heads, *refs):
        o_refs, (part, o_v, sem_o) = refs[:MEMBERS], refs[MEMBERS:]
        wait_all(start_out(o_refs, o_v, tab, base + 4, sem_o))
        for i in range(tiles):
            h = heads[i * TILE : (i + 1) * TILE, :]
            for j in range(MEMBERS):
                y = dot(h, o_v[j]).astype(BF)
                store_members(
                    part, tab, base, pl.ds(i * per, per), y, pl.ds(j * Q_LOC, Q_LOC)
                )

    return pl.pallas_call(
        kernel,
        out_shape=jax.ShapeDtypeStruct((MEMBERS, nt, 32, width), BF),
        in_specs=[SMEM, VM] + [ANY] * MEMBERS,
        out_specs=VM,
        scratch_shapes=[
            pltpu.VMEM((MEMBERS, Q_LOC, Q_LOC), BF),
            pltpu.SemaphoreType.DMA((4,)),
        ],
        compiler_params=params(24),
        cost_estimate=cost(2 * 10**9, 6 << 20),
        name="project_out",
    )(table, heads, *wout)


def attention_backward(table, base, af, ab, rows_m, wout, q, k, v, cosine, sine, width):
    n = len(af)
    tiles = PAIR_TOK // TILE
    per = TILE // KEYROWS
    nt = PAIR_TOK // KEYROWS
    wide = rows_m[0].shape[2]

    def kernel(*refs):
        tab = refs[0]
        f_refs = refs[1 : 1 + n]
        b_refs = refs[1 + n : 1 + 2 * n]
        m_refs = refs[1 + 2 * n : 5 + 2 * n]
        o_refs = refs[5 + 2 * n : 9 + 2 * n]
        q_ref, k_ref, v_ref, cos_ref, sin_ref = refs[9 + 2 * n : 14 + 2 * n]
        da, dqkv = refs[14 + 2 * n : 16 + 2 * n]
        m_v, w_v, o_v, dh_s, dq_s, dk_s, dv_s, sem_m, sem_w, sem_o = refs[16 + 2 * n :]
        cm = start_rows(m_refs, m_v, tab, base, sem_m)
        co = start_out(o_refs, o_v, tab, base + 4, sem_o)
        cw = start_weights(f_refs, b_refs, Q_LOC, 2 * KV_LOC, w_v, tab, sem_w)
        dk_s[...] = jnp.zeros_like(dk_s)
        dv_s[...] = jnp.zeros_like(dv_s)
        wait_all(co)
        wait_all(cm)
        first_len = tab[base + 8]

        def heads_back(i, carry):
            total = None
            for j in range(MEMBERS):
                block = m_v[pl.ds(i * per, per), :, j * Q_LOC : (j + 1) * Q_LOC]
                y = dot_nt(block.reshape(TILE, Q_LOC), o_v[j])
                total = y if total is None else total + y
            total = total.astype(BF)
            for j in range(KVH):
                for h in range(GROUP):
                    c = (j * GROUP + h) * HEAD
                    for r in range(per):
                        dh_s[j, i * per + r, h * KEYROWS : (h + 1) * KEYROWS, :] = total[
                            r * KEYROWS : (r + 1) * KEYROWS, c : c + HEAD
                        ]
            return carry

        lax.fori_loop(0, tiles, heads_back, 0)
        for c in range(tiles):
            extent = (c + 1) * TILE

            def attend(i, carry, c=c, extent=extent):
                t = c * per + i
                bias = bias_for(t, extent, first_len)
                for j in range(KVH):
                    qb = q_ref[j, t]
                    db = dh_s[j, t]
                    kb = k_ref[j, :extent, :]
                    s = dot_nt(qb, kb) + bias
                    top = jnp.max(s, axis=1, keepdims=True)
                    p = jnp.exp(s - top)
                    p = p * (1.0 / jnp.sum(p, axis=1, keepdims=True))
                    dp = dot_nt(db, v_ref[j, :extent, :])
                    prod = p * dp
                    delta = jnp.sum(prod, axis=1, keepdims=True)
                    ds = (prod - p * delta).astype(BF)
                    dq_s[j, t] = dot(ds, kb) * 0.125
                    dk_s[j, :extent, :] += dot_tn(ds, qb)
                    dv_s[j, :extent, :] += dot_tn(p.astype(BF), db)
                return carry

            lax.fori_loop(0, per, attend, 0)
        wait_all(cw)

        def inputs_back(i, carry):
            rows = pl.ds(pl.multiple_of(i * TILE, TILE), TILE)
            cols = []
            for j in range(KVH):
                for h in range(GROUP):
                    cols.append(
                        jnp.concatenate(
                            [
                                dq_s[j, i * per + r, h * KEYROWS : (h + 1) * KEYROWS, :]
                                for r in range(per)
                            ],
                            0,
                        )
                    )
            cols += [dk_s[j, rows, :] for j in range(KVH)]
            joined = jnp.concatenate(cols, 1).astype(BF).astype(F32)
            turned = turn(joined, cos_ref[rows, :], -sin_ref[rows, :])
            value = jnp.concatenate([dv_s[j, rows, :] for j in range(KVH)], 1)
            out = jnp.concatenate([turned, value], 1).astype(BF)
            dqkv[rows, :] = out
            y = dot_nt(out, w_v[...]).astype(BF)
            store_members(da, tab, base, pl.ds(i * per, per), y)
            return carry

        lax.fori_loop(0, tiles, inputs_back, 0)

    return pl.pallas_call(
        kernel,
        out_shape=(
            jax.ShapeDtypeStruct((MEMBERS, nt, 32, width), BF),
            jax.ShapeDtypeStruct((PAIR_TOK, QKV), BF),
        ),
        in_specs=[SMEM] + [ANY] * (2 * n + 8) + [VM] * 5,
        out_specs=(VM,) * 2,
        scratch_shapes=[
            pltpu.VMEM((nt, KEYROWS, wide), BF),
            pltpu.VMEM((width, QKV), BF),
            pltpu.VMEM((MEMBERS, Q_LOC, Q_LOC), BF),
            pltpu.VMEM((KVH, nt, GROUP * KEYROWS, HEAD), BF),
            pltpu.VMEM((KVH, nt, GROUP * KEYROWS, HEAD), F32),
            pltpu.VMEM((KVH, PAIR_TOK, HEAD), F32),
            pltpu.VMEM((KVH, PAIR_TOK, HEAD), F32),
            pltpu.SemaphoreType.DMA((4,)),
            pltpu.SemaphoreType.DMA((2 * n,)),
            pltpu.SemaphoreType.DMA((4,)),
        ],
        compiler_params=params(56),
        cost_estimate=cost(20 * 10**9, 16 << 20, 5 * 10**6),
        name="attention_backward",
    )(table, *af, *ab, *rows_m, *wout, q, k, v, cosine, sine)


def attention_grads(table, base, a_all, rows_b, rows_m, heads, dqkv, width, n):
    nt = PAIR_TOK // KEYROWS
    step = Q_LOC
    chunk = width // n
    owners = step // chunk
    wide = rows_m[0].shape[2]
    wide_f = Q_LOC + OUT_F
    wide_b = 2 * KV_LOC + OUT_B + LANE

    def kernel(*refs):
        tab = refs[0]
        b_refs, m_refs = refs[1:5], refs[5:9]
        a_ref, heads_ref, d_ref = refs[9:12]
        gf, gb, go = refs[12:15]
        b_v, m_v, sem_b, sem_m = refs[15:]
        j = pl.program_id(0)

        @pl.when(j == 0)
        def _():
            cb = start_rows(b_refs, b_v, tab, base, sem_b)
            cm = start_rows(m_refs, m_v, tab, base, sem_m)
            wait_all(cb)
            wait_all(cm)

        cols = pl.ds(pl.multiple_of(j * step, step), step)
        a = a_ref[...].reshape(PAIR_TOK, step)
        gq = dot_tn(a, d_ref[...]).astype(BF)
        b = b_v[:, :, cols].reshape(PAIR_TOK, step)
        gr = dot_tn(b, m_v[:, :, width:].reshape(PAIR_TOK, LANE)).astype(BF)
        for h in range(owners):
            rows = slice(h * chunk, (h + 1) * chunk)
            to_f = tab[base + 10 + j * owners + h]
            to_b = tab[base + 10 + n + j * owners + h]
            gf[to_f, :, :Q_LOC] = gq[rows, :Q_LOC]
            gb[to_b, :, : 2 * KV_LOC] = gq[rows, Q_LOC:]
            gb[to_b, :, 2 * KV_LOC + OUT_B :] = gr[rows, :]
        m = m_v[:, :, cols].reshape(PAIR_TOK, step)
        go[tab[base + 4 + j]] = dot_tn(heads_ref[...], m).astype(BF)

    return pl.pallas_call(
        kernel,
        grid=(width // step,),
        out_shape=(
            jax.ShapeDtypeStruct((n, chunk, wide_f), BF),
            jax.ShapeDtypeStruct((n, chunk, wide_b), BF),
            jax.ShapeDtypeStruct((MEMBERS, Q_LOC, Q_LOC), BF),
        ),
        in_specs=[SMEM]
        + [ANY] * 8
        + [
            pl.BlockSpec((nt, KEYROWS, step), lambda j: (0, 0, j)),
            pl.BlockSpec((PAIR_TOK, Q_LOC), lambda j: (0, 0)),
            pl.BlockSpec((PAIR_TOK, QKV), lambda j: (0, 0)),
        ],
        out_specs=(
            pl.BlockSpec((n, chunk, wide_f), lambda j: (0, 0, 0)),
            pl.BlockSpec((n, chunk, wide_b), lambda j: (0, 0, 0)),
            pl.BlockSpec((MEMBERS, Q_LOC, Q_LOC), lambda j: (0, 0, 0)),
        ),
        scratch_shapes=[
            pltpu.VMEM((nt, KEYROWS, width), BF),
            pltpu.VMEM((nt, KEYROWS, wide), BF),
            pltpu.SemaphoreType.DMA((4,)),
            pltpu.SemaphoreType.DMA((4,)),
        ],
        compiler_params=params(48),
        cost_estimate=cost(4 * 10**9, 16 << 20),
        name="attention_grads",
    )(table, *rows_b, *rows_m, a_all, heads, dqkv)


def pack_out_grads(table, base, pieces, part_f, part_b):
    n, chunk, wide_f = part_f.shape
    wide_b = part_b.shape[2]
    owners = n // MEMBERS

    def kernel(*refs):
        tab = refs[0]
        ins = refs[1 : 1 + MEMBERS]
        out_f, out_b, sems = refs[3 + MEMBERS :]
        copies = []
        for k in range(MEMBERS):
            for h in range(owners):
                owner = tab[base + 4 + k] * owners + h
                rows = pl.ds(h * chunk, chunk)
                copies.append(
                    pltpu.make_async_copy(
                        ins[k].at[rows, pl.ds(0, OUT_F)],
                        out_f.at[tab[base + 10 + owner], :, pl.ds(Q_LOC, OUT_F)],
                        sems.at[2 * (k * owners + h)],
                    )
                )
                copies.append(
                    pltpu.make_async_copy(
                        ins[k].at[rows, pl.ds(OUT_F, OUT_B)],
                        out_b.at[tab[base + 10 + n + owner], :, pl.ds(2 * KV_LOC, OUT_B)],
                        sems.at[2 * (k * owners + h) + 1],
                    )
                )
        for c in copies:
            c.start()
        wait_all(copies)

    return pl.pallas_call(
        kernel,
        out_shape=(
            jax.ShapeDtypeStruct(part_f.shape, BF),
            jax.ShapeDtypeStruct(part_b.shape, BF),
        ),
        in_specs=[SMEM] + [VM] * MEMBERS + [ANY, ANY],
        out_specs=(ANY, ANY),
        input_output_aliases={1 + MEMBERS: 0, 2 + MEMBERS: 1},
        scratch_shapes=[pltpu.SemaphoreType.DMA((2 * n,))],
        cost_estimate=cost(0, 3 << 20),
        name="pack_out_grads",
    )(table, *pieces, part_f, part_b)


def place_attention(places, shares):
    rows, width = shares[0].shape

    def kernel(*refs):
        tab = refs[0]
        ins = refs[1 : 1 + MEMBERS]
        gq, gk, gv, go, hold = refs[1 + MEMBERS :]
        for k in range(MEMBERS):
            hold[tab[k]] = ins[k][...].astype(F32)
        at = Q_LOC + OUT_F
        for j in range(MEMBERS):
            gq[:, j * Q_LOC : (j + 1) * Q_LOC] = hold[j, :, :Q_LOC]
            gk[:, j * KV_LOC : (j + 1) * KV_LOC] = hold[j, :, at : at + KV_LOC]
            gv[:, j * KV_LOC : (j + 1) * KV_LOC] = hold[j, :, at + KV_LOC : at + 2 * KV_LOC]
            go[:, j * Q_LOC : j * Q_LOC + OUT_F] = hold[j, :, Q_LOC:at]
            go[:, j * Q_LOC + OUT_F : (j + 1) * Q_LOC] = hold[j, :, at + 2 * KV_LOC :]

    return pl.pallas_call(
        kernel,
        out_shape=tuple(
            jax.ShapeDtypeStruct((rows, MEMBERS * size), F32)
            for size in (Q_LOC, KV_LOC, KV_LOC, Q_LOC)
        ),
        in_specs=[SMEM] + [VM] * MEMBERS,
        out_specs=(VM,) * 4,
        scratch_shapes=[pltpu.VMEM((MEMBERS, rows, width), F32)],
        cost_estimate=cost(0, 6 * MEMBERS * rows * width),
        name="place_attention",
    )(places, *shares)


def expert_kernel(table, base, slot, count, pieces, rows_b, rows_d, router, width, hidden, groups, ringed, offsets):
    many = len(pieces)
    n = many // 2
    half = 3 * hidden // 2
    nt = PAIR_TOK // KEYROWS
    tiles = PAIR_TOK // TILE
    per = TILE // KEYROWS
    step = TILE
    chunk = width // groups
    owners = step // chunk
    cuts = width // step
    wide = width + LANE

    def kernel(*refs):
        tab = refs[0]
        w_refs = refs[1 : 1 + many]
        b_refs = refs[1 + many : 5 + many]
        d_refs = refs[5 + many : 9 + many]
        r_ref = refs[9 + many]
        db, out = refs[10 + many : 12 + many]
        grads = refs[12 + many : 14 + many] if ringed else refs[12 + many : 13 + many]
        scratch = refs[14 + many :] if ringed else refs[13 + many :]
        w_v, b_v, d_v, dgu_v, gh_v, db_v, out_v, sem_w, sem_b, sem_d = scratch[:10]
        i = pl.program_id(0)

        def fetch(e):
            if many == 1:
                cols = pl.ds(e * 3 * hidden, 3 * hidden)
                return [pltpu.make_async_copy(w_refs[0].at[:, cols], w_v.at[e], sem_w.at[e])]
            copies = []
            for at in range(many):
                side = at // n
                rows = w_refs[at].shape[0]
                copies.append(
                    pltpu.make_async_copy(
                        w_refs[at].at[:, pl.ds(offsets[side] + e * half, half)],
                        w_v.at[
                            e,
                            pl.ds(pl.multiple_of(tab[at], 16), rows),
                            pl.ds(side * half, half),
                        ],
                        sem_w.at[e * many + at],
                    )
                )
            return copies

        @pl.when(i == 0)
        def _():
            cb = start_rows(b_refs, b_v, tab, base, sem_b)
            for e in range(count):
                for c in fetch(e):
                    c.start()
            cd = start_rows(d_refs, d_v, tab, base, sem_d)
            wait_all(cb)
            wait_all(cd)

        @pl.when(i < tiles)
        def _():
            at = pl.ds(i * per, per)
            b = b_v[at].reshape(TILE, width)
            mark = d_v[at, :, width:].reshape(TILE, LANE).astype(F32)
            lanes = lax.broadcasted_iota(jnp.int32, (TILE, LANE), 1)
            logits = jnp.where(mark > 0.0, dot(b, r_ref[...]), NEG)
            top = jnp.max(logits, axis=1, keepdims=True)
            weight = jnp.where(mark > 0.0, jnp.exp(logits - top), 0.0)
            gates = weight / jnp.sum(weight, axis=1, keepdims=True)
            rows = pl.ds(pl.multiple_of(i * TILE, TILE), TILE)

            def one(e, extra):
                for c in range(count):

                    @pl.when((i == 0) & (e == c))
                    def _(c=c):
                        wait_all(fetch(c))

                expert = tab[base + 9] + slot + e
                b = b_v[at].reshape(TILE, width)
                dy = d_v[at, :, :width].reshape(TILE, width)
                gate = jnp.sum(jnp.where(lanes == expert, gates, 0.0), axis=1, keepdims=True)
                gu = dot(b, w_v[e, :, : 2 * hidden])
                back = dot(dy, w_v[e, :, 2 * hidden :])
                g = gu[:, :hidden]
                u = gu[:, hidden:]
                sig = 1.0 / (1.0 + jnp.exp(-g))
                act = g * sig
                hb = (act * u).astype(BF)
                hf = hb.astype(F32)
                dgate = jnp.sum(hf * back, axis=1, keepdims=True)
                gh = (hf * gate).astype(BF)
                dh = back * gate
                dg = dh * u * (sig * (1.0 + g * (1.0 - sig)))
                dgu = jnp.concatenate([dg, dh * act], 1).astype(BF)
                dgu_v[e, rows, :] = dgu
                gh_v[e, rows, :] = gh
                y = dot_nt(dgu, w_v[e, :, : 2 * hidden])
                z = dot_nt(gh, w_v[e, :, 2 * hidden :])

                @pl.when(e == 0)
                def _():
                    db_v[...] = y
                    out_v[...] = z

                @pl.when(e > 0)
                def _():
                    db_v[...] += y
                    out_v[...] += z

                high = dgate.astype(BF).astype(F32)
                low = dgate - high
                return extra + jnp.where(
                    lanes == expert, high, jnp.where(lanes == expert + LANE // 2, low, 0.0)
                )

            extra = lax.fori_loop(0, count, one, jnp.zeros((TILE, LANE), F32))
            whole = slice(None)
            store_members(db, tab, base, whole, db_v[...].astype(BF), pl.ds(0, width))
            store_members(db, tab, base, whole, extra.astype(BF), pl.ds(width, LANE))
            store_members(out, tab, base, whole, out_v[...].astype(BF))

        @pl.when(i >= tiles)
        def _():
            cols = pl.ds(pl.multiple_of((i - tiles) * step, step), step)
            b = b_v[:, :, cols].reshape(PAIR_TOK, step)
            dy = d_v[:, :, cols].reshape(PAIR_TOK, step)
            if not ringed:
                grads[0][:, : 2 * hidden] = dot_tn(b, dgu_v[0]).astype(BF)
                grads[0][:, 2 * hidden :] = dot_tn(dy, gh_v[0]).astype(BF)
            else:
                g_v, sem_g = scratch[10:]
                j = i - tiles
                for e in range(count):
                    one = dot_tn(b, dgu_v[e]).astype(BF)
                    g_v[0, j, :, e * half : (e + 1) * half] = one[:, :half]
                    g_v[1, j, :, e * half : e * half + 2 * hidden - half] = one[:, half:]
                    two = dot_tn(dy, gh_v[e]).astype(BF)
                    g_v[1, j, :, e * half + 2 * hidden - half : (e + 1) * half] = two

                def send(j, h, side):
                    owner = j * owners + h
                    return pltpu.make_async_copy(
                        g_v.at[side, j, pl.ds(h * chunk, chunk)],
                        grads[side].at[tab[base + 10 + side * groups + owner]],
                        sem_g.at[side * groups + owner],
                    )

                for h in range(owners):
                    for side in range(2):
                        send(j, h, side).start()

                @pl.when(j == cuts - 1)
                def _():
                    for t in range(cuts):
                        for h in range(owners):
                            for side in range(2):
                                send(t, h, side).wait()

    if ringed:
        grad_specs = (ANY, ANY)
        grad_shapes = (jax.ShapeDtypeStruct((groups, chunk, count * half), BF),) * 2
        more = [
            pltpu.VMEM((2, cuts, step, count * half), BF),
            pltpu.SemaphoreType.DMA((2 * groups,)),
        ]
    else:
        grad_specs = (
            pl.BlockSpec((step, 3 * hidden), lambda i: (jnp.maximum(i - tiles, 0), 0)),
        )
        grad_shapes = (jax.ShapeDtypeStruct((width, 3 * hidden), BF),)
        more = []
    return pl.pallas_call(
        kernel,
        grid=(tiles + cuts,),
        out_shape=(
            jax.ShapeDtypeStruct((MEMBERS, nt, 32, wide), BF),
            jax.ShapeDtypeStruct((MEMBERS, nt, 32, width), BF),
        )
        + grad_shapes,
        in_specs=[SMEM] + [ANY] * (many + 8) + [pl.BlockSpec((width, LANE), lambda i: (0, 0))],
        out_specs=(
            pl.BlockSpec(
                (MEMBERS, per, 32, wide), lambda i: (0, jnp.minimum(i, tiles - 1), 0, 0)
            ),
            pl.BlockSpec(
                (MEMBERS, per, 32, width), lambda i: (0, jnp.minimum(i, tiles - 1), 0, 0)
            ),
        )
        + grad_specs,
        scratch_shapes=[
            pltpu.VMEM((count, width, 3 * hidden), BF),
            pltpu.VMEM((nt, KEYROWS, width), BF),
            pltpu.VMEM((nt, KEYROWS, wide), BF),
            pltpu.VMEM((count, PAIR_TOK, 2 * hidden), BF),
            pltpu.VMEM((count, PAIR_TOK, hidden), BF),
            pltpu.VMEM((TILE, width), F32),
            pltpu.VMEM((TILE, width), F32),
            pltpu.SemaphoreType.DMA((count * many,)),
            pltpu.SemaphoreType.DMA((4,)),
            pltpu.SemaphoreType.DMA((4,)),
        ]
        + more,
        compiler_params=params(58),
        cost_estimate=cost(17 * 10**9 * count, (12 + 14 * count) << 20, 10**6 * count),
        name="expert",
    )(table, *pieces, *rows_b, *rows_d, router)


def turn_out_weight(places, af, ab):
    n = len(af)
    rows = af[0].shape[0]

    def kernel(*refs):
        tab = refs[0]
        f_refs = refs[1 : 1 + n]
        b_refs = refs[1 + n : 1 + 2 * n]
        out, sems = refs[1 + 2 * n :]
        copies = []
        for s in range(n):
            at = pl.ds(pl.multiple_of(tab[n + s], 16), rows)
            copies.append(
                pltpu.make_async_copy(
                    f_refs[s].at[:, pl.ds(Q_LOC, OUT_F)],
                    out.at[tab[s], at, pl.ds(0, OUT_F)],
                    sems.at[s],
                )
            )
            at = pl.ds(pl.multiple_of(tab[3 * n + s], 16), rows)
            copies.append(
                pltpu.make_async_copy(
                    b_refs[s].at[:, pl.ds(2 * KV_LOC, OUT_B)],
                    out.at[tab[2 * n + s], at, pl.ds(OUT_F, OUT_B)],
                    sems.at[n + s],
                )
            )
        for c in copies:
            c.start()
        wait_all(copies)

    return pl.pallas_call(
        kernel,
        out_shape=jax.ShapeDtypeStruct((MEMBERS, Q_LOC, Q_LOC), BF),
        in_specs=[SMEM] + [ANY] * (2 * n),
        out_specs=VM,
        scratch_shapes=[pltpu.SemaphoreType.DMA((2 * n,))],
        cost_estimate=cost(0, 3 << 20),
        name="turn_out_weight",
    )(places, *af, *ab)


def ring_place(index, n):
    return jnp.where(index % 2 == 0, index // 2, n - 1 - index // 2)


def ring_index(place, n):
    return jnp.where(place < n // 2, 2 * place, 2 * (n - 1 - place) + 1)


def ring_pairs(n):
    ring = list(range(0, n, 2)) + list(range(n - 1, 0, -2))
    ahead = [(ring[i], ring[(i + 1) % n]) for i in range(n)]
    back = [(b, a) for a, b in ahead]
    return ahead, back


def after(value, *deps):
    return lax.optimization_barrier((value,) + deps)[0]


def swap(values, bits):
    return lax.ppermute(values, "seq", [(i, i ^ bits) for i in range(MEMBERS)])


def share_rows(values):
    across = swap(values, 2)
    return [values, swap(values, 1), across, swap(across, 1)]


def body(
    tokens,
    cotangent,
    routes,
    lengths,
    deal_order,
    attn_gain,
    query_weight,
    key_matrix,
    value_matrix,
    out_weight,
    moe_gain,
    router_weight,
    expert_weight,
):
    n = lax.axis_size("dp")
    group = lax.axis_index("dp")
    member = lax.axis_index("seq")
    slots, block, width = tokens.shape
    units = PAIR_TOK // (MEMBERS * block)
    local_rows = query_weight.shape[0]
    n_expert = router_weight.shape[1]
    hidden = expert_weight.shape[2] // 3
    per = n_expert // MEMBERS
    ahead, back = ring_pairs(n)
    natural = block == 32

    place = ring_place(group, n)
    steps = jnp.arange(n, dtype=jnp.int32)
    from_f = ring_index((place - steps) % n, n).astype(jnp.int32)
    from_b = ring_index((place + steps) % n, n).astype(jnp.int32)
    xors = jnp.bitwise_xor(jnp.arange(MEMBERS, dtype=jnp.int32), member)
    row_place = xors if natural else jnp.arange(MEMBERS, dtype=jnp.int32)
    first_seq = deal_order[2 * group]
    first_len = lengths[first_seq]
    first = (first_len // (MEMBERS * block)).reshape(1)
    base = 2 * n
    table = jnp.concatenate(
        [
            from_f * local_rows,
            from_b * local_rows,
            row_place,
            xors,
            jnp.stack([first_len, per * member]),
            (place - ring_place(steps, n)) % n,
            (ring_place(steps, n) - place) % n,
        ]
    ).astype(jnp.int32)
    share = n // MEMBERS
    out_places = jnp.concatenate(
        [
            jnp.bitwise_xor(from_f // share, member),
            from_f % share * local_rows,
            jnp.bitwise_xor(from_b // share, member),
            from_b % share * local_rows,
        ]
    ).astype(jnp.int32)

    sent_x = pick_rows(tokens, deal_order)
    dealt_x = lax.all_to_all(sent_x, "dp", split_axis=0, concat_axis=0, tiled=True)
    x_rows = take_rows(dealt_x, first, units)

    def cut(values, size):
        return lax.dynamic_slice_in_dim(values, member * size, size, axis=1).astype(BF)

    small = jnp.concatenate(
        [
            router_weight,
            jnp.zeros((local_rows, GAINS_AT - n_expert), F32),
            attn_gain[:, None],
            moe_gain[:, None],
            jnp.zeros((local_rows, LANE - GAINS_AT - 2), F32),
        ],
        1,
    ).astype(BF)
    out_cols = cut(out_weight, Q_LOC)
    attn_f = jnp.concatenate([cut(query_weight, Q_LOC), out_cols[:, :OUT_F], small], 1)
    attn_b = jnp.concatenate(
        [cut(key_matrix, KV_LOC), cut(value_matrix, KV_LOC), out_cols[:, OUT_F:]], 1
    )
    expert_first = expert_weight.transpose(1, 0, 2)
    expert_own = lax.dynamic_slice_in_dim(expert_first, per * member, per, axis=0).astype(BF)

    def rows_of(chunks):
        if natural:
            return chunks
        w = chunks[0].shape[2]
        whole = jnp.zeros((units, MEMBERS, block, w), BF)
        for k in range(MEMBERS):
            whole = lax.dynamic_update_slice(whole, chunks[k][:, None], (0, xors[k], 0, 0))
        whole = whole.reshape(PAIR_TOK // KEYROWS, MEMBERS, 32, w)
        return [whole[:, j] for j in range(MEMBERS)]

    def scatter_parts(parts):
        if natural:
            shaped = parts
        else:
            shaped = []
            for p in parts:
                rows = p.transpose(1, 0, 2, 3).reshape(units, MEMBERS, block, p.shape[3])
                shaped.append(
                    [
                        lax.dynamic_index_in_dim(rows, xors[k], axis=1, keepdims=False)
                        for k in range(MEMBERS)
                    ]
                )

        def part(k):
            total = None
            for p in shaped:
                one = p[k].astype(F32)
                total = one if total is None else total + one
            return total

        return part

    def scatter_near(part, *deps):
        far = swap(after(part(3).astype(BF), *deps), 1)
        near = swap(after(part(1).astype(BF), *deps), 1)
        hop = (part(2) + far.astype(F32)).astype(BF)
        return near, hop

    def scatter_end(part, near, cross):
        return part(0) + near.astype(F32) + cross.astype(F32)

    class Gather:
        def __init__(self, f, b):
            self.fs, self.bs = [f], [b]

        def step(self, *deps):
            if len(self.fs) < n:
                self.fs.append(lax.ppermute(after(self.fs[-1], *deps), "dp", ahead))
                self.bs.append(lax.ppermute(after(self.bs[-1], *deps), "dp", back))

        def last(self, ago=1):
            return self.fs[-ago], self.bs[-ago]

        def finish(self):
            while len(self.fs) < n:
                self.step()

    class Scatter:
        def __init__(self, part_f, part_b):
            self.parts = part_f, part_b
            self.sums = part_f(1), part_b(1)
            self.at = 1

        def step(self, *deps):
            if self.at < n:
                f = lax.ppermute(after(self.sums[0], *deps), "dp", ahead)
                b = lax.ppermute(after(self.sums[1], *deps), "dp", back)
                self.at += 1
                own = [part(self.at % n) for part in self.parts]
                self.sums = tuple(
                    (got.astype(F32) + mine.astype(F32)).astype(BF)
                    for got, mine in zip((f, b), own)
                )

        def finish(self):
            while self.at < n:
                self.step()
            return self.sums

    half = 3 * hidden // 2
    ring = Gather(
        after(jnp.concatenate([attn_f, expert_own[0, :, :half]], 1), sent_x),
        after(jnp.concatenate([attn_b, expert_own[0, :, half:]], 1), sent_x),
    )
    offsets = (attn_f.shape[1], attn_b.shape[1])
    sent_d = pick_marked(after(cotangent, sent_x), routes, deal_order)
    ring.step()
    ring.step(sent_d)
    x_across, x_near = swap(x_rows, 2), swap(x_rows, 1)
    ring.step(x_rows)
    dealt_d = lax.all_to_all(
        after(sent_d, *ring.last(2)), "dp", split_axis=0, concat_axis=0, tiled=True
    )
    ring.finish()
    ring_fs, ring_bs = ring.fs, ring.bs
    others = per - 1
    second = Gather(
        after(jnp.concatenate([expert_own[e, :, :half] for e in range(1, per)], 1), *ring.last()),
        after(jnp.concatenate([expert_own[e, :, half:] for e in range(1, per)], 1), *ring.last()),
    )
    second.step()
    turned = turn_out_weight(out_places, ring_fs, ring_bs)
    wout = [turned[0]] + [swap(turned[k], k) for k in range(1, MEMBERS)]

    row = jnp.arange(PAIR_TOK, dtype=jnp.int32)
    pos = row - jnp.where(row >= first_len, first_len, 0)
    freq = rope_base ** (-(jnp.arange(HEAD // 2, dtype=F32) * 2.0 / HEAD))
    angle = pos.astype(F32)[:, None] * freq[None, :]
    cosine = jnp.concatenate([jnp.cos(angle)] * 4, 1)
    sine = jnp.sin(angle)
    sine = jnp.concatenate([-sine, sine, -sine, sine], 1)

    rows_x = [after(x_rows, turned), x_near, x_across, swap(x_across, 1)]
    a_all, q, k, v, heads, router, gains = attention_forward(
        table, base, ring_fs, ring_bs, rows_of(rows_x), cosine, sine, width
    )
    second.step(heads)
    d_rows = take_rows(dealt_d, first, units)
    part = project_out(table, base, after(heads, d_rows, *second.last(2)), wout, width)
    gain_a = gains[0:1]
    gain_m = gains[1:2]
    mix = scatter_parts([part])
    mix_near, mix_hop = scatter_near(mix)
    mix_cross = swap(mix_hop, 2)
    second.step(mix_hop)
    middle = after(x_rows, *second.last(2)).astype(F32) + scatter_end(mix, mix_near, mix_cross)

    inverse = lax.rsqrt(jnp.mean(middle * middle, axis=-1, keepdims=True) + eps_norm)
    b_rows = (middle * inverse * gain_m).astype(BF)
    b_across, b_near = swap(b_rows, 2), swap(b_rows, 1)
    second.step(b_rows)
    d_own_rows = after(d_rows, b_rows, *second.last(2))
    d_across, d_near = swap(d_own_rows, 2), swap(d_own_rows, 1)
    second.step(b_across)
    second.finish()
    rows_b = rows_of([b_rows, b_near, b_across, swap(b_across, 1)])
    rows_d = rows_of([d_rows, d_near, d_across, swap(d_across, 1)])

    db, out, grad = expert_kernel(
        table,
        base,
        0,
        1,
        ring_fs + ring_bs,
        rows_b,
        rows_d,
        router,
        width,
        hidden,
        n,
        False,
        offsets,
    )
    dbs, outs = [db], [out]
    first_share = lax.psum_scatter(grad, "dp", scatter_dimension=0, tiled=True)
    db, out, grad_f, grad_b = expert_kernel(
        after(table, dbs[0]),
        base,
        1,
        others,
        second.fs + second.bs,
        rows_b,
        rows_d,
        router,
        width,
        hidden,
        n,
        True,
        (0, 0),
    )
    dbs.append(db)
    outs.append(out)
    shed = Scatter(lambda s: grad_f[s], lambda s: grad_b[s])
    shed.step()

    own_b = b_rows.reshape(units * block, width)
    mark = d_rows[:, :, width:].reshape(units * block, LANE).astype(F32)
    logits = dot(own_b, router)
    gates = jax.nn.softmax(jnp.where(mark > 0.0, logits, -jnp.inf), axis=-1)

    back_part = scatter_parts(dbs)
    back_near, back_hop = scatter_near(back_part)
    back_cross = swap(back_hop, 2)
    shed.step(back_hop)
    back_sum = scatter_end(back_part, back_near, back_cross).reshape(units * block, width + LANE)
    extra = back_sum[:, width:]
    dgate = extra + jnp.roll(extra, -(LANE // 2), axis=1)
    dgate = jnp.where(mark > 0.0, dgate, 0.0)
    dlogits = (gates * (dgate - jnp.sum(gates * dgate, axis=-1, keepdims=True))).astype(BF)
    db_own = back_sum[:, :width] + dot_nt(dlogits, router)
    mid_own = middle.reshape(units * block, width)
    inv_own = inverse.reshape(units * block, 1)
    d_own = d_rows[:, :, :width].reshape(units * block, width).astype(F32)
    normed = mid_own * inv_own
    scaled = db_own * gain_m
    dmiddle = d_own + inv_own * (
        scaled - normed * jnp.mean(scaled * normed, axis=-1, keepdims=True)
    )
    dmix = jnp.concatenate([dmiddle.astype(BF), dlogits], 1).reshape(units, block, width + LANE)
    m_across, m_near = swap(dmix, 2), swap(dmix, 1)
    shed.step(dmix)
    out_part = scatter_parts(outs)
    out_near, out_hop = scatter_near(out_part, dmix)
    m_far = swap(m_across, 1)
    out_cross = swap(after(out_hop, m_across), 2)
    shed.step(m_across)
    result = middle + scatter_end(out_part, out_near, out_cross)
    sent_out = spread_rows(result.astype(BF), first, slots)
    back_out = lax.all_to_all(sent_out, "dp", split_axis=0, concat_axis=0, tiled=True)
    rows_m = rows_of([after(dmix, sent_out, first_share, *shed.sums), m_near, m_across, m_far])
    first_shares = share_rows(first_share)

    da, dqkv = attention_backward(
        table, base, ring_fs, ring_bs, rows_m, wout, q, k, v, cosine, sine, width
    )
    shed.step(da)
    da_part = scatter_parts([da])
    da_near, da_hop = scatter_near(da_part, back_out)
    da_cross = swap(da_hop, 2)
    half_f, half_b, gout = attention_grads(
        table, base, a_all, rows_b, rows_m, after(heads, da_hop), dqkv, width, n
    )
    gout = after(gout, da_cross)
    pieces = [gout[0]] + [swap(gout[kk], kk) for kk in range(1, MEMBERS)]
    full_f, full_b = pack_out_grads(table, base, pieces, half_f, half_b)
    da_own = scatter_end(da_part, da_near, da_cross).reshape(units * block, width)
    x_own = x_rows.reshape(units * block, width).astype(F32)
    inv_x = lax.rsqrt(jnp.mean(x_own * x_own, axis=-1, keepdims=True) + eps_norm)
    normed_x = x_own * inv_x
    scaled_x = da_own * gain_a
    grad_x = dmiddle + inv_x * (
        scaled_x - normed_x * jnp.mean(scaled_x * normed_x, axis=-1, keepdims=True)
    )

    sent_grad = spread_rows(grad_x.reshape(units, block, width).astype(BF), first, slots)
    back_grad = lax.all_to_all(sent_grad, "dp", split_axis=0, concat_axis=0, tiled=True)
    output = place_rows(after(back_out, sent_grad), deal_order)
    grad_tokens = place_rows(back_grad, deal_order)

    pair_f, pair_b = shed.finish()
    pair_share = jnp.concatenate([pair_f, pair_b], 1)
    pair_shares = share_rows(pair_share)
    grad_first, gain_first = place_experts(
        xors, first_shares, expert_first, 0, 1, False, per, None
    )
    grad_first, gain_rest = place_experts(
        xors, pair_shares, expert_first, 1, others, True, per, grad_first
    )
    full_f = after(full_f, pair_f, sent_grad)
    full_b = after(full_b, pair_b, sent_grad)
    final = Scatter(lambda s: full_f[s], lambda s: full_b[s])
    final.step()
    final.step(output)
    final.step()
    final.step()
    final.step(gain_rest)
    final.step(grad_tokens)
    share_f, share_b = final.finish()
    small_grad = share_b[:, full_b.shape[2] - LANE :]
    shares = share_rows(jnp.concatenate([share_f, share_b[:, : full_b.shape[2] - LANE]], 1))

    grad_query, grad_key, grad_value, grad_out = place_attention(xors, shares)
    grad_router = small_grad[:, :n_expert].astype(F32)
    grad_experts = grad_first.transpose(1, 0, 2)

    def low(values):
        return values.astype(BF).astype(F32)

    grad_attn_gain = (
        jnp.sum(low(query_weight) * grad_query, axis=1)
        + jnp.sum(low(key_matrix) * grad_key, axis=1)
        + jnp.sum(low(value_matrix) * grad_value, axis=1)
    ) / low(attn_gain)
    grad_moe_gain = (
        jnp.sum(gain_first + gain_rest, axis=1)
        + jnp.sum(low(router_weight) * grad_router, axis=1)
    ) / low(moe_gain)

    return (
        output,
        grad_tokens,
        grad_attn_gain,
        grad_query,
        grad_key,
        grad_value,
        grad_out,
        grad_moe_gain,
        grad_router,
        grad_experts,
    )


def solution(mesh):
    rows = P(None, ("dp", "seq"), None)
    placed = (
        rows,
        rows,
        rows,
        P(),
        P(),
        P("dp"),
        P("dp", None),
        P("dp", None),
        P("dp", None),
        P("dp", None),
        P("dp"),
        P("dp", None),
        P("dp", None, None),
    )
    return jax.shard_map(
        body,
        mesh=mesh,
        in_specs=placed,
        out_specs=(
            rows,
            rows,
            P("dp"),
            P("dp", None),
            P("dp", None),
            P("dp", None),
            P("dp", None),
            P("dp"),
            P("dp", None),
            P("dp", None, None),
        ),
        check_vma=False,
    )
```

```python
import jax
import jax.numpy as jnp
from jax import lax
from jax.experimental import pallas as pl
from jax.experimental.pallas import tpu as pltpu
from jax.sharding import PartitionSpec as P

QUERY_HEADS = 24
KEY_VALUE_HEADS = 8
HEAD = 64
PAIR_TOK = 1152
MEMBERS = 4
LANE = 128
TILE = 384
KEYROWS = 128
UNIT = PAIR_TOK // KEYROWS // 1
eps_norm = 1e-06
rope_base = 10000.0
NEG = -1e30
BF = jnp.bfloat16
F32 = jnp.float32

Q_LOC = QUERY_HEADS // MEMBERS * HEAD
KV_LOC = KEY_VALUE_HEADS // MEMBERS * HEAD
KVH = KEY_VALUE_HEADS // MEMBERS
GROUP = QUERY_HEADS // KEY_VALUE_HEADS
QKV = Q_LOC + 2 * KV_LOC
OUT_F = LANE
OUT_B = Q_LOC - OUT_F
GAINS_AT = 64

ANY = pl.BlockSpec(memory_space=pl.ANY)
SMEM = pl.BlockSpec(memory_space=pltpu.SMEM)
VM = pl.BlockSpec(memory_space=pltpu.VMEM)


def params(megabytes):
    return pltpu.CompilerParams(vmem_limit_bytes=megabytes << 20)


def cost(flops, moved, trans=0):
    return pl.CostEstimate(flops=flops // 100, bytes_accessed=moved // 100, transcendentals=trans // 100)


def dot(a, b):
    return lax.dot_general(a, b, (((1,), (0,)), ((), ())), preferred_element_type=F32)


def dot_nt(a, b):
    return lax.dot_general(a, b, (((1,), (1,)), ((), ())), preferred_element_type=F32)


def dot_tn(a, b):
    return lax.dot_general(a, b, (((0,), (0,)), ((), ())), preferred_element_type=F32)


def pick_rows(values, order):
    count = values.shape[0]

    def kernel(order_ref, in_ref, out_ref, sems):
        copies = [
            pltpu.make_async_copy(in_ref.at[order_ref[i]], out_ref.at[i], sems.at[i])
            for i in range(count)
        ]
        for c in copies:
            c.start()
        wait_all(copies)

    return pl.pallas_call(
        kernel,
        out_shape=jax.ShapeDtypeStruct(values.shape, values.dtype),
        in_specs=[SMEM, ANY],
        out_specs=VM,
        scratch_shapes=[pltpu.SemaphoreType.DMA((count,))],
        cost_estimate=cost(0, 4 * values.size),
        name="pick",
    )(order, values)


def pick_marked(values, routes, order):
    count, block, width = values.shape
    topk = routes.shape[2]

    def kernel(order_ref, in_ref, route_ref, out_ref, sems):
        copies = [
            pltpu.make_async_copy(
                in_ref.at[order_ref[i]], out_ref.at[i, :, pl.ds(0, width)], sems.at[i]
            )
            for i in range(count)
        ]
        for c in copies:
            c.start()
        lanes = lax.broadcasted_iota(jnp.int32, (block, LANE), 1)

        def mark_one(i, carry):
            routed = route_ref[order_ref[i]]
            mark = jnp.zeros((block, LANE), F32)
            for k in range(topk):
                mark = mark + jnp.where(routed[:, k : k + 1] == lanes, 1.0, 0.0)
            out_ref[i, :, width:] = mark.astype(BF)
            return carry

        lax.fori_loop(0, count, mark_one, 0)
        wait_all(copies)

    return pl.pallas_call(
        kernel,
        out_shape=jax.ShapeDtypeStruct((count, block, width + LANE), values.dtype),
        in_specs=[SMEM, ANY, VM],
        out_specs=VM,
        scratch_shapes=[pltpu.SemaphoreType.DMA((count,))],
        cost_estimate=cost(0, 4 * values.size),
        name="pick_marked",
    )(order, values, routes)


def take_rows(dealt, first, units):
    _, block, width = dealt.shape

    def kernel(first_ref, in_ref, out_ref, sems):
        copies = []
        for t in range(units):
            source = jnp.where(t < first_ref[0], 2 * t, 2 * (t - first_ref[0]) + 1)
            copies.append(pltpu.make_async_copy(in_ref.at[source], out_ref.at[t], sems.at[t]))
            copies[-1].start()
        wait_all(copies)

    return pl.pallas_call(
        kernel,
        out_shape=jax.ShapeDtypeStruct((units, block, width), BF),
        in_specs=[SMEM, ANY],
        out_specs=VM,
        scratch_shapes=[pltpu.SemaphoreType.DMA((units,))],
        cost_estimate=cost(0, 4 * units * block * width),
        name="take_rows",
    )(first, dealt)


def spread_rows(rows, first, slots):
    units, block, width = rows.shape

    def kernel(first_ref, in_ref, out_ref):
        for i in range(slots):
            u = i // 2 if i % 2 == 0 else first_ref[0] + i // 2
            limit = first_ref[0] if i % 2 == 0 else units - first_ref[0]
            keep = i // 2 < limit

            @pl.when(keep)
            def _():
                out_ref[i] = in_ref[jnp.minimum(u, units - 1)]

            @pl.when(jnp.logical_not(keep))
            def _():
                out_ref[i] = jnp.zeros((block, width), BF)

    return pl.pallas_call(
        kernel,
        out_shape=jax.ShapeDtypeStruct((slots, block, width), BF),
        in_specs=[SMEM, VM],
        out_specs=VM,
        cost_estimate=cost(0, 4 * slots * block * width),
        name="spread_rows",
    )(first, rows)


def place_rows(values, order):
    count, block, width = values.shape

    def kernel(order_ref, in_ref, out_ref, hold, sems):
        copies = []
        for j in range(count):
            hold[j] = in_ref[j].astype(F32)
            copies.append(
                pltpu.make_async_copy(hold.at[j], out_ref.at[order_ref[j]], sems.at[j])
            )
            copies[-1].start()
        wait_all(copies)

    return pl.pallas_call(
        kernel,
        out_shape=jax.ShapeDtypeStruct(values.shape, F32),
        in_specs=[SMEM, VM],
        out_specs=ANY,
        scratch_shapes=[
            pltpu.VMEM(values.shape, F32),
            pltpu.SemaphoreType.DMA((count,)),
        ],
        cost_estimate=cost(0, 6 * values.size),
        name="place_rows",
    )(order, values)


def place_experts(places, shares, weight, lo, count, split, per, total):
    rows = shares[0].shape[0]
    width = shares[0].shape[1] // count
    half = width // 2
    used = 2 * width // 3

    def kernel(*refs):
        tab = refs[0]
        ins = refs[1 : 1 + MEMBERS]
        weight_ref = refs[1 + MEMBERS]
        out, gain, hold, w_v, sems, sem_w = refs[-6:]
        loads = []
        for k in range(MEMBERS):
            for e in range(count):
                at = k * count + e
                loads.append(
                    pltpu.make_async_copy(
                        weight_ref.at[tab[k] * per + lo + e, :, pl.ds(0, used)],
                        w_v.at[tab[k] * count + e],
                        sem_w.at[at],
                    )
                )
                loads[-1].start()
        copies = []
        for k in range(MEMBERS):
            for e in range(count):
                at = tab[k] * count + e
                for side in range(2):
                    col = (side * count + e) * half if split else e * width + side * half
                    hold[at, :, side * half : (side + 1) * half] = ins[k][
                        :, col : col + half
                    ].astype(F32)
                copies.append(
                    pltpu.make_async_copy(
                        hold.at[at], out.at[tab[k] * per + lo + e], sems.at[k * count + e]
                    )
                )
                copies[-1].start()
        wait_all(loads)
        gain[...] = jnp.zeros_like(gain)

        def add(at, carry):
            total = jnp.zeros((rows, LANE), F32)
            for c in range(used // LANE):
                cols = slice(c * LANE, (c + 1) * LANE)
                total = total + w_v[at, :, cols].astype(BF).astype(F32) * hold[at, :, cols]
            gain[...] += total
            return carry

        lax.fori_loop(0, MEMBERS * count, add, 0)
        wait_all(copies)

    before = [] if total is None else [total]
    return pl.pallas_call(
        kernel,
        out_shape=(
            jax.ShapeDtypeStruct((MEMBERS * per, rows, width), F32),
            jax.ShapeDtypeStruct((rows, LANE), F32),
        ),
        in_specs=[SMEM] + [VM] * MEMBERS + [ANY] * (1 + len(before)),
        out_specs=(ANY, VM),
        input_output_aliases={2 + MEMBERS: 0} if before else {},
        scratch_shapes=[
            pltpu.VMEM((MEMBERS * count, rows, width), F32),
            pltpu.VMEM((MEMBERS * count, rows, used), F32),
            pltpu.SemaphoreType.DMA((MEMBERS * count,)),
            pltpu.SemaphoreType.DMA((MEMBERS * count,)),
        ],
        compiler_params=params(40),
        cost_estimate=cost(0, 6 * MEMBERS * count * rows * width),
        name="place_experts",
    )(places, *shares, weight, *before)


def start_rows(refs, scratch, table, at, sems):
    copies = []
    for k in range(MEMBERS):
        place = pl.multiple_of(table[at + k] * 32, 32)
        copies.append(
            pltpu.make_async_copy(refs[k], scratch.at[:, pl.ds(place, 32), :], sems.at[k])
        )
        copies[-1].start()
    return copies


def start_weights(refs_f, refs_b, wf, wb, scratch, table, sems):
    copies = []
    n = len(refs_f)
    for s in range(n):
        rows = refs_f[s].shape[0]
        row_f = pl.multiple_of(table[s], 16)
        row_b = pl.multiple_of(table[n + s], 16)
        copies.append(
            pltpu.make_async_copy(
                refs_f[s].at[:, pl.ds(0, wf)],
                scratch.at[pl.ds(row_f, rows), pl.ds(0, wf)],
                sems.at[s],
            )
        )
        copies.append(
            pltpu.make_async_copy(
                refs_b[s].at[:, pl.ds(0, wb)],
                scratch.at[pl.ds(row_b, rows), pl.ds(wf, wb)],
                sems.at[n + s],
            )
        )
    for c in copies:
        c.start()
    return copies


def start_out(refs, scratch, table, at, sems):
    copies = []
    for k in range(MEMBERS):
        copies.append(pltpu.make_async_copy(refs[k], scratch.at[table[at + k]], sems.at[k]))
        copies[-1].start()
    return copies


def store_members(out, table, at, tiles, values, cols=None):
    per = values.shape[0] // KEYROWS
    shaped = values.reshape(per, KEYROWS, values.shape[1])
    for j in range(MEMBERS):
        piece = shaped[:, j * 32 : (j + 1) * 32]
        if cols is None:
            out[table[at + j], tiles] = piece
        else:
            out[table[at + j], tiles, :, cols] = piece


def wait_all(copies):
    for c in copies:
        c.wait()


def turn(values, cosine, sine):
    width = values.shape[1]
    lanes = lax.broadcasted_iota(jnp.int32, values.shape, 1)
    low = pltpu.roll(values, width - HEAD // 2, 1)
    high = pltpu.roll(values, HEAD // 2, 1)
    swapped = jnp.where(lanes % HEAD < HEAD // 2, low, high)
    reps = width // LANE
    return values * jnp.concatenate([cosine] * reps, 1) + swapped * jnp.concatenate([sine] * reps, 1)


def bias_for(t, extent, first_len):
    gi = lax.broadcasted_iota(jnp.int32, (KEYROWS, extent), 0) + t * KEYROWS
    gj = lax.broadcasted_iota(jnp.int32, (KEYROWS, extent), 1)
    allowed = (gj <= gi) & ((gi < first_len) | (gj >= first_len))
    return jnp.concatenate([jnp.where(allowed, 0.0, NEG)] * GROUP, 0)


def attention_forward(table, base, af, ab, rows_x, cosine, sine, width):
    n = len(af)
    tiles = PAIR_TOK // TILE
    per = TILE // KEYROWS
    nt = PAIR_TOK // KEYROWS
    chunk = af[0].shape[0]

    def kernel(*refs):
        tab = refs[0]
        f_refs = refs[1 : 1 + n]
        b_refs = refs[1 + n : 1 + 2 * n]
        x_refs = refs[1 + 2 * n : 5 + 2 * n]
        cos_ref, sin_ref = refs[5 + 2 * n : 7 + 2 * n]
        a_out, q_out, k_out, v_out, heads, small, gains = refs[7 + 2 * n : 14 + 2 * n]
        w_v, sem_x, sem_w, sem_s = refs[14 + 2 * n :]
        cs = []
        for s in range(n):
            row = pl.ds(pl.multiple_of(tab[s], 16), chunk)
            cs.append(
                pltpu.make_async_copy(
                    f_refs[s].at[:, pl.ds(Q_LOC + OUT_F, LANE)], small.at[row, :], sem_s.at[s]
                )
            )
            cs[-1].start()
        cw = start_weights(f_refs, b_refs, Q_LOC, 2 * KV_LOC, w_v, tab, sem_w)
        cx = start_rows(x_refs, a_out, tab, base, sem_x)
        wait_all(cs)
        pick = lax.broadcasted_iota(jnp.int32, (8, LANE), 1)
        pick = pick == lax.broadcasted_iota(jnp.int32, (8, LANE), 0) + GAINS_AT
        gains[...] = dot_nt(pick.astype(F32).astype(BF), small[...])
        wait_all(cw)
        wait_all(cx)
        first_len = tab[base + 8]

        def project(i, carry):
            at = pl.ds(i * per, per)
            x = a_out[at].reshape(TILE, width).astype(F32)
            scale = lax.rsqrt(jnp.mean(x * x, axis=-1, keepdims=True) + eps_norm)
            block = (x * scale * gains[0:1, :]).astype(BF)
            a_out[at] = block.reshape(per, KEYROWS, width)
            y = dot(block, w_v[...])
            rows = pl.ds(pl.multiple_of(i * TILE, TILE), TILE)
            turned = turn(y[:, : Q_LOC + KV_LOC], cos_ref[rows, :], sin_ref[rows, :])
            q = (turned[:, :Q_LOC] * 0.125).astype(BF)
            k = turned[:, Q_LOC:].astype(BF)
            v = y[:, Q_LOC + KV_LOC :].astype(BF)
            for j in range(KVH):
                k_out[j, rows, :] = k[:, j * HEAD : (j + 1) * HEAD]
                v_out[j, rows, :] = v[:, j * HEAD : (j + 1) * HEAD]
                for h in range(GROUP):
                    c = (j * GROUP + h) * HEAD
                    for r in range(per):
                        q_out[j, i * per + r, h * KEYROWS : (h + 1) * KEYROWS, :] = q[
                            r * KEYROWS : (r + 1) * KEYROWS, c : c + HEAD
                        ]
            return carry

        lax.fori_loop(0, tiles, project, 0)
        for c in range(tiles):
            extent = (c + 1) * TILE

            def attend(i, carry, c=c, extent=extent):
                t = c * per + i
                bias = bias_for(t, extent, first_len)
                mixed = []
                for j in range(KVH):
                    s = dot_nt(q_out[j, t], k_out[j, :extent, :]) + bias
                    top = jnp.max(s, axis=1, keepdims=True)
                    p = jnp.exp(s - top)
                    total = jnp.sum(p, axis=1, keepdims=True)
                    o = dot(p.astype(BF), v_out[j, :extent, :]) / total
                    mixed += [o[h * KEYROWS : (h + 1) * KEYROWS] for h in range(GROUP)]
                rows = pl.ds(pl.multiple_of(t * KEYROWS, KEYROWS), KEYROWS)
                heads[rows, :] = jnp.concatenate(mixed, 1).astype(BF)
                return carry

            lax.fori_loop(0, per, attend, 0)

    return pl.pallas_call(
        kernel,
        out_shape=(
            jax.ShapeDtypeStruct((nt, KEYROWS, width), BF),
            jax.ShapeDtypeStruct((KVH, nt, GROUP * KEYROWS, HEAD), BF),
            jax.ShapeDtypeStruct((KVH, PAIR_TOK, HEAD), BF),
            jax.ShapeDtypeStruct((KVH, PAIR_TOK, HEAD), BF),
            jax.ShapeDtypeStruct((PAIR_TOK, Q_LOC), BF),
            jax.ShapeDtypeStruct((width, LANE), BF),
            jax.ShapeDtypeStruct((8, width), F32),
        ),
        in_specs=[SMEM] + [ANY] * (2 * n + 4) + [VM, VM],
        out_specs=(VM,) * 7,
        scratch_shapes=[
            pltpu.VMEM((width, QKV), BF),
            pltpu.SemaphoreType.DMA((4,)),
            pltpu.SemaphoreType.DMA((2 * n,)),
            pltpu.SemaphoreType.DMA((n,)),
        ],
        compiler_params=params(48),
        cost_estimate=cost(12 * 10**9, 14 << 20, 5 * 10**6),
        name="attention_forward",
    )(table, *af, *ab, *rows_x, cosine, sine)


def project_out(table, base, heads, wout, width):
    tiles = PAIR_TOK // TILE
    per = TILE // KEYROWS
    nt = PAIR_TOK // KEYROWS

    def kernel(tab, heads, *refs):
        o_refs, (part, o_v, sem_o) = refs[:MEMBERS], refs[MEMBERS:]
        wait_all(start_out(o_refs, o_v, tab, base + 4, sem_o))
        for i in range(tiles):
            h = heads[i * TILE : (i + 1) * TILE, :]
            for j in range(MEMBERS):
                y = dot(h, o_v[j]).astype(BF)
                store_members(
                    part, tab, base, pl.ds(i * per, per), y, pl.ds(j * Q_LOC, Q_LOC)
                )

    return pl.pallas_call(
        kernel,
        out_shape=jax.ShapeDtypeStruct((MEMBERS, nt, 32, width), BF),
        in_specs=[SMEM, VM] + [ANY] * MEMBERS,
        out_specs=VM,
        scratch_shapes=[
            pltpu.VMEM((MEMBERS, Q_LOC, Q_LOC), BF),
            pltpu.SemaphoreType.DMA((4,)),
        ],
        compiler_params=params(24),
        cost_estimate=cost(2 * 10**9, 6 << 20),
        name="project_out",
    )(table, heads, *wout)


def attention_backward(table, base, af, ab, rows_m, wout, q, k, v, cosine, sine, width):
    n = len(af)
    tiles = PAIR_TOK // TILE
    per = TILE // KEYROWS
    nt = PAIR_TOK // KEYROWS
    wide = rows_m[0].shape[2]

    def kernel(*refs):
        tab = refs[0]
        f_refs = refs[1 : 1 + n]
        b_refs = refs[1 + n : 1 + 2 * n]
        m_refs = refs[1 + 2 * n : 5 + 2 * n]
        o_refs = refs[5 + 2 * n : 9 + 2 * n]
        q_ref, k_ref, v_ref, cos_ref, sin_ref = refs[9 + 2 * n : 14 + 2 * n]
        da, dqkv = refs[14 + 2 * n : 16 + 2 * n]
        m_v, w_v, o_v, dh_s, dq_s, dk_s, dv_s, sem_m, sem_w, sem_o = refs[16 + 2 * n :]
        cm = start_rows(m_refs, m_v, tab, base, sem_m)
        co = start_out(o_refs, o_v, tab, base + 4, sem_o)
        cw = start_weights(f_refs, b_refs, Q_LOC, 2 * KV_LOC, w_v, tab, sem_w)
        dk_s[...] = jnp.zeros_like(dk_s)
        dv_s[...] = jnp.zeros_like(dv_s)
        wait_all(co)
        wait_all(cm)
        first_len = tab[base + 8]

        def heads_back(i, carry):
            total = None
            for j in range(MEMBERS):
                block = m_v[pl.ds(i * per, per), :, j * Q_LOC : (j + 1) * Q_LOC]
                y = dot_nt(block.reshape(TILE, Q_LOC), o_v[j])
                total = y if total is None else total + y
            total = total.astype(BF)
            for j in range(KVH):
                for h in range(GROUP):
                    c = (j * GROUP + h) * HEAD
                    for r in range(per):
                        dh_s[j, i * per + r, h * KEYROWS : (h + 1) * KEYROWS, :] = total[
                            r * KEYROWS : (r + 1) * KEYROWS, c : c + HEAD
                        ]
            return carry

        lax.fori_loop(0, tiles, heads_back, 0)
        for c in range(tiles):
            extent = (c + 1) * TILE

            def attend(i, carry, c=c, extent=extent):
                t = c * per + i
                bias = bias_for(t, extent, first_len)
                for j in range(KVH):
                    qb = q_ref[j, t]
                    db = dh_s[j, t]
                    kb = k_ref[j, :extent, :]
                    s = dot_nt(qb, kb) + bias
                    top = jnp.max(s, axis=1, keepdims=True)
                    p = jnp.exp(s - top)
                    p = p * (1.0 / jnp.sum(p, axis=1, keepdims=True))
                    dp = dot_nt(db, v_ref[j, :extent, :])
                    prod = p * dp
                    delta = jnp.sum(prod, axis=1, keepdims=True)
                    ds = (prod - p * delta).astype(BF)
                    dq_s[j, t] = dot(ds, kb) * 0.125
                    dk_s[j, :extent, :] += dot_tn(ds, qb)
                    dv_s[j, :extent, :] += dot_tn(p.astype(BF), db)
                return carry

            lax.fori_loop(0, per, attend, 0)
        wait_all(cw)

        def inputs_back(i, carry):
            rows = pl.ds(pl.multiple_of(i * TILE, TILE), TILE)
            cols = []
            for j in range(KVH):
                for h in range(GROUP):
                    cols.append(
                        jnp.concatenate(
                            [
                                dq_s[j, i * per + r, h * KEYROWS : (h + 1) * KEYROWS, :]
                                for r in range(per)
                            ],
                            0,
                        )
                    )
            cols += [dk_s[j, rows, :] for j in range(KVH)]
            joined = jnp.concatenate(cols, 1).astype(BF).astype(F32)
            turned = turn(joined, cos_ref[rows, :], -sin_ref[rows, :])
            value = jnp.concatenate([dv_s[j, rows, :] for j in range(KVH)], 1)
            out = jnp.concatenate([turned, value], 1).astype(BF)
            dqkv[rows, :] = out
            y = dot_nt(out, w_v[...]).astype(BF)
            store_members(da, tab, base, pl.ds(i * per, per), y)
            return carry

        lax.fori_loop(0, tiles, inputs_back, 0)

    return pl.pallas_call(
        kernel,
        out_shape=(
            jax.ShapeDtypeStruct((MEMBERS, nt, 32, width), BF),
            jax.ShapeDtypeStruct((PAIR_TOK, QKV), BF),
        ),
        in_specs=[SMEM] + [ANY] * (2 * n + 8) + [VM] * 5,
        out_specs=(VM,) * 2,
        scratch_shapes=[
            pltpu.VMEM((nt, KEYROWS, wide), BF),
            pltpu.VMEM((width, QKV), BF),
            pltpu.VMEM((MEMBERS, Q_LOC, Q_LOC), BF),
            pltpu.VMEM((KVH, nt, GROUP * KEYROWS, HEAD), BF),
            pltpu.VMEM((KVH, nt, GROUP * KEYROWS, HEAD), F32),
            pltpu.VMEM((KVH, PAIR_TOK, HEAD), F32),
            pltpu.VMEM((KVH, PAIR_TOK, HEAD), F32),
            pltpu.SemaphoreType.DMA((4,)),
            pltpu.SemaphoreType.DMA((2 * n,)),
            pltpu.SemaphoreType.DMA((4,)),
        ],
        compiler_params=params(56),
        cost_estimate=cost(20 * 10**9, 16 << 20, 5 * 10**6),
        name="attention_backward",
    )(table, *af, *ab, *rows_m, *wout, q, k, v, cosine, sine)


def attention_grads(table, base, a_all, rows_b, rows_m, heads, dqkv, width, n):
    nt = PAIR_TOK // KEYROWS
    step = Q_LOC
    chunk = width // n
    owners = step // chunk
    wide = rows_m[0].shape[2]
    wide_f = Q_LOC + OUT_F
    wide_b = 2 * KV_LOC + OUT_B + LANE

    def kernel(*refs):
        tab = refs[0]
        b_refs, m_refs = refs[1:5], refs[5:9]
        a_ref, heads_ref, d_ref = refs[9:12]
        gf, gb, go = refs[12:15]
        b_v, m_v, sem_b, sem_m = refs[15:]
        j = pl.program_id(0)

        @pl.when(j == 0)
        def _():
            cb = start_rows(b_refs, b_v, tab, base, sem_b)
            cm = start_rows(m_refs, m_v, tab, base, sem_m)
            wait_all(cb)
            wait_all(cm)

        cols = pl.ds(pl.multiple_of(j * step, step), step)
        a = a_ref[...].reshape(PAIR_TOK, step)
        gq = dot_tn(a, d_ref[...]).astype(BF)
        b = b_v[:, :, cols].reshape(PAIR_TOK, step)
        gr = dot_tn(b, m_v[:, :, width:].reshape(PAIR_TOK, LANE)).astype(BF)
        for h in range(owners):
            rows = slice(h * chunk, (h + 1) * chunk)
            to_f = tab[base + 10 + j * owners + h]
            to_b = tab[base + 10 + n + j * owners + h]
            gf[to_f, :, :Q_LOC] = gq[rows, :Q_LOC]
            gb[to_b, :, : 2 * KV_LOC] = gq[rows, Q_LOC:]
            gb[to_b, :, 2 * KV_LOC + OUT_B :] = gr[rows, :]
        m = m_v[:, :, cols].reshape(PAIR_TOK, step)
        go[tab[base + 4 + j]] = dot_tn(heads_ref[...], m).astype(BF)

    return pl.pallas_call(
        kernel,
        grid=(width // step,),
        out_shape=(
            jax.ShapeDtypeStruct((n, chunk, wide_f), BF),
            jax.ShapeDtypeStruct((n, chunk, wide_b), BF),
            jax.ShapeDtypeStruct((MEMBERS, Q_LOC, Q_LOC), BF),
        ),
        in_specs=[SMEM]
        + [ANY] * 8
        + [
            pl.BlockSpec((nt, KEYROWS, step), lambda j: (0, 0, j)),
            pl.BlockSpec((PAIR_TOK, Q_LOC), lambda j: (0, 0)),
            pl.BlockSpec((PAIR_TOK, QKV), lambda j: (0, 0)),
        ],
        out_specs=(
            pl.BlockSpec((n, chunk, wide_f), lambda j: (0, 0, 0)),
            pl.BlockSpec((n, chunk, wide_b), lambda j: (0, 0, 0)),
            pl.BlockSpec((MEMBERS, Q_LOC, Q_LOC), lambda j: (0, 0, 0)),
        ),
        scratch_shapes=[
            pltpu.VMEM((nt, KEYROWS, width), BF),
            pltpu.VMEM((nt, KEYROWS, wide), BF),
            pltpu.SemaphoreType.DMA((4,)),
            pltpu.SemaphoreType.DMA((4,)),
        ],
        compiler_params=params(48),
        cost_estimate=cost(4 * 10**9, 16 << 20),
        name="attention_grads",
    )(table, *rows_b, *rows_m, a_all, heads, dqkv)


def pack_out_grads(table, base, pieces, part_f, part_b):
    n, chunk, wide_f = part_f.shape
    wide_b = part_b.shape[2]
    owners = n // MEMBERS

    def kernel(*refs):
        tab = refs[0]
        ins = refs[1 : 1 + MEMBERS]
        out_f, out_b, sems = refs[3 + MEMBERS :]
        copies = []
        for k in range(MEMBERS):
            for h in range(owners):
                owner = tab[base + 4 + k] * owners + h
                rows = pl.ds(h * chunk, chunk)
                copies.append(
                    pltpu.make_async_copy(
                        ins[k].at[rows, pl.ds(0, OUT_F)],
                        out_f.at[tab[base + 10 + owner], :, pl.ds(Q_LOC, OUT_F)],
                        sems.at[2 * (k * owners + h)],
                    )
                )
                copies.append(
                    pltpu.make_async_copy(
                        ins[k].at[rows, pl.ds(OUT_F, OUT_B)],
                        out_b.at[tab[base + 10 + n + owner], :, pl.ds(2 * KV_LOC, OUT_B)],
                        sems.at[2 * (k * owners + h) + 1],
                    )
                )
        for c in copies:
            c.start()
        wait_all(copies)

    return pl.pallas_call(
        kernel,
        out_shape=(
            jax.ShapeDtypeStruct(part_f.shape, BF),
            jax.ShapeDtypeStruct(part_b.shape, BF),
        ),
        in_specs=[SMEM] + [VM] * MEMBERS + [ANY, ANY],
        out_specs=(ANY, ANY),
        input_output_aliases={1 + MEMBERS: 0, 2 + MEMBERS: 1},
        scratch_shapes=[pltpu.SemaphoreType.DMA((2 * n,))],
        cost_estimate=cost(0, 3 << 20),
        name="pack_out_grads",
    )(table, *pieces, part_f, part_b)


def place_attention(places, shares):
    rows, width = shares[0].shape

    def kernel(*refs):
        tab = refs[0]
        ins = refs[1 : 1 + MEMBERS]
        gq, gk, gv, go, hold = refs[1 + MEMBERS :]
        for k in range(MEMBERS):
            hold[tab[k]] = ins[k][...].astype(F32)
        at = Q_LOC + OUT_F
        for j in range(MEMBERS):
            gq[:, j * Q_LOC : (j + 1) * Q_LOC] = hold[j, :, :Q_LOC]
            gk[:, j * KV_LOC : (j + 1) * KV_LOC] = hold[j, :, at : at + KV_LOC]
            gv[:, j * KV_LOC : (j + 1) * KV_LOC] = hold[j, :, at + KV_LOC : at + 2 * KV_LOC]
            go[:, j * Q_LOC : j * Q_LOC + OUT_F] = hold[j, :, Q_LOC:at]
            go[:, j * Q_LOC + OUT_F : (j + 1) * Q_LOC] = hold[j, :, at + 2 * KV_LOC :]

    return pl.pallas_call(
        kernel,
        out_shape=tuple(
            jax.ShapeDtypeStruct((rows, MEMBERS * size), F32)
            for size in (Q_LOC, KV_LOC, KV_LOC, Q_LOC)
        ),
        in_specs=[SMEM] + [VM] * MEMBERS,
        out_specs=(VM,) * 4,
        scratch_shapes=[pltpu.VMEM((MEMBERS, rows, width), F32)],
        cost_estimate=cost(0, 6 * MEMBERS * rows * width),
        name="place_attention",
    )(places, *shares)


def expert_kernel(table, base, slot, count, pieces, rows_b, rows_d, router, width, hidden, groups, ringed, offsets):
    many = len(pieces)
    n = many // 2
    half = 3 * hidden // 2
    nt = PAIR_TOK // KEYROWS
    tiles = PAIR_TOK // TILE
    per = TILE // KEYROWS
    step = TILE
    chunk = width // groups
    owners = step // chunk
    cuts = width // step
    wide = width + LANE

    def kernel(*refs):
        tab = refs[0]
        w_refs = refs[1 : 1 + many]
        b_refs = refs[1 + many : 5 + many]
        d_refs = refs[5 + many : 9 + many]
        r_ref = refs[9 + many]
        db, out = refs[10 + many : 12 + many]
        grads = refs[12 + many : 14 + many] if ringed else refs[12 + many : 13 + many]
        scratch = refs[14 + many :] if ringed else refs[13 + many :]
        w_v, b_v, d_v, dgu_v, gh_v, db_v, out_v, sem_w, sem_b, sem_d = scratch[:10]
        i = pl.program_id(0)

        def fetch(e):
            if many == 1:
                cols = pl.ds(e * 3 * hidden, 3 * hidden)
                return [pltpu.make_async_copy(w_refs[0].at[:, cols], w_v.at[e], sem_w.at[e])]
            copies = []
            for at in range(many):
                side = at // n
                rows = w_refs[at].shape[0]
                copies.append(
                    pltpu.make_async_copy(
                        w_refs[at].at[:, pl.ds(offsets[side] + e * half, half)],
                        w_v.at[
                            e,
                            pl.ds(pl.multiple_of(tab[at], 16), rows),
                            pl.ds(side * half, half),
                        ],
                        sem_w.at[e * many + at],
                    )
                )
            return copies

        @pl.when(i == 0)
        def _():
            cb = start_rows(b_refs, b_v, tab, base, sem_b)
            for e in range(count):
                for c in fetch(e):
                    c.start()
            cd = start_rows(d_refs, d_v, tab, base, sem_d)
            wait_all(cb)
            wait_all(cd)

        @pl.when(i < tiles)
        def _():
            at = pl.ds(i * per, per)
            b = b_v[at].reshape(TILE, width)
            mark = d_v[at, :, width:].reshape(TILE, LANE).astype(F32)
            lanes = lax.broadcasted_iota(jnp.int32, (TILE, LANE), 1)
            logits = jnp.where(mark > 0.0, dot(b, r_ref[...]), NEG)
            top = jnp.max(logits, axis=1, keepdims=True)
            weight = jnp.where(mark > 0.0, jnp.exp(logits - top), 0.0)
            gates = weight / jnp.sum(weight, axis=1, keepdims=True)
            rows = pl.ds(pl.multiple_of(i * TILE, TILE), TILE)

            def one(e, extra):
                for c in range(count):

                    @pl.when((i == 0) & (e == c))
                    def _(c=c):
                        wait_all(fetch(c))

                expert = tab[base + 9] + slot + e
                b = b_v[at].reshape(TILE, width)
                dy = d_v[at, :, :width].reshape(TILE, width)
                gate = jnp.sum(jnp.where(lanes == expert, gates, 0.0), axis=1, keepdims=True)
                gu = dot(b, w_v[e, :, : 2 * hidden])
                back = dot(dy, w_v[e, :, 2 * hidden :])
                g = gu[:, :hidden]
                u = gu[:, hidden:]
                sig = 1.0 / (1.0 + jnp.exp(-g))
                act = g * sig
                hb = (act * u).astype(BF)
                hf = hb.astype(F32)
                dgate = jnp.sum(hf * back, axis=1, keepdims=True)
                gh = (hf * gate).astype(BF)
                dh = back * gate
                dg = dh * u * (sig * (1.0 + g * (1.0 - sig)))
                dgu = jnp.concatenate([dg, dh * act], 1).astype(BF)
                dgu_v[e, rows, :] = dgu
                gh_v[e, rows, :] = gh
                y = dot_nt(dgu, w_v[e, :, : 2 * hidden])
                z = dot_nt(gh, w_v[e, :, 2 * hidden :])

                @pl.when(e == 0)
                def _():
                    db_v[...] = y
                    out_v[...] = z

                @pl.when(e > 0)
                def _():
                    db_v[...] += y
                    out_v[...] += z

                high = dgate.astype(BF).astype(F32)
                low = dgate - high
                return extra + jnp.where(
                    lanes == expert, high, jnp.where(lanes == expert + LANE // 2, low, 0.0)
                )

            extra = lax.fori_loop(0, count, one, jnp.zeros((TILE, LANE), F32))
            whole = slice(None)
            store_members(db, tab, base, whole, db_v[...].astype(BF), pl.ds(0, width))
            store_members(db, tab, base, whole, extra.astype(BF), pl.ds(width, LANE))
            store_members(out, tab, base, whole, out_v[...].astype(BF))

        @pl.when(i >= tiles)
        def _():
            cols = pl.ds(pl.multiple_of((i - tiles) * step, step), step)
            b = b_v[:, :, cols].reshape(PAIR_TOK, step)
            dy = d_v[:, :, cols].reshape(PAIR_TOK, step)
            if not ringed:
                grads[0][:, : 2 * hidden] = dot_tn(b, dgu_v[0]).astype(BF)
                grads[0][:, 2 * hidden :] = dot_tn(dy, gh_v[0]).astype(BF)
            else:
                g_v, sem_g = scratch[10:]
                j = i - tiles
                for e in range(count):
                    one = dot_tn(b, dgu_v[e]).astype(BF)
                    g_v[0, j, :, e * half : (e + 1) * half] = one[:, :half]
                    g_v[1, j, :, e * half : e * half + 2 * hidden - half] = one[:, half:]
                    two = dot_tn(dy, gh_v[e]).astype(BF)
                    g_v[1, j, :, e * half + 2 * hidden - half : (e + 1) * half] = two

                def send(j, h, side):
                    owner = j * owners + h
                    return pltpu.make_async_copy(
                        g_v.at[side, j, pl.ds(h * chunk, chunk)],
                        grads[side].at[tab[base + 10 + side * groups + owner]],
                        sem_g.at[side * groups + owner],
                    )

                for h in range(owners):
                    for side in range(2):
                        send(j, h, side).start()

                @pl.when(j == cuts - 1)
                def _():
                    for t in range(cuts):
                        for h in range(owners):
                            for side in range(2):
                                send(t, h, side).wait()

    if ringed:
        grad_specs = (ANY, ANY)
        grad_shapes = (jax.ShapeDtypeStruct((groups, chunk, count * half), BF),) * 2
        more = [
            pltpu.VMEM((2, cuts, step, count * half), BF),
            pltpu.SemaphoreType.DMA((2 * groups,)),
        ]
    else:
        grad_specs = (
            pl.BlockSpec((step, 3 * hidden), lambda i: (jnp.maximum(i - tiles, 0), 0)),
        )
        grad_shapes = (jax.ShapeDtypeStruct((width, 3 * hidden), BF),)
        more = []
    return pl.pallas_call(
        kernel,
        grid=(tiles + cuts,),
        out_shape=(
            jax.ShapeDtypeStruct((MEMBERS, nt, 32, wide), BF),
            jax.ShapeDtypeStruct((MEMBERS, nt, 32, width), BF),
        )
        + grad_shapes,
        in_specs=[SMEM] + [ANY] * (many + 8) + [pl.BlockSpec((width, LANE), lambda i: (0, 0))],
        out_specs=(
            pl.BlockSpec(
                (MEMBERS, per, 32, wide), lambda i: (0, jnp.minimum(i, tiles - 1), 0, 0)
            ),
            pl.BlockSpec(
                (MEMBERS, per, 32, width), lambda i: (0, jnp.minimum(i, tiles - 1), 0, 0)
            ),
        )
        + grad_specs,
        scratch_shapes=[
            pltpu.VMEM((count, width, 3 * hidden), BF),
            pltpu.VMEM((nt, KEYROWS, width), BF),
            pltpu.VMEM((nt, KEYROWS, wide), BF),
            pltpu.VMEM((count, PAIR_TOK, 2 * hidden), BF),
            pltpu.VMEM((count, PAIR_TOK, hidden), BF),
            pltpu.VMEM((TILE, width), F32),
            pltpu.VMEM((TILE, width), F32),
            pltpu.SemaphoreType.DMA((count * many,)),
            pltpu.SemaphoreType.DMA((4,)),
            pltpu.SemaphoreType.DMA((4,)),
        ]
        + more,
        compiler_params=params(58),
        cost_estimate=cost(17 * 10**9 * count, (12 + 14 * count) << 20, 10**6 * count),
        name="expert",
    )(table, *pieces, *rows_b, *rows_d, router)


def turn_out_weight(places, af, ab):
    n = len(af)
    rows = af[0].shape[0]

    def kernel(*refs):
        tab = refs[0]
        f_refs = refs[1 : 1 + n]
        b_refs = refs[1 + n : 1 + 2 * n]
        out, sems = refs[1 + 2 * n :]
        copies = []
        for s in range(n):
            at = pl.ds(pl.multiple_of(tab[n + s], 16), rows)
            copies.append(
                pltpu.make_async_copy(
                    f_refs[s].at[:, pl.ds(Q_LOC, OUT_F)],
                    out.at[tab[s], at, pl.ds(0, OUT_F)],
                    sems.at[s],
                )
            )
            at = pl.ds(pl.multiple_of(tab[3 * n + s], 16), rows)
            copies.append(
                pltpu.make_async_copy(
                    b_refs[s].at[:, pl.ds(2 * KV_LOC, OUT_B)],
                    out.at[tab[2 * n + s], at, pl.ds(OUT_F, OUT_B)],
                    sems.at[n + s],
                )
            )
        for c in copies:
            c.start()
        wait_all(copies)

    return pl.pallas_call(
        kernel,
        out_shape=jax.ShapeDtypeStruct((MEMBERS, Q_LOC, Q_LOC), BF),
        in_specs=[SMEM] + [ANY] * (2 * n),
        out_specs=VM,
        scratch_shapes=[pltpu.SemaphoreType.DMA((2 * n,))],
        cost_estimate=cost(0, 3 << 20),
        name="turn_out_weight",
    )(places, *af, *ab)


def ring_place(index, n):
    return jnp.where(index % 2 == 0, index // 2, n - 1 - index // 2)


def ring_index(place, n):
    return jnp.where(place < n // 2, 2 * place, 2 * (n - 1 - place) + 1)


def ring_pairs(n):
    ring = list(range(0, n, 2)) + list(range(n - 1, 0, -2))
    ahead = [(ring[i], ring[(i + 1) % n]) for i in range(n)]
    back = [(b, a) for a, b in ahead]
    return ahead, back


def after(value, *deps):
    return lax.optimization_barrier((value,) + deps)[0]


def swap(values, bits):
    return lax.ppermute(values, "seq", [(i, i ^ bits) for i in range(MEMBERS)])


def share_rows(values):
    across = swap(values, 2)
    return [values, swap(values, 1), across, swap(across, 1)]


def body(
    tokens,
    cotangent,
    routes,
    lengths,
    deal_order,
    attn_gain,
    query_weight,
    key_matrix,
    value_matrix,
    out_weight,
    moe_gain,
    router_weight,
    expert_weight,
):
    n = lax.axis_size("dp")
    group = lax.axis_index("dp")
    member = lax.axis_index("seq")
    slots, block, width = tokens.shape
    units = PAIR_TOK // (MEMBERS * block)
    local_rows = query_weight.shape[0]
    n_expert = router_weight.shape[1]
    hidden = expert_weight.shape[2] // 3
    per = n_expert // MEMBERS
    ahead, back = ring_pairs(n)
    natural = block == 32

    place = ring_place(group, n)
    steps = jnp.arange(n, dtype=jnp.int32)
    from_f = ring_index((place - steps) % n, n).astype(jnp.int32)
    from_b = ring_index((place + steps) % n, n).astype(jnp.int32)
    xors = jnp.bitwise_xor(jnp.arange(MEMBERS, dtype=jnp.int32), member)
    row_place = xors if natural else jnp.arange(MEMBERS, dtype=jnp.int32)
    first_seq = deal_order[2 * group]
    first_len = lengths[first_seq]
    first = (first_len // (MEMBERS * block)).reshape(1)
    base = 2 * n
    table = jnp.concatenate(
        [
            from_f * local_rows,
            from_b * local_rows,
            row_place,
            xors,
            jnp.stack([first_len, per * member]),
            (place - ring_place(steps, n)) % n,
            (ring_place(steps, n) - place) % n,
        ]
    ).astype(jnp.int32)
    share = n // MEMBERS
    out_places = jnp.concatenate(
        [
            jnp.bitwise_xor(from_f // share, member),
            from_f % share * local_rows,
            jnp.bitwise_xor(from_b // share, member),
            from_b % share * local_rows,
        ]
    ).astype(jnp.int32)

    sent_x = pick_rows(tokens, deal_order)
    dealt_x = lax.all_to_all(sent_x, "dp", split_axis=0, concat_axis=0, tiled=True)
    x_rows = take_rows(dealt_x, first, units)

    def cut(values, size):
        return lax.dynamic_slice_in_dim(values, member * size, size, axis=1).astype(BF)

    small = jnp.concatenate(
        [
            router_weight,
            jnp.zeros((local_rows, GAINS_AT - n_expert), F32),
            attn_gain[:, None],
            moe_gain[:, None],
            jnp.zeros((local_rows, LANE - GAINS_AT - 2), F32),
        ],
        1,
    ).astype(BF)
    out_cols = cut(out_weight, Q_LOC)
    attn_f = jnp.concatenate([cut(query_weight, Q_LOC), out_cols[:, :OUT_F], small], 1)
    attn_b = jnp.concatenate(
        [cut(key_matrix, KV_LOC), cut(value_matrix, KV_LOC), out_cols[:, OUT_F:]], 1
    )
    expert_first = expert_weight.transpose(1, 0, 2)
    expert_own = lax.dynamic_slice_in_dim(expert_first, per * member, per, axis=0).astype(BF)

    def rows_of(chunks):
        if natural:
            return chunks
        w = chunks[0].shape[2]
        whole = jnp.zeros((units, MEMBERS, block, w), BF)
        for k in range(MEMBERS):
            whole = lax.dynamic_update_slice(whole, chunks[k][:, None], (0, xors[k], 0, 0))
        whole = whole.reshape(PAIR_TOK // KEYROWS, MEMBERS, 32, w)
        return [whole[:, j] for j in range(MEMBERS)]

    def scatter_parts(parts):
        if natural:
            shaped = parts
        else:
            shaped = []
            for p in parts:
                rows = p.transpose(1, 0, 2, 3).reshape(units, MEMBERS, block, p.shape[3])
                shaped.append(
                    [
                        lax.dynamic_index_in_dim(rows, xors[k], axis=1, keepdims=False)
                        for k in range(MEMBERS)
                    ]
                )

        def part(k):
            total = None
            for p in shaped:
                one = p[k].astype(F32)
                total = one if total is None else total + one
            return total

        return part

    def scatter_near(part, *deps):
        far = swap(after(part(3).astype(BF), *deps), 1)
        near = swap(after(part(1).astype(BF), *deps), 1)
        hop = (part(2) + far.astype(F32)).astype(BF)
        return near, hop

    def scatter_end(part, near, cross):
        return part(0) + near.astype(F32) + cross.astype(F32)

    class Gather:
        def __init__(self, f, b):
            self.fs, self.bs = [f], [b]

        def step(self, *deps):
            if len(self.fs) < n:
                self.fs.append(lax.ppermute(after(self.fs[-1], *deps), "dp", ahead))
                self.bs.append(lax.ppermute(after(self.bs[-1], *deps), "dp", back))

        def last(self, ago=1):
            return self.fs[-ago], self.bs[-ago]

        def finish(self):
            while len(self.fs) < n:
                self.step()

    class Scatter:
        def __init__(self, part_f, part_b):
            self.parts = part_f, part_b
            self.sums = part_f(1), part_b(1)
            self.at = 1

        def step(self, *deps):
            if self.at < n:
                f = lax.ppermute(after(self.sums[0], *deps), "dp", ahead)
                b = lax.ppermute(after(self.sums[1], *deps), "dp", back)
                self.at += 1
                own = [part(self.at % n) for part in self.parts]
                self.sums = tuple(
                    (got.astype(F32) + mine.astype(F32)).astype(BF)
                    for got, mine in zip((f, b), own)
                )

        def finish(self):
            while self.at < n:
                self.step()
            return self.sums

    row = jnp.arange(PAIR_TOK, dtype=jnp.int32)
    pos = row - jnp.where(row >= first_len, first_len, 0)
    freq = rope_base ** (-(jnp.arange(HEAD // 2, dtype=F32) * 2.0 / HEAD))
    angle = pos.astype(F32)[:, None] * freq[None, :]
    cosine = jnp.concatenate([jnp.cos(angle)] * 4, 1)
    sine = jnp.sin(angle)
    sine = jnp.concatenate([-sine, sine, -sine, sine], 1)

    half = 3 * hidden // 2
    ring = Gather(
        after(jnp.concatenate([attn_f, expert_own[0, :, :half]], 1), sent_x),
        after(jnp.concatenate([attn_b, expert_own[0, :, half:]], 1), sent_x),
    )
    offsets = (attn_f.shape[1], attn_b.shape[1])
    sent_d = pick_marked(after(cotangent, sent_x), routes, deal_order)
    ring.step()
    ring.step(sent_d)
    x_across, x_near = swap(x_rows, 2), swap(x_rows, 1)
    others = per - 1
    second_f = jnp.concatenate([expert_own[e, :, :half] for e in range(1, per)], 1)
    second_b = jnp.concatenate([expert_own[e, :, half:] for e in range(1, per)], 1)
    ring.step(x_rows)
    ring.step(cosine, sine)
    ring.step(x_across, second_f, second_b)
    x_far = swap(x_across, 1)
    ring.finish()
    dealt_d = lax.all_to_all(
        after(sent_d, *ring.last()), "dp", split_axis=0, concat_axis=0, tiled=True
    )
    ring_fs, ring_bs = ring.fs, ring.bs
    second = Gather(after(second_f, *ring.last()), after(second_b, *ring.last()))
    second.step()
    turned = turn_out_weight(out_places, ring_fs, ring_bs)
    wout = [turned[0]] + [swap(turned[k], k) for k in range(1, MEMBERS)]

    rows_x = [after(x_rows, turned), x_near, x_across, x_far]
    a_all, q, k, v, heads, router, gains = attention_forward(
        table, base, ring_fs, ring_bs, rows_of(rows_x), cosine, sine, width
    )
    second.step(heads)
    d_rows = take_rows(dealt_d, first, units)
    part = project_out(table, base, after(heads, d_rows, *second.last(2)), wout, width)
    gain_a = gains[0:1]
    gain_m = gains[1:2]
    mix = scatter_parts([part])
    mix_near, mix_hop = scatter_near(mix)
    mix_cross = swap(mix_hop, 2)
    second.step(mix_hop)
    middle = after(x_rows, *second.last(2)).astype(F32) + scatter_end(mix, mix_near, mix_cross)

    inverse = lax.rsqrt(jnp.mean(middle * middle, axis=-1, keepdims=True) + eps_norm)
    b_rows = (middle * inverse * gain_m).astype(BF)
    b_across, b_near = swap(b_rows, 2), swap(b_rows, 1)
    second.step(b_rows)
    d_own_rows = after(d_rows, b_rows, *second.last(2))
    d_across, d_near = swap(d_own_rows, 2), swap(d_own_rows, 1)
    second.step(b_across)
    second.finish()
    rows_b = rows_of([b_rows, b_near, b_across, swap(b_across, 1)])
    rows_d = rows_of([d_rows, d_near, d_across, swap(d_across, 1)])

    db, out, grad = expert_kernel(
        table,
        base,
        0,
        1,
        ring_fs + ring_bs,
        rows_b,
        rows_d,
        router,
        width,
        hidden,
        n,
        False,
        offsets,
    )
    dbs, outs = [db], [out]
    first_share = lax.psum_scatter(grad, "dp", scatter_dimension=0, tiled=True)
    db, out, grad_f, grad_b = expert_kernel(
        after(table, dbs[0]),
        base,
        1,
        others,
        second.fs + second.bs,
        rows_b,
        rows_d,
        router,
        width,
        hidden,
        n,
        True,
        (0, 0),
    )
    dbs.append(db)
    outs.append(out)
    shed = Scatter(lambda s: grad_f[s], lambda s: grad_b[s])
    shed.step()

    own_b = b_rows.reshape(units * block, width)
    mark = d_rows[:, :, width:].reshape(units * block, LANE).astype(F32)
    logits = dot(own_b, router)
    gates = jax.nn.softmax(jnp.where(mark > 0.0, logits, -jnp.inf), axis=-1)

    back_part = scatter_parts(dbs)
    back_near, back_hop = scatter_near(back_part)
    back_cross = swap(back_hop, 2)
    shed.step(back_hop)
    back_sum = scatter_end(back_part, back_near, back_cross).reshape(units * block, width + LANE)
    extra = back_sum[:, width:]
    dgate = extra + jnp.roll(extra, -(LANE // 2), axis=1)
    dgate = jnp.where(mark > 0.0, dgate, 0.0)
    dlogits = (gates * (dgate - jnp.sum(gates * dgate, axis=-1, keepdims=True))).astype(BF)
    db_own = back_sum[:, :width] + dot_nt(dlogits, router)
    mid_own = middle.reshape(units * block, width)
    inv_own = inverse.reshape(units * block, 1)
    d_own = d_rows[:, :, :width].reshape(units * block, width).astype(F32)
    normed = mid_own * inv_own
    scaled = db_own * gain_m
    dmiddle = d_own + inv_own * (
        scaled - normed * jnp.mean(scaled * normed, axis=-1, keepdims=True)
    )
    dmix = jnp.concatenate([dmiddle.astype(BF), dlogits], 1).reshape(units, block, width + LANE)
    m_across, m_near = swap(dmix, 2), swap(dmix, 1)
    shed.step(dmix)
    out_part = scatter_parts(outs)
    out_near, out_hop = scatter_near(out_part, dmix)
    m_far = swap(m_across, 1)
    out_cross = swap(after(out_hop, m_across), 2)
    shed.step(m_across)
    result = middle + scatter_end(out_part, out_near, out_cross)
    sent_out = spread_rows(result.astype(BF), first, slots)
    back_out = lax.all_to_all(sent_out, "dp", split_axis=0, concat_axis=0, tiled=True)
    rows_m = rows_of([after(dmix, sent_out, first_share, *shed.sums), m_near, m_across, m_far])
    first_shares = share_rows(first_share)

    da, dqkv = attention_backward(
        table, base, ring_fs, ring_bs, rows_m, wout, q, k, v, cosine, sine, width
    )
    shed.step(da)
    da_part = scatter_parts([da])
    da_near, da_hop = scatter_near(da_part, back_out)
    da_cross = swap(da_hop, 2)
    half_f, half_b, gout = attention_grads(
        table, base, a_all, rows_b, rows_m, after(heads, da_hop), dqkv, width, n
    )
    gout = after(gout, da_cross)
    pieces = [gout[0]] + [swap(gout[kk], kk) for kk in range(1, MEMBERS)]
    full_f, full_b = pack_out_grads(table, base, pieces, half_f, half_b)
    da_own = scatter_end(da_part, da_near, da_cross).reshape(units * block, width)
    x_own = x_rows.reshape(units * block, width).astype(F32)
    inv_x = lax.rsqrt(jnp.mean(x_own * x_own, axis=-1, keepdims=True) + eps_norm)
    normed_x = x_own * inv_x
    scaled_x = da_own * gain_a
    grad_x = dmiddle + inv_x * (
        scaled_x - normed_x * jnp.mean(scaled_x * normed_x, axis=-1, keepdims=True)
    )

    sent_grad = spread_rows(grad_x.reshape(units, block, width).astype(BF), first, slots)
    back_grad = lax.all_to_all(sent_grad, "dp", split_axis=0, concat_axis=0, tiled=True)
    output = place_rows(after(back_out, sent_grad), deal_order)
    grad_tokens = place_rows(back_grad, deal_order)

    pair_f, pair_b = shed.finish()
    pair_share = jnp.concatenate([pair_f, pair_b], 1)
    pair_shares = share_rows(pair_share)
    grad_first, gain_first = place_experts(
        xors, first_shares, expert_first, 0, 1, False, per, None
    )
    grad_first, gain_rest = place_experts(
        xors, pair_shares, expert_first, 1, others, True, per, grad_first
    )
    full_f = after(full_f, pair_f, sent_grad)
    full_b = after(full_b, pair_b, sent_grad)
    final = Scatter(lambda s: full_f[s], lambda s: full_b[s])
    final.step()
    final.step(output)
    final.step()
    final.step()
    final.step(gain_rest)
    final.step(grad_tokens)
    share_f, share_b = final.finish()
    small_grad = share_b[:, full_b.shape[2] - LANE :]
    shares = share_rows(jnp.concatenate([share_f, share_b[:, : full_b.shape[2] - LANE]], 1))

    grad_query, grad_key, grad_value, grad_out = place_attention(xors, shares)
    grad_router = small_grad[:, :n_expert].astype(F32)
    grad_experts = grad_first.transpose(1, 0, 2)

    def low(values):
        return values.astype(BF).astype(F32)

    grad_attn_gain = (
        jnp.sum(low(query_weight) * grad_query, axis=1)
        + jnp.sum(low(key_matrix) * grad_key, axis=1)
        + jnp.sum(low(value_matrix) * grad_value, axis=1)
    ) / low(attn_gain)
    grad_moe_gain = (
        jnp.sum(gain_first + gain_rest, axis=1)
        + jnp.sum(low(router_weight) * grad_router, axis=1)
    ) / low(moe_gain)

    return (
        output,
        grad_tokens,
        grad_attn_gain,
        grad_query,
        grad_key,
        grad_value,
        grad_out,
        grad_moe_gain,
        grad_router,
        grad_experts,
    )


def solution(mesh):
    rows = P(None, ("dp", "seq"), None)
    placed = (
        rows,
        rows,
        rows,
        P(),
        P(),
        P("dp"),
        P("dp", None),
        P("dp", None),
        P("dp", None),
        P("dp", None),
        P("dp"),
        P("dp", None),
        P("dp", None, None),
    )
    return jax.shard_map(
        body,
        mesh=mesh,
        in_specs=placed,
        out_specs=(
            rows,
            rows,
            P("dp"),
            P("dp", None),
            P("dp", None),
            P("dp", None),
            P("dp", None),
            P("dp"),
            P("dp", None),
            P("dp", None, None),
        ),
        check_vma=False,
    )
```

```python
import jax
import jax.numpy as jnp
from jax import lax
from jax.experimental import pallas as pl
from jax.experimental.pallas import tpu as pltpu
from jax.sharding import PartitionSpec as P

QUERY_HEADS = 24
KEY_VALUE_HEADS = 8
HEAD = 64
PAIR_TOK = 1152
MEMBERS = 4
LANE = 128
TILE = 384
KEYROWS = 128
UNIT = PAIR_TOK // KEYROWS // 1
eps_norm = 1e-06
rope_base = 10000.0
NEG = -1e30
BF = jnp.bfloat16
F32 = jnp.float32

Q_LOC = QUERY_HEADS // MEMBERS * HEAD
KV_LOC = KEY_VALUE_HEADS // MEMBERS * HEAD
KVH = KEY_VALUE_HEADS // MEMBERS
GROUP = QUERY_HEADS // KEY_VALUE_HEADS
QKV = Q_LOC + 2 * KV_LOC
OUT_F = LANE
OUT_B = Q_LOC - OUT_F
GAINS_AT = 64

ANY = pl.BlockSpec(memory_space=pl.ANY)
SMEM = pl.BlockSpec(memory_space=pltpu.SMEM)
VM = pl.BlockSpec(memory_space=pltpu.VMEM)


def params(megabytes):
    return pltpu.CompilerParams(vmem_limit_bytes=megabytes << 20)


def cost(flops, moved, trans=0):
    return pl.CostEstimate(flops=flops // 100, bytes_accessed=moved // 100, transcendentals=trans // 100)


def dot(a, b):
    return lax.dot_general(a, b, (((1,), (0,)), ((), ())), preferred_element_type=F32)


def dot_nt(a, b):
    return lax.dot_general(a, b, (((1,), (1,)), ((), ())), preferred_element_type=F32)


def dot_tn(a, b):
    return lax.dot_general(a, b, (((0,), (0,)), ((), ())), preferred_element_type=F32)


def pick_rows(values, order):
    count = values.shape[0]

    def kernel(order_ref, in_ref, out_ref, sems):
        copies = [
            pltpu.make_async_copy(in_ref.at[order_ref[i]], out_ref.at[i], sems.at[i])
            for i in range(count)
        ]
        for c in copies:
            c.start()
        wait_all(copies)

    return pl.pallas_call(
        kernel,
        out_shape=jax.ShapeDtypeStruct(values.shape, values.dtype),
        in_specs=[SMEM, ANY],
        out_specs=VM,
        scratch_shapes=[pltpu.SemaphoreType.DMA((count,))],
        cost_estimate=cost(0, 4 * values.size),
        name="pick",
    )(order, values)


def pick_marked(values, routes, order):
    count, block, width = values.shape
    topk = routes.shape[2]

    def kernel(order_ref, in_ref, route_ref, out_ref, sems):
        copies = [
            pltpu.make_async_copy(
                in_ref.at[order_ref[i]], out_ref.at[i, :, pl.ds(0, width)], sems.at[i]
            )
            for i in range(count)
        ]
        for c in copies:
            c.start()
        lanes = lax.broadcasted_iota(jnp.int32, (block, LANE), 1)

        def mark_one(i, carry):
            routed = route_ref[order_ref[i]]
            mark = jnp.zeros((block, LANE), F32)
            for k in range(topk):
                mark = mark + jnp.where(routed[:, k : k + 1] == lanes, 1.0, 0.0)
            out_ref[i, :, width:] = mark.astype(BF)
            return carry

        lax.fori_loop(0, count, mark_one, 0)
        wait_all(copies)

    return pl.pallas_call(
        kernel,
        out_shape=jax.ShapeDtypeStruct((count, block, width + LANE), values.dtype),
        in_specs=[SMEM, ANY, VM],
        out_specs=VM,
        scratch_shapes=[pltpu.SemaphoreType.DMA((count,))],
        cost_estimate=cost(0, 4 * values.size),
        name="pick_marked",
    )(order, values, routes)


def take_rows(dealt, first, units):
    _, block, width = dealt.shape

    def kernel(first_ref, in_ref, out_ref, sems):
        copies = []
        for t in range(units):
            source = jnp.where(t < first_ref[0], 2 * t, 2 * (t - first_ref[0]) + 1)
            copies.append(pltpu.make_async_copy(in_ref.at[source], out_ref.at[t], sems.at[t]))
            copies[-1].start()
        wait_all(copies)

    return pl.pallas_call(
        kernel,
        out_shape=jax.ShapeDtypeStruct((units, block, width), BF),
        in_specs=[SMEM, ANY],
        out_specs=VM,
        scratch_shapes=[pltpu.SemaphoreType.DMA((units,))],
        cost_estimate=cost(0, 4 * units * block * width),
        name="take_rows",
    )(first, dealt)


def spread_rows(rows, first, slots):
    units, block, width = rows.shape

    def kernel(first_ref, in_ref, out_ref):
        for i in range(slots):
            u = i // 2 if i % 2 == 0 else first_ref[0] + i // 2
            limit = first_ref[0] if i % 2 == 0 else units - first_ref[0]
            keep = i // 2 < limit

            @pl.when(keep)
            def _():
                out_ref[i] = in_ref[jnp.minimum(u, units - 1)]

            @pl.when(jnp.logical_not(keep))
            def _():
                out_ref[i] = jnp.zeros((block, width), BF)

    return pl.pallas_call(
        kernel,
        out_shape=jax.ShapeDtypeStruct((slots, block, width), BF),
        in_specs=[SMEM, VM],
        out_specs=VM,
        cost_estimate=cost(0, 4 * slots * block * width),
        name="spread_rows",
    )(first, rows)


def place_rows(values, order):
    count, block, width = values.shape

    def kernel(order_ref, in_ref, out_ref, hold, sems):
        copies = []
        for j in range(count):
            hold[j] = in_ref[j].astype(F32)
            copies.append(
                pltpu.make_async_copy(hold.at[j], out_ref.at[order_ref[j]], sems.at[j])
            )
            copies[-1].start()
        wait_all(copies)

    return pl.pallas_call(
        kernel,
        out_shape=jax.ShapeDtypeStruct(values.shape, F32),
        in_specs=[SMEM, VM],
        out_specs=ANY,
        scratch_shapes=[
            pltpu.VMEM(values.shape, F32),
            pltpu.SemaphoreType.DMA((count,)),
        ],
        cost_estimate=cost(0, 6 * values.size),
        name="place_rows",
    )(order, values)


def place_experts(places, shares, weight, lo, count, split, per, total):
    rows = shares[0].shape[0]
    width = shares[0].shape[1] // count
    half = width // 2
    used = 2 * width // 3

    def kernel(*refs):
        tab = refs[0]
        ins = refs[1 : 1 + MEMBERS]
        weight_ref = refs[1 + MEMBERS]
        out, gain, hold, w_v, sems, sem_w = refs[-6:]
        loads = []
        for k in range(MEMBERS):
            for e in range(count):
                at = k * count + e
                loads.append(
                    pltpu.make_async_copy(
                        weight_ref.at[tab[k] * per + lo + e, :, pl.ds(0, used)],
                        w_v.at[tab[k] * count + e],
                        sem_w.at[at],
                    )
                )
                loads[-1].start()
        copies = []
        for k in range(MEMBERS):
            for e in range(count):
                at = tab[k] * count + e
                for side in range(2):
                    col = (side * count + e) * half if split else e * width + side * half
                    hold[at, :, side * half : (side + 1) * half] = ins[k][
                        :, col : col + half
                    ].astype(F32)
                copies.append(
                    pltpu.make_async_copy(
                        hold.at[at], out.at[tab[k] * per + lo + e], sems.at[k * count + e]
                    )
                )
                copies[-1].start()
        wait_all(loads)
        gain[...] = jnp.zeros_like(gain)

        def add(at, carry):
            total = jnp.zeros((rows, LANE), F32)
            for c in range(used // LANE):
                cols = slice(c * LANE, (c + 1) * LANE)
                total = total + w_v[at, :, cols].astype(BF).astype(F32) * hold[at, :, cols]
            gain[...] += total
            return carry

        lax.fori_loop(0, MEMBERS * count, add, 0)
        wait_all(copies)

    before = [] if total is None else [total]
    return pl.pallas_call(
        kernel,
        out_shape=(
            jax.ShapeDtypeStruct((MEMBERS * per, rows, width), F32),
            jax.ShapeDtypeStruct((rows, LANE), F32),
        ),
        in_specs=[SMEM] + [VM] * MEMBERS + [ANY] * (1 + len(before)),
        out_specs=(ANY, VM),
        input_output_aliases={2 + MEMBERS: 0} if before else {},
        scratch_shapes=[
            pltpu.VMEM((MEMBERS * count, rows, width), F32),
            pltpu.VMEM((MEMBERS * count, rows, used), F32),
            pltpu.SemaphoreType.DMA((MEMBERS * count,)),
            pltpu.SemaphoreType.DMA((MEMBERS * count,)),
        ],
        compiler_params=params(40),
        cost_estimate=cost(0, 6 * MEMBERS * count * rows * width),
        name="place_experts",
    )(places, *shares, weight, *before)


def start_rows(refs, scratch, table, at, sems):
    copies = []
    for k in range(MEMBERS):
        place = pl.multiple_of(table[at + k] * 32, 32)
        copies.append(
            pltpu.make_async_copy(refs[k], scratch.at[:, pl.ds(place, 32), :], sems.at[k])
        )
        copies[-1].start()
    return copies


def start_weights(refs_f, refs_b, wf, wb, scratch, table, sems):
    copies = []
    n = len(refs_f)
    for s in range(n):
        rows = refs_f[s].shape[0]
        row_f = pl.multiple_of(table[s], 16)
        row_b = pl.multiple_of(table[n + s], 16)
        copies.append(
            pltpu.make_async_copy(
                refs_f[s].at[:, pl.ds(0, wf)],
                scratch.at[pl.ds(row_f, rows), pl.ds(0, wf)],
                sems.at[s],
            )
        )
        copies.append(
            pltpu.make_async_copy(
                refs_b[s].at[:, pl.ds(0, wb)],
                scratch.at[pl.ds(row_b, rows), pl.ds(wf, wb)],
                sems.at[n + s],
            )
        )
    for c in copies:
        c.start()
    return copies


def start_out(refs, scratch, table, at, sems):
    copies = []
    for k in range(MEMBERS):
        copies.append(pltpu.make_async_copy(refs[k], scratch.at[table[at + k]], sems.at[k]))
        copies[-1].start()
    return copies


def store_members(out, table, at, tiles, values, cols=None):
    per = values.shape[0] // KEYROWS
    shaped = values.reshape(per, KEYROWS, values.shape[1])
    for j in range(MEMBERS):
        piece = shaped[:, j * 32 : (j + 1) * 32]
        if cols is None:
            out[table[at + j], tiles] = piece
        else:
            out[table[at + j], tiles, :, cols] = piece


def wait_all(copies):
    for c in copies:
        c.wait()


def turn(values, cosine, sine):
    width = values.shape[1]
    lanes = lax.broadcasted_iota(jnp.int32, values.shape, 1)
    low = pltpu.roll(values, width - HEAD // 2, 1)
    high = pltpu.roll(values, HEAD // 2, 1)
    swapped = jnp.where(lanes % HEAD < HEAD // 2, low, high)
    reps = width // LANE
    return values * jnp.concatenate([cosine] * reps, 1) + swapped * jnp.concatenate([sine] * reps, 1)


def bias_for(t, extent, first_len):
    gi = lax.broadcasted_iota(jnp.int32, (KEYROWS, extent), 0) + t * KEYROWS
    gj = lax.broadcasted_iota(jnp.int32, (KEYROWS, extent), 1)
    allowed = (gj <= gi) & ((gi < first_len) | (gj >= first_len))
    return jnp.concatenate([jnp.where(allowed, 0.0, NEG)] * GROUP, 0)


def attention_forward(table, base, af, ab, rows_x, cosine, sine, width):
    n = len(af)
    tiles = PAIR_TOK // TILE
    per = TILE // KEYROWS
    nt = PAIR_TOK // KEYROWS
    chunk = af[0].shape[0]

    def kernel(*refs):
        tab = refs[0]
        f_refs = refs[1 : 1 + n]
        b_refs = refs[1 + n : 1 + 2 * n]
        x_refs = refs[1 + 2 * n : 5 + 2 * n]
        cos_ref, sin_ref = refs[5 + 2 * n : 7 + 2 * n]
        a_out, q_out, k_out, v_out, heads, small, gains = refs[7 + 2 * n : 14 + 2 * n]
        w_v, sem_x, sem_w, sem_s = refs[14 + 2 * n :]
        cs = []
        for s in range(n):
            row = pl.ds(pl.multiple_of(tab[s], 16), chunk)
            cs.append(
                pltpu.make_async_copy(
                    f_refs[s].at[:, pl.ds(Q_LOC + OUT_F, LANE)], small.at[row, :], sem_s.at[s]
                )
            )
            cs[-1].start()
        cw = start_weights(f_refs, b_refs, Q_LOC, 2 * KV_LOC, w_v, tab, sem_w)
        cx = start_rows(x_refs, a_out, tab, base, sem_x)
        wait_all(cs)
        pick = lax.broadcasted_iota(jnp.int32, (8, LANE), 1)
        pick = pick == lax.broadcasted_iota(jnp.int32, (8, LANE), 0) + GAINS_AT
        gains[...] = dot_nt(pick.astype(F32).astype(BF), small[...])
        wait_all(cw)
        wait_all(cx)
        first_len = tab[base + 8]

        def project(i, carry):
            at = pl.ds(i * per, per)
            x = a_out[at].reshape(TILE, width).astype(F32)
            scale = lax.rsqrt(jnp.mean(x * x, axis=-1, keepdims=True) + eps_norm)
            block = (x * scale * gains[0:1, :]).astype(BF)
            a_out[at] = block.reshape(per, KEYROWS, width)
            y = dot(block, w_v[...])
            rows = pl.ds(pl.multiple_of(i * TILE, TILE), TILE)
            turned = turn(y[:, : Q_LOC + KV_LOC], cos_ref[rows, :], sin_ref[rows, :])
            q = (turned[:, :Q_LOC] * 0.125).astype(BF)
            k = turned[:, Q_LOC:].astype(BF)
            v = y[:, Q_LOC + KV_LOC :].astype(BF)
            for j in range(KVH):
                k_out[j, rows, :] = k[:, j * HEAD : (j + 1) * HEAD]
                v_out[j, rows, :] = v[:, j * HEAD : (j + 1) * HEAD]
                for h in range(GROUP):
                    c = (j * GROUP + h) * HEAD
                    for r in range(per):
                        q_out[j, i * per + r, h * KEYROWS : (h + 1) * KEYROWS, :] = q[
                            r * KEYROWS : (r + 1) * KEYROWS, c : c + HEAD
                        ]
            return carry

        lax.fori_loop(0, tiles, project, 0)
        for c in range(tiles):
            extent = (c + 1) * TILE

            def attend(i, carry, c=c, extent=extent):
                t = c * per + i
                bias = bias_for(t, extent, first_len)
                mixed = []
                for j in range(KVH):
                    s = dot_nt(q_out[j, t], k_out[j, :extent, :]) + bias
                    top = jnp.max(s, axis=1, keepdims=True)
                    p = jnp.exp(s - top)
                    total = jnp.sum(p, axis=1, keepdims=True)
                    o = dot(p.astype(BF), v_out[j, :extent, :]) / total
                    mixed += [o[h * KEYROWS : (h + 1) * KEYROWS] for h in range(GROUP)]
                rows = pl.ds(pl.multiple_of(t * KEYROWS, KEYROWS), KEYROWS)
                heads[rows, :] = jnp.concatenate(mixed, 1).astype(BF)
                return carry

            lax.fori_loop(0, per, attend, 0)

    return pl.pallas_call(
        kernel,
        out_shape=(
            jax.ShapeDtypeStruct((nt, KEYROWS, width), BF),
            jax.ShapeDtypeStruct((KVH, nt, GROUP * KEYROWS, HEAD), BF),
            jax.ShapeDtypeStruct((KVH, PAIR_TOK, HEAD), BF),
            jax.ShapeDtypeStruct((KVH, PAIR_TOK, HEAD), BF),
            jax.ShapeDtypeStruct((PAIR_TOK, Q_LOC), BF),
            jax.ShapeDtypeStruct((width, LANE), BF),
            jax.ShapeDtypeStruct((8, width), F32),
        ),
        in_specs=[SMEM] + [ANY] * (2 * n + 4) + [VM, VM],
        out_specs=(VM,) * 7,
        scratch_shapes=[
            pltpu.VMEM((width, QKV), BF),
            pltpu.SemaphoreType.DMA((4,)),
            pltpu.SemaphoreType.DMA((2 * n,)),
            pltpu.SemaphoreType.DMA((n,)),
        ],
        compiler_params=params(48),
        cost_estimate=cost(12 * 10**9, 14 << 20, 5 * 10**6),
        name="attention_forward",
    )(table, *af, *ab, *rows_x, cosine, sine)


def project_out(table, base, heads, wout, width):
    tiles = PAIR_TOK // TILE
    per = TILE // KEYROWS
    nt = PAIR_TOK // KEYROWS

    def kernel(tab, heads, *refs):
        o_refs, (part, o_v, sem_o) = refs[:MEMBERS], refs[MEMBERS:]
        wait_all(start_out(o_refs, o_v, tab, base + 4, sem_o))
        for i in range(tiles):
            h = heads[i * TILE : (i + 1) * TILE, :]
            for j in range(MEMBERS):
                y = dot(h, o_v[j]).astype(BF)
                store_members(
                    part, tab, base, pl.ds(i * per, per), y, pl.ds(j * Q_LOC, Q_LOC)
                )

    return pl.pallas_call(
        kernel,
        out_shape=jax.ShapeDtypeStruct((MEMBERS, nt, 32, width), BF),
        in_specs=[SMEM, VM] + [ANY] * MEMBERS,
        out_specs=VM,
        scratch_shapes=[
            pltpu.VMEM((MEMBERS, Q_LOC, Q_LOC), BF),
            pltpu.SemaphoreType.DMA((4,)),
        ],
        compiler_params=params(24),
        cost_estimate=cost(2 * 10**9, 6 << 20),
        name="project_out",
    )(table, heads, *wout)


def attention_backward(table, base, af, ab, rows_m, wout, q, k, v, cosine, sine, width):
    n = len(af)
    tiles = PAIR_TOK // TILE
    per = TILE // KEYROWS
    nt = PAIR_TOK // KEYROWS
    wide = rows_m[0].shape[2]

    def kernel(*refs):
        tab = refs[0]
        f_refs = refs[1 : 1 + n]
        b_refs = refs[1 + n : 1 + 2 * n]
        m_refs = refs[1 + 2 * n : 5 + 2 * n]
        o_refs = refs[5 + 2 * n : 9 + 2 * n]
        q_ref, k_ref, v_ref, cos_ref, sin_ref = refs[9 + 2 * n : 14 + 2 * n]
        da, dqkv = refs[14 + 2 * n : 16 + 2 * n]
        m_v, w_v, o_v, dh_s, dq_s, dk_s, dv_s, sem_m, sem_w, sem_o = refs[16 + 2 * n :]
        cm = start_rows(m_refs, m_v, tab, base, sem_m)
        co = start_out(o_refs, o_v, tab, base + 4, sem_o)
        cw = start_weights(f_refs, b_refs, Q_LOC, 2 * KV_LOC, w_v, tab, sem_w)
        dk_s[...] = jnp.zeros_like(dk_s)
        dv_s[...] = jnp.zeros_like(dv_s)
        wait_all(co)
        wait_all(cm)
        first_len = tab[base + 8]

        def heads_back(i, carry):
            total = None
            for j in range(MEMBERS):
                block = m_v[pl.ds(i * per, per), :, j * Q_LOC : (j + 1) * Q_LOC]
                y = dot_nt(block.reshape(TILE, Q_LOC), o_v[j])
                total = y if total is None else total + y
            total = total.astype(BF)
            for j in range(KVH):
                for h in range(GROUP):
                    c = (j * GROUP + h) * HEAD
                    for r in range(per):
                        dh_s[j, i * per + r, h * KEYROWS : (h + 1) * KEYROWS, :] = total[
                            r * KEYROWS : (r + 1) * KEYROWS, c : c + HEAD
                        ]
            return carry

        lax.fori_loop(0, tiles, heads_back, 0)
        for c in range(tiles):
            extent = (c + 1) * TILE

            def attend(i, carry, c=c, extent=extent):
                t = c * per + i
                bias = bias_for(t, extent, first_len)
                for j in range(KVH):
                    qb = q_ref[j, t]
                    db = dh_s[j, t]
                    kb = k_ref[j, :extent, :]
                    s = dot_nt(qb, kb) + bias
                    top = jnp.max(s, axis=1, keepdims=True)
                    p = jnp.exp(s - top)
                    p = p * (1.0 / jnp.sum(p, axis=1, keepdims=True))
                    dp = dot_nt(db, v_ref[j, :extent, :])
                    prod = p * dp
                    delta = jnp.sum(prod, axis=1, keepdims=True)
                    ds = (prod - p * delta).astype(BF)
                    dq_s[j, t] = dot(ds, kb) * 0.125
                    dk_s[j, :extent, :] += dot_tn(ds, qb)
                    dv_s[j, :extent, :] += dot_tn(p.astype(BF), db)
                return carry

            lax.fori_loop(0, per, attend, 0)
        wait_all(cw)

        def inputs_back(i, carry):
            rows = pl.ds(pl.multiple_of(i * TILE, TILE), TILE)
            cols = []
            for j in range(KVH):
                for h in range(GROUP):
                    cols.append(
                        jnp.concatenate(
                            [
                                dq_s[j, i * per + r, h * KEYROWS : (h + 1) * KEYROWS, :]
                                for r in range(per)
                            ],
                            0,
                        )
                    )
            cols += [dk_s[j, rows, :] for j in range(KVH)]
            joined = jnp.concatenate(cols, 1).astype(BF).astype(F32)
            turned = turn(joined, cos_ref[rows, :], -sin_ref[rows, :])
            value = jnp.concatenate([dv_s[j, rows, :] for j in range(KVH)], 1)
            out = jnp.concatenate([turned, value], 1).astype(BF)
            dqkv[rows, :] = out
            y = dot_nt(out, w_v[...]).astype(BF)
            store_members(da, tab, base, pl.ds(i * per, per), y)
            return carry

        lax.fori_loop(0, tiles, inputs_back, 0)

    return pl.pallas_call(
        kernel,
        out_shape=(
            jax.ShapeDtypeStruct((MEMBERS, nt, 32, width), BF),
            jax.ShapeDtypeStruct((PAIR_TOK, QKV), BF),
        ),
        in_specs=[SMEM] + [ANY] * (2 * n + 8) + [VM] * 5,
        out_specs=(VM,) * 2,
        scratch_shapes=[
            pltpu.VMEM((nt, KEYROWS, wide), BF),
            pltpu.VMEM((width, QKV), BF),
            pltpu.VMEM((MEMBERS, Q_LOC, Q_LOC), BF),
            pltpu.VMEM((KVH, nt, GROUP * KEYROWS, HEAD), BF),
            pltpu.VMEM((KVH, nt, GROUP * KEYROWS, HEAD), F32),
            pltpu.VMEM((KVH, PAIR_TOK, HEAD), F32),
            pltpu.VMEM((KVH, PAIR_TOK, HEAD), F32),
            pltpu.SemaphoreType.DMA((4,)),
            pltpu.SemaphoreType.DMA((2 * n,)),
            pltpu.SemaphoreType.DMA((4,)),
        ],
        compiler_params=params(56),
        cost_estimate=cost(20 * 10**9, 16 << 20, 5 * 10**6),
        name="attention_backward",
    )(table, *af, *ab, *rows_m, *wout, q, k, v, cosine, sine)


def attention_grads(table, base, a_all, rows_b, rows_m, heads, dqkv, width, n):
    nt = PAIR_TOK // KEYROWS
    step = Q_LOC
    chunk = width // n
    owners = step // chunk
    wide = rows_m[0].shape[2]
    wide_f = Q_LOC + OUT_F
    wide_b = 2 * KV_LOC + OUT_B + LANE

    def kernel(*refs):
        tab = refs[0]
        b_refs, m_refs = refs[1:5], refs[5:9]
        a_ref, heads_ref, d_ref = refs[9:12]
        gf, gb, go = refs[12:15]
        b_v, m_v, sem_b, sem_m = refs[15:]
        j = pl.program_id(0)

        @pl.when(j == 0)
        def _():
            cb = start_rows(b_refs, b_v, tab, base, sem_b)
            cm = start_rows(m_refs, m_v, tab, base, sem_m)
            wait_all(cb)
            wait_all(cm)

        cols = pl.ds(pl.multiple_of(j * step, step), step)
        a = a_ref[...].reshape(PAIR_TOK, step)
        gq = dot_tn(a, d_ref[...]).astype(BF)
        b = b_v[:, :, cols].reshape(PAIR_TOK, step)
        gr = dot_tn(b, m_v[:, :, width:].reshape(PAIR_TOK, LANE)).astype(BF)
        for h in range(owners):
            rows = slice(h * chunk, (h + 1) * chunk)
            to_f = tab[base + 10 + j * owners + h]
            to_b = tab[base + 10 + n + j * owners + h]
            gf[to_f, :, :Q_LOC] = gq[rows, :Q_LOC]
            gb[to_b, :, : 2 * KV_LOC] = gq[rows, Q_LOC:]
            gb[to_b, :, 2 * KV_LOC + OUT_B :] = gr[rows, :]
        m = m_v[:, :, cols].reshape(PAIR_TOK, step)
        go[tab[base + 4 + j]] = dot_tn(heads_ref[...], m).astype(BF)

    return pl.pallas_call(
        kernel,
        grid=(width // step,),
        out_shape=(
            jax.ShapeDtypeStruct((n, chunk, wide_f), BF),
            jax.ShapeDtypeStruct((n, chunk, wide_b), BF),
            jax.ShapeDtypeStruct((MEMBERS, Q_LOC, Q_LOC), BF),
        ),
        in_specs=[SMEM]
        + [ANY] * 8
        + [
            pl.BlockSpec((nt, KEYROWS, step), lambda j: (0, 0, j)),
            pl.BlockSpec((PAIR_TOK, Q_LOC), lambda j: (0, 0)),
            pl.BlockSpec((PAIR_TOK, QKV), lambda j: (0, 0)),
        ],
        out_specs=(
            pl.BlockSpec((n, chunk, wide_f), lambda j: (0, 0, 0)),
            pl.BlockSpec((n, chunk, wide_b), lambda j: (0, 0, 0)),
            pl.BlockSpec((MEMBERS, Q_LOC, Q_LOC), lambda j: (0, 0, 0)),
        ),
        scratch_shapes=[
            pltpu.VMEM((nt, KEYROWS, width), BF),
            pltpu.VMEM((nt, KEYROWS, wide), BF),
            pltpu.SemaphoreType.DMA((4,)),
            pltpu.SemaphoreType.DMA((4,)),
        ],
        compiler_params=params(48),
        cost_estimate=cost(4 * 10**9, 16 << 20),
        name="attention_grads",
    )(table, *rows_b, *rows_m, a_all, heads, dqkv)


def pack_out_grads(table, base, pieces, part_f, part_b):
    n, chunk, wide_f = part_f.shape
    wide_b = part_b.shape[2]
    owners = n // MEMBERS

    def kernel(*refs):
        tab = refs[0]
        ins = refs[1 : 1 + MEMBERS]
        out_f, out_b, sems = refs[3 + MEMBERS :]
        copies = []
        for k in range(MEMBERS):
            for h in range(owners):
                owner = tab[base + 4 + k] * owners + h
                rows = pl.ds(h * chunk, chunk)
                copies.append(
                    pltpu.make_async_copy(
                        ins[k].at[rows, pl.ds(0, OUT_F)],
                        out_f.at[tab[base + 10 + owner], :, pl.ds(Q_LOC, OUT_F)],
                        sems.at[2 * (k * owners + h)],
                    )
                )
                copies.append(
                    pltpu.make_async_copy(
                        ins[k].at[rows, pl.ds(OUT_F, OUT_B)],
                        out_b.at[tab[base + 10 + n + owner], :, pl.ds(2 * KV_LOC, OUT_B)],
                        sems.at[2 * (k * owners + h) + 1],
                    )
                )
        for c in copies:
            c.start()
        wait_all(copies)

    return pl.pallas_call(
        kernel,
        out_shape=(
            jax.ShapeDtypeStruct(part_f.shape, BF),
            jax.ShapeDtypeStruct(part_b.shape, BF),
        ),
        in_specs=[SMEM] + [VM] * MEMBERS + [ANY, ANY],
        out_specs=(ANY, ANY),
        input_output_aliases={1 + MEMBERS: 0, 2 + MEMBERS: 1},
        scratch_shapes=[pltpu.SemaphoreType.DMA((2 * n,))],
        cost_estimate=cost(0, 3 << 20),
        name="pack_out_grads",
    )(table, *pieces, part_f, part_b)


def place_attention(places, shares):
    rows, width = shares[0].shape

    def kernel(*refs):
        tab = refs[0]
        ins = refs[1 : 1 + MEMBERS]
        gq, gk, gv, go, hold = refs[1 + MEMBERS :]
        for k in range(MEMBERS):
            hold[tab[k]] = ins[k][...].astype(F32)
        at = Q_LOC + OUT_F
        for j in range(MEMBERS):
            gq[:, j * Q_LOC : (j + 1) * Q_LOC] = hold[j, :, :Q_LOC]
            gk[:, j * KV_LOC : (j + 1) * KV_LOC] = hold[j, :, at : at + KV_LOC]
            gv[:, j * KV_LOC : (j + 1) * KV_LOC] = hold[j, :, at + KV_LOC : at + 2 * KV_LOC]
            go[:, j * Q_LOC : j * Q_LOC + OUT_F] = hold[j, :, Q_LOC:at]
            go[:, j * Q_LOC + OUT_F : (j + 1) * Q_LOC] = hold[j, :, at + 2 * KV_LOC :]

    return pl.pallas_call(
        kernel,
        out_shape=tuple(
            jax.ShapeDtypeStruct((rows, MEMBERS * size), F32)
            for size in (Q_LOC, KV_LOC, KV_LOC, Q_LOC)
        ),
        in_specs=[SMEM] + [VM] * MEMBERS,
        out_specs=(VM,) * 4,
        scratch_shapes=[pltpu.VMEM((MEMBERS, rows, width), F32)],
        cost_estimate=cost(0, 6 * MEMBERS * rows * width),
        name="place_attention",
    )(places, *shares)


def expert_kernel(table, base, slot, count, pieces, rows_b, rows_d, router, width, hidden, groups, ringed, offsets):
    many = len(pieces)
    n = many // 2
    half = 3 * hidden // 2
    nt = PAIR_TOK // KEYROWS
    tiles = PAIR_TOK // TILE
    per = TILE // KEYROWS
    step = TILE
    chunk = width // groups
    owners = step // chunk
    cuts = width // step
    wide = width + LANE

    def kernel(*refs):
        tab = refs[0]
        w_refs = refs[1 : 1 + many]
        b_refs = refs[1 + many : 5 + many]
        d_refs = refs[5 + many : 9 + many]
        r_ref = refs[9 + many]
        db, out = refs[10 + many : 12 + many]
        grads = refs[12 + many : 14 + many] if ringed else refs[12 + many : 13 + many]
        scratch = refs[14 + many :] if ringed else refs[13 + many :]
        w_v, b_v, d_v, dgu_v, gh_v, db_v, out_v, sem_w, sem_b, sem_d = scratch[:10]
        i = pl.program_id(0)

        def fetch(e):
            if many == 1:
                cols = pl.ds(e * 3 * hidden, 3 * hidden)
                return [pltpu.make_async_copy(w_refs[0].at[:, cols], w_v.at[e], sem_w.at[e])]
            copies = []
            for at in range(many):
                side = at // n
                rows = w_refs[at].shape[0]
                copies.append(
                    pltpu.make_async_copy(
                        w_refs[at].at[:, pl.ds(offsets[side] + e * half, half)],
                        w_v.at[
                            e,
                            pl.ds(pl.multiple_of(tab[at], 16), rows),
                            pl.ds(side * half, half),
                        ],
                        sem_w.at[e * many + at],
                    )
                )
            return copies

        @pl.when(i == 0)
        def _():
            cb = start_rows(b_refs, b_v, tab, base, sem_b)
            for e in range(count):
                for c in fetch(e):
                    c.start()
            cd = start_rows(d_refs, d_v, tab, base, sem_d)
            wait_all(cb)
            wait_all(cd)

        @pl.when(i < tiles)
        def _():
            at = pl.ds(i * per, per)
            b = b_v[at].reshape(TILE, width)
            mark = d_v[at, :, width:].reshape(TILE, LANE).astype(F32)
            lanes = lax.broadcasted_iota(jnp.int32, (TILE, LANE), 1)
            logits = jnp.where(mark > 0.0, dot(b, r_ref[...]), NEG)
            top = jnp.max(logits, axis=1, keepdims=True)
            weight = jnp.where(mark > 0.0, jnp.exp(logits - top), 0.0)
            gates = weight / jnp.sum(weight, axis=1, keepdims=True)
            rows = pl.ds(pl.multiple_of(i * TILE, TILE), TILE)

            def one(e, extra):
                for c in range(count):

                    @pl.when((i == 0) & (e == c))
                    def _(c=c):
                        wait_all(fetch(c))

                expert = tab[base + 9] + slot + e
                b = b_v[at].reshape(TILE, width)
                dy = d_v[at, :, :width].reshape(TILE, width)
                gate = jnp.sum(jnp.where(lanes == expert, gates, 0.0), axis=1, keepdims=True)
                gu = dot(b, w_v[e, :, : 2 * hidden])
                back = dot(dy, w_v[e, :, 2 * hidden :])
                g = gu[:, :hidden]
                u = gu[:, hidden:]
                sig = 1.0 / (1.0 + jnp.exp(-g))
                act = g * sig
                hb = (act * u).astype(BF)
                hf = hb.astype(F32)
                dgate = jnp.sum(hf * back, axis=1, keepdims=True)
                gh = (hf * gate).astype(BF)
                dh = back * gate
                dg = dh * u * (sig * (1.0 + g * (1.0 - sig)))
                dgu = jnp.concatenate([dg, dh * act], 1).astype(BF)
                dgu_v[e, rows, :] = dgu
                gh_v[e, rows, :] = gh
                y = dot_nt(dgu, w_v[e, :, : 2 * hidden])
                z = dot_nt(gh, w_v[e, :, 2 * hidden :])

                @pl.when(e == 0)
                def _():
                    db_v[...] = y
                    out_v[...] = z

                @pl.when(e > 0)
                def _():
                    db_v[...] += y
                    out_v[...] += z

                high = dgate.astype(BF).astype(F32)
                low = dgate - high
                return extra + jnp.where(
                    lanes == expert, high, jnp.where(lanes == expert + LANE // 2, low, 0.0)
                )

            extra = lax.fori_loop(0, count, one, jnp.zeros((TILE, LANE), F32))
            whole = slice(None)
            store_members(db, tab, base, whole, db_v[...].astype(BF), pl.ds(0, width))
            store_members(db, tab, base, whole, extra.astype(BF), pl.ds(width, LANE))
            store_members(out, tab, base, whole, out_v[...].astype(BF))

        @pl.when(i >= tiles)
        def _():
            cols = pl.ds(pl.multiple_of((i - tiles) * step, step), step)
            b = b_v[:, :, cols].reshape(PAIR_TOK, step)
            dy = d_v[:, :, cols].reshape(PAIR_TOK, step)
            if not ringed:
                grads[0][:, : 2 * hidden] = dot_tn(b, dgu_v[0]).astype(BF)
                grads[0][:, 2 * hidden :] = dot_tn(dy, gh_v[0]).astype(BF)
            else:
                g_v, sem_g = scratch[10:]
                j = i - tiles
                for e in range(count):
                    one = dot_tn(b, dgu_v[e]).astype(BF)
                    g_v[0, j, :, e * half : (e + 1) * half] = one[:, :half]
                    g_v[1, j, :, e * half : e * half + 2 * hidden - half] = one[:, half:]
                    two = dot_tn(dy, gh_v[e]).astype(BF)
                    g_v[1, j, :, e * half + 2 * hidden - half : (e + 1) * half] = two

                def send(j, h, side):
                    owner = j * owners + h
                    return pltpu.make_async_copy(
                        g_v.at[side, j, pl.ds(h * chunk, chunk)],
                        grads[side].at[tab[base + 10 + side * groups + owner]],
                        sem_g.at[side * groups + owner],
                    )

                for h in range(owners):
                    for side in range(2):
                        send(j, h, side).start()

                @pl.when(j == cuts - 1)
                def _():
                    for t in range(cuts):
                        for h in range(owners):
                            for side in range(2):
                                send(t, h, side).wait()

    if ringed:
        grad_specs = (ANY, ANY)
        grad_shapes = (jax.ShapeDtypeStruct((groups, chunk, count * half), BF),) * 2
        more = [
            pltpu.VMEM((2, cuts, step, count * half), BF),
            pltpu.SemaphoreType.DMA((2 * groups,)),
        ]
    else:
        grad_specs = (
            pl.BlockSpec((step, 3 * hidden), lambda i: (jnp.maximum(i - tiles, 0), 0)),
        )
        grad_shapes = (jax.ShapeDtypeStruct((width, 3 * hidden), BF),)
        more = []
    return pl.pallas_call(
        kernel,
        grid=(tiles + cuts,),
        out_shape=(
            jax.ShapeDtypeStruct((MEMBERS, nt, 32, wide), BF),
            jax.ShapeDtypeStruct((MEMBERS, nt, 32, width), BF),
        )
        + grad_shapes,
        in_specs=[SMEM] + [ANY] * (many + 8) + [pl.BlockSpec((width, LANE), lambda i: (0, 0))],
        out_specs=(
            pl.BlockSpec(
                (MEMBERS, per, 32, wide), lambda i: (0, jnp.minimum(i, tiles - 1), 0, 0)
            ),
            pl.BlockSpec(
                (MEMBERS, per, 32, width), lambda i: (0, jnp.minimum(i, tiles - 1), 0, 0)
            ),
        )
        + grad_specs,
        scratch_shapes=[
            pltpu.VMEM((count, width, 3 * hidden), BF),
            pltpu.VMEM((nt, KEYROWS, width), BF),
            pltpu.VMEM((nt, KEYROWS, wide), BF),
            pltpu.VMEM((count, PAIR_TOK, 2 * hidden), BF),
            pltpu.VMEM((count, PAIR_TOK, hidden), BF),
            pltpu.VMEM((TILE, width), F32),
            pltpu.VMEM((TILE, width), F32),
            pltpu.SemaphoreType.DMA((count * many,)),
            pltpu.SemaphoreType.DMA((4,)),
            pltpu.SemaphoreType.DMA((4,)),
        ]
        + more,
        compiler_params=params(58),
        cost_estimate=cost(17 * 10**9 * count, (12 + 14 * count) << 20, 10**6 * count),
        name="expert",
    )(table, *pieces, *rows_b, *rows_d, router)


def turn_out_weight(places, af, ab):
    n = len(af)
    rows = af[0].shape[0]

    def kernel(*refs):
        tab = refs[0]
        f_refs = refs[1 : 1 + n]
        b_refs = refs[1 + n : 1 + 2 * n]
        out, sems = refs[1 + 2 * n :]
        copies = []
        for s in range(n):
            at = pl.ds(pl.multiple_of(tab[n + s], 16), rows)
            copies.append(
                pltpu.make_async_copy(
                    f_refs[s].at[:, pl.ds(Q_LOC, OUT_F)],
                    out.at[tab[s], at, pl.ds(0, OUT_F)],
                    sems.at[s],
                )
            )
            at = pl.ds(pl.multiple_of(tab[3 * n + s], 16), rows)
            copies.append(
                pltpu.make_async_copy(
                    b_refs[s].at[:, pl.ds(2 * KV_LOC, OUT_B)],
                    out.at[tab[2 * n + s], at, pl.ds(OUT_F, OUT_B)],
                    sems.at[n + s],
                )
            )
        for c in copies:
            c.start()
        wait_all(copies)

    return pl.pallas_call(
        kernel,
        out_shape=jax.ShapeDtypeStruct((MEMBERS, Q_LOC, Q_LOC), BF),
        in_specs=[SMEM] + [ANY] * (2 * n),
        out_specs=VM,
        scratch_shapes=[pltpu.SemaphoreType.DMA((2 * n,))],
        cost_estimate=cost(0, 3 << 20),
        name="turn_out_weight",
    )(places, *af, *ab)


def ring_place(index, n):
    return jnp.where(index % 2 == 0, index // 2, n - 1 - index // 2)


def ring_index(place, n):
    return jnp.where(place < n // 2, 2 * place, 2 * (n - 1 - place) + 1)


def ring_pairs(n):
    ring = list(range(0, n, 2)) + list(range(n - 1, 0, -2))
    ahead = [(ring[i], ring[(i + 1) % n]) for i in range(n)]
    back = [(b, a) for a, b in ahead]
    return ahead, back


def after(value, *deps):
    return lax.optimization_barrier((value,) + deps)[0]


def swap(values, bits):
    return lax.ppermute(values, "seq", [(i, i ^ bits) for i in range(MEMBERS)])


def share_rows(values):
    across = swap(values, 2)
    return [values, swap(values, 1), across, swap(across, 1)]


def body(
    tokens,
    cotangent,
    routes,
    lengths,
    deal_order,
    attn_gain,
    query_weight,
    key_matrix,
    value_matrix,
    out_weight,
    moe_gain,
    router_weight,
    expert_weight,
):
    n = lax.axis_size("dp")
    group = lax.axis_index("dp")
    member = lax.axis_index("seq")
    slots, block, width = tokens.shape
    units = PAIR_TOK // (MEMBERS * block)
    local_rows = query_weight.shape[0]
    n_expert = router_weight.shape[1]
    hidden = expert_weight.shape[2] // 3
    per = n_expert // MEMBERS
    ahead, back = ring_pairs(n)
    natural = block == 32

    place = ring_place(group, n)
    steps = jnp.arange(n, dtype=jnp.int32)
    from_f = ring_index((place - steps) % n, n).astype(jnp.int32)
    from_b = ring_index((place + steps) % n, n).astype(jnp.int32)
    xors = jnp.bitwise_xor(jnp.arange(MEMBERS, dtype=jnp.int32), member)
    row_place = xors if natural else jnp.arange(MEMBERS, dtype=jnp.int32)
    first_seq = deal_order[2 * group]
    first_len = lengths[first_seq]
    first = (first_len // (MEMBERS * block)).reshape(1)
    base = 2 * n
    table = jnp.concatenate(
        [
            from_f * local_rows,
            from_b * local_rows,
            row_place,
            xors,
            jnp.stack([first_len, per * member]),
            (place - ring_place(steps, n)) % n,
            (ring_place(steps, n) - place) % n,
        ]
    ).astype(jnp.int32)
    share = n // MEMBERS
    out_places = jnp.concatenate(
        [
            jnp.bitwise_xor(from_f // share, member),
            from_f % share * local_rows,
            jnp.bitwise_xor(from_b // share, member),
            from_b % share * local_rows,
        ]
    ).astype(jnp.int32)

    sent_x = pick_rows(tokens, deal_order)
    dealt_x = lax.all_to_all(sent_x, "dp", split_axis=0, concat_axis=0, tiled=True)
    x_rows = take_rows(dealt_x, first, units)

    def cut(values, size):
        return lax.dynamic_slice_in_dim(values, member * size, size, axis=1).astype(BF)

    small = jnp.concatenate(
        [
            router_weight,
            jnp.zeros((local_rows, GAINS_AT - n_expert), F32),
            attn_gain[:, None],
            moe_gain[:, None],
            jnp.zeros((local_rows, LANE - GAINS_AT - 2), F32),
        ],
        1,
    ).astype(BF)
    out_cols = cut(out_weight, Q_LOC)
    attn_f = jnp.concatenate([cut(query_weight, Q_LOC), out_cols[:, :OUT_F], small], 1)
    attn_b = jnp.concatenate(
        [cut(key_matrix, KV_LOC), cut(value_matrix, KV_LOC), out_cols[:, OUT_F:]], 1
    )
    expert_first = expert_weight.transpose(1, 0, 2)
    expert_own = lax.dynamic_slice_in_dim(expert_first, per * member, per, axis=0).astype(BF)

    def rows_of(chunks):
        if natural:
            return chunks
        w = chunks[0].shape[2]
        whole = jnp.zeros((units, MEMBERS, block, w), BF)
        for k in range(MEMBERS):
            whole = lax.dynamic_update_slice(whole, chunks[k][:, None], (0, xors[k], 0, 0))
        whole = whole.reshape(PAIR_TOK // KEYROWS, MEMBERS, 32, w)
        return [whole[:, j] for j in range(MEMBERS)]

    def scatter_parts(parts):
        if natural:
            shaped = parts
        else:
            shaped = []
            for p in parts:
                rows = p.transpose(1, 0, 2, 3).reshape(units, MEMBERS, block, p.shape[3])
                shaped.append(
                    [
                        lax.dynamic_index_in_dim(rows, xors[k], axis=1, keepdims=False)
                        for k in range(MEMBERS)
                    ]
                )

        def part(k):
            total = None
            for p in shaped:
                one = p[k].astype(F32)
                total = one if total is None else total + one
            return total

        return part

    def scatter_near(part, *deps):
        far = swap(after(part(3).astype(BF), *deps), 1)
        near = swap(after(part(1).astype(BF), *deps), 1)
        hop = (part(2) + far.astype(F32)).astype(BF)
        return near, hop

    def scatter_end(part, near, cross):
        return part(0) + near.astype(F32) + cross.astype(F32)

    class Gather:
        def __init__(self, f, b):
            self.fs, self.bs = [f], [b]

        def step(self, *deps):
            if len(self.fs) < n:
                self.fs.append(lax.ppermute(after(self.fs[-1], *deps), "dp", ahead))
                self.bs.append(lax.ppermute(after(self.bs[-1], *deps), "dp", back))

        def last(self, ago=1):
            return self.fs[-ago], self.bs[-ago]

        def finish(self):
            while len(self.fs) < n:
                self.step()

    class Scatter:
        def __init__(self, part_f, part_b):
            self.parts = part_f, part_b
            self.sums = part_f(1), part_b(1)
            self.at = 1

        def step(self, *deps):
            if self.at < n:
                f = lax.ppermute(after(self.sums[0], *deps), "dp", ahead)
                b = lax.ppermute(after(self.sums[1], *deps), "dp", back)
                self.at += 1
                own = [part(self.at % n) for part in self.parts]
                self.sums = tuple(
                    (got.astype(F32) + mine.astype(F32)).astype(BF)
                    for got, mine in zip((f, b), own)
                )

        def finish(self):
            while self.at < n:
                self.step()
            return self.sums

    row = jnp.arange(PAIR_TOK, dtype=jnp.int32)
    pos = row - jnp.where(row >= first_len, first_len, 0)
    freq = rope_base ** (-(jnp.arange(HEAD // 2, dtype=F32) * 2.0 / HEAD))
    angle = pos.astype(F32)[:, None] * freq[None, :]
    cosine = jnp.concatenate([jnp.cos(angle)] * 4, 1)
    sine = jnp.sin(angle)
    sine = jnp.concatenate([-sine, sine, -sine, sine], 1)

    half = 3 * hidden // 2
    ring = Gather(
        after(jnp.concatenate([attn_f, expert_own[0, :, :half]], 1), sent_x),
        after(jnp.concatenate([attn_b, expert_own[0, :, half:]], 1), sent_x),
    )
    offsets = (attn_f.shape[1], attn_b.shape[1])
    sent_d = pick_marked(after(cotangent, sent_x), routes, deal_order)
    ring.step()
    ring.step(sent_d)
    x_across, x_near = swap(x_rows, 2), swap(x_rows, 1)
    others = per - 1
    second_f = jnp.concatenate([expert_own[e, :, :half] for e in range(1, per)], 1)
    second_b = jnp.concatenate([expert_own[e, :, half:] for e in range(1, per)], 1)
    ring.step(x_rows)
    ring.step(cosine, sine)
    ring.step(x_across, second_f, second_b)
    x_far = swap(x_across, 1)
    ring.finish()
    dealt_d = lax.all_to_all(
        after(sent_d, *ring.last()), "dp", split_axis=0, concat_axis=0, tiled=True
    )
    ring_fs, ring_bs = ring.fs, ring.bs
    second = Gather(after(second_f, *ring.last()), after(second_b, *ring.last()))
    second.step()
    turned = turn_out_weight(out_places, ring_fs, ring_bs)
    wout = [turned[0]] + [swap(turned[k], k) for k in range(1, MEMBERS)]

    rows_x = [after(x_rows, turned), x_near, x_across, x_far]
    a_all, q, k, v, heads, router, gains = attention_forward(
        table, base, ring_fs, ring_bs, rows_of(rows_x), cosine, sine, width
    )
    second.step(heads)
    d_rows = take_rows(dealt_d, first, units)
    part = project_out(table, base, after(heads, d_rows, *second.last(2)), wout, width)
    gain_a = gains[0:1]
    gain_m = gains[1:2]
    mix = scatter_parts([part])
    mix_near, mix_hop = scatter_near(mix)
    mix_cross = swap(mix_hop, 2)
    second.step(mix_hop)
    middle = after(x_rows, *second.last(2)).astype(F32) + scatter_end(mix, mix_near, mix_cross)

    inverse = lax.rsqrt(jnp.mean(middle * middle, axis=-1, keepdims=True) + eps_norm)
    b_rows = (middle * inverse * gain_m).astype(BF)
    b_across, b_near = swap(b_rows, 2), swap(b_rows, 1)
    second.step(b_rows)
    d_own_rows = after(d_rows, b_rows, *second.last(2))
    d_across, d_near = swap(d_own_rows, 2), swap(d_own_rows, 1)
    second.step(b_across)
    second.finish()
    rows_b = rows_of([b_rows, b_near, b_across, swap(b_across, 1)])
    rows_d = rows_of([d_rows, d_near, d_across, swap(d_across, 1)])

    db, out, grad = expert_kernel(
        table,
        base,
        0,
        1,
        ring_fs + ring_bs,
        rows_b,
        rows_d,
        router,
        width,
        hidden,
        n,
        False,
        offsets,
    )
    dbs, outs = [db], [out]
    first_share = lax.psum_scatter(grad, "dp", scatter_dimension=0, tiled=True)
    db, out, grad_f, grad_b = expert_kernel(
        after(table, dbs[0]),
        base,
        1,
        others,
        second.fs + second.bs,
        rows_b,
        rows_d,
        router,
        width,
        hidden,
        n,
        True,
        (0, 0),
    )
    dbs.append(db)
    outs.append(out)
    shed = Scatter(lambda s: grad_f[s], lambda s: grad_b[s])
    shed.step()

    own_b = b_rows.reshape(units * block, width)
    mark = d_rows[:, :, width:].reshape(units * block, LANE).astype(F32)
    logits = dot(own_b, router)
    gates = jax.nn.softmax(jnp.where(mark > 0.0, logits, -jnp.inf), axis=-1)

    back_part = scatter_parts(dbs)
    back_near, back_hop = scatter_near(back_part)
    back_cross = swap(back_hop, 2)
    shed.step(back_hop)
    back_sum = scatter_end(back_part, back_near, back_cross).reshape(units * block, width + LANE)
    extra = back_sum[:, width:]
    dgate = extra + jnp.roll(extra, -(LANE // 2), axis=1)
    dgate = jnp.where(mark > 0.0, dgate, 0.0)
    dlogits = (gates * (dgate - jnp.sum(gates * dgate, axis=-1, keepdims=True))).astype(BF)
    db_own = back_sum[:, :width] + dot_nt(dlogits, router)
    mid_own = middle.reshape(units * block, width)
    inv_own = inverse.reshape(units * block, 1)
    d_own = d_rows[:, :, :width].reshape(units * block, width).astype(F32)
    normed = mid_own * inv_own
    scaled = db_own * gain_m
    dmiddle = d_own + inv_own * (
        scaled - normed * jnp.mean(scaled * normed, axis=-1, keepdims=True)
    )
    dmix = jnp.concatenate([dmiddle.astype(BF), dlogits], 1).reshape(units, block, width + LANE)
    m_across, m_near = swap(dmix, 2), swap(dmix, 1)
    shed.step(dmix)
    out_part = scatter_parts(outs)
    out_near, out_hop = scatter_near(out_part, dmix)
    m_far = swap(m_across, 1)
    out_cross = swap(after(out_hop, m_across), 2)
    shed.step(m_across)
    result = middle + scatter_end(out_part, out_near, out_cross)
    sent_out = spread_rows(result.astype(BF), first, slots)
    back_out = lax.all_to_all(sent_out, "dp", split_axis=0, concat_axis=0, tiled=True)
    rows_m = rows_of([after(dmix, sent_out, first_share, *shed.sums), m_near, m_across, m_far])
    first_shares = share_rows(first_share)

    da, dqkv = attention_backward(
        table, base, ring_fs, ring_bs, rows_m, wout, q, k, v, cosine, sine, width
    )
    shed.step(da)
    half_f, half_b, gout = attention_grads(
        table, base, a_all, rows_b, rows_m, heads, dqkv, width, n
    )
    da_part = scatter_parts([da])
    da_near, da_hop = scatter_near(da_part, back_out, gout)
    da_cross = swap(da_hop, 2)
    gout = after(gout, da_cross)
    pieces = [gout[0]] + [swap(gout[kk], kk) for kk in range(1, MEMBERS)]
    full_f, full_b = pack_out_grads(table, base, pieces, half_f, half_b)
    da_own = scatter_end(da_part, da_near, da_cross).reshape(units * block, width)
    x_own = x_rows.reshape(units * block, width).astype(F32)
    inv_x = lax.rsqrt(jnp.mean(x_own * x_own, axis=-1, keepdims=True) + eps_norm)
    normed_x = x_own * inv_x
    scaled_x = da_own * gain_a
    grad_x = dmiddle + inv_x * (
        scaled_x - normed_x * jnp.mean(scaled_x * normed_x, axis=-1, keepdims=True)
    )

    sent_grad = spread_rows(grad_x.reshape(units, block, width).astype(BF), first, slots)
    back_grad = lax.all_to_all(sent_grad, "dp", split_axis=0, concat_axis=0, tiled=True)
    output = place_rows(after(back_out, sent_grad), deal_order)
    grad_tokens = place_rows(back_grad, deal_order)

    pair_f, pair_b = shed.finish()
    pair_share = jnp.concatenate([pair_f, pair_b], 1)
    pair_shares = share_rows(pair_share)
    grad_first, gain_first = place_experts(
        xors, first_shares, expert_first, 0, 1, False, per, None
    )
    grad_first, gain_rest = place_experts(
        xors, pair_shares, expert_first, 1, others, True, per, grad_first
    )
    full_f = after(full_f, pair_f, sent_grad)
    full_b = after(full_b, pair_b, sent_grad)
    final = Scatter(lambda s: full_f[s], lambda s: full_b[s])
    final.step()
    final.step(output)
    final.step()
    final.step()
    final.step(gain_rest)
    final.step(grad_tokens)
    share_f, share_b = final.finish()
    small_grad = share_b[:, full_b.shape[2] - LANE :]
    shares = share_rows(jnp.concatenate([share_f, share_b[:, : full_b.shape[2] - LANE]], 1))

    grad_query, grad_key, grad_value, grad_out = place_attention(xors, shares)
    grad_router = small_grad[:, :n_expert].astype(F32)
    grad_experts = grad_first.transpose(1, 0, 2)

    def low(values):
        return values.astype(BF).astype(F32)

    grad_attn_gain = (
        jnp.sum(low(query_weight) * grad_query, axis=1)
        + jnp.sum(low(key_matrix) * grad_key, axis=1)
        + jnp.sum(low(value_matrix) * grad_value, axis=1)
    ) / low(attn_gain)
    grad_moe_gain = (
        jnp.sum(gain_first + gain_rest, axis=1)
        + jnp.sum(low(router_weight) * grad_router, axis=1)
    ) / low(moe_gain)

    return (
        output,
        grad_tokens,
        grad_attn_gain,
        grad_query,
        grad_key,
        grad_value,
        grad_out,
        grad_moe_gain,
        grad_router,
        grad_experts,
    )


def solution(mesh):
    rows = P(None, ("dp", "seq"), None)
    placed = (
        rows,
        rows,
        rows,
        P(),
        P(),
        P("dp"),
        P("dp", None),
        P("dp", None),
        P("dp", None),
        P("dp", None),
        P("dp"),
        P("dp", None),
        P("dp", None, None),
    )
    return jax.shard_map(
        body,
        mesh=mesh,
        in_specs=placed,
        out_specs=(
            rows,
            rows,
            P("dp"),
            P("dp", None),
            P("dp", None),
            P("dp", None),
            P("dp", None),
            P("dp"),
            P("dp", None),
            P("dp", None, None),
        ),
        check_vma=False,
    )
```

```python
import jax
import jax.numpy as jnp
from jax import lax
from jax.experimental import pallas as pl
from jax.experimental.pallas import tpu as pltpu
from jax.sharding import PartitionSpec as P

QUERY_HEADS = 24
KEY_VALUE_HEADS = 8
HEAD = 64
PAIR_TOK = 1152
MEMBERS = 4
LANE = 128
TILE = 384
KEYROWS = 128
UNIT = PAIR_TOK // KEYROWS // 1
eps_norm = 1e-06
rope_base = 10000.0
NEG = -1e30
BF = jnp.bfloat16
F32 = jnp.float32

Q_LOC = QUERY_HEADS // MEMBERS * HEAD
KV_LOC = KEY_VALUE_HEADS // MEMBERS * HEAD
KVH = KEY_VALUE_HEADS // MEMBERS
GROUP = QUERY_HEADS // KEY_VALUE_HEADS
QKV = Q_LOC + 2 * KV_LOC
OUT_F = LANE
OUT_B = Q_LOC - OUT_F
GAINS_AT = 64

ANY = pl.BlockSpec(memory_space=pl.ANY)
SMEM = pl.BlockSpec(memory_space=pltpu.SMEM)
VM = pl.BlockSpec(memory_space=pltpu.VMEM)


def params(megabytes):
    return pltpu.CompilerParams(vmem_limit_bytes=megabytes << 20)


def cost(flops, moved, trans=0):
    return pl.CostEstimate(flops=flops // 100, bytes_accessed=moved // 100, transcendentals=trans // 100)


def dot(a, b):
    return lax.dot_general(a, b, (((1,), (0,)), ((), ())), preferred_element_type=F32)


def dot_nt(a, b):
    return lax.dot_general(a, b, (((1,), (1,)), ((), ())), preferred_element_type=F32)


def dot_tn(a, b):
    return lax.dot_general(a, b, (((0,), (0,)), ((), ())), preferred_element_type=F32)


def pick_rows(values, order):
    count = values.shape[0]

    def kernel(order_ref, in_ref, out_ref, sems):
        copies = [
            pltpu.make_async_copy(in_ref.at[order_ref[i]], out_ref.at[i], sems.at[i])
            for i in range(count)
        ]
        for c in copies:
            c.start()
        wait_all(copies)

    return pl.pallas_call(
        kernel,
        out_shape=jax.ShapeDtypeStruct(values.shape, values.dtype),
        in_specs=[SMEM, ANY],
        out_specs=VM,
        scratch_shapes=[pltpu.SemaphoreType.DMA((count,))],
        cost_estimate=cost(0, 4 * values.size),
        name="pick",
    )(order, values)


def pick_marked(values, routes, order):
    count, block, width = values.shape
    topk = routes.shape[2]

    def kernel(order_ref, in_ref, route_ref, out_ref, sems):
        copies = [
            pltpu.make_async_copy(
                in_ref.at[order_ref[i]], out_ref.at[i, :, pl.ds(0, width)], sems.at[i]
            )
            for i in range(count)
        ]
        for c in copies:
            c.start()
        lanes = lax.broadcasted_iota(jnp.int32, (block, LANE), 1)

        def mark_one(i, carry):
            routed = route_ref[order_ref[i]]
            mark = jnp.zeros((block, LANE), F32)
            for k in range(topk):
                mark = mark + jnp.where(routed[:, k : k + 1] == lanes, 1.0, 0.0)
            out_ref[i, :, width:] = mark.astype(BF)
            return carry

        lax.fori_loop(0, count, mark_one, 0)
        wait_all(copies)

    return pl.pallas_call(
        kernel,
        out_shape=jax.ShapeDtypeStruct((count, block, width + LANE), values.dtype),
        in_specs=[SMEM, ANY, VM],
        out_specs=VM,
        scratch_shapes=[pltpu.SemaphoreType.DMA((count,))],
        cost_estimate=cost(0, 4 * values.size),
        name="pick_marked",
    )(order, values, routes)


def take_rows(dealt, first, units):
    _, block, width = dealt.shape

    def kernel(first_ref, in_ref, out_ref, sems):
        copies = []
        for t in range(units):
            source = jnp.where(t < first_ref[0], 2 * t, 2 * (t - first_ref[0]) + 1)
            copies.append(pltpu.make_async_copy(in_ref.at[source], out_ref.at[t], sems.at[t]))
            copies[-1].start()
        wait_all(copies)

    return pl.pallas_call(
        kernel,
        out_shape=jax.ShapeDtypeStruct((units, block, width), BF),
        in_specs=[SMEM, ANY],
        out_specs=VM,
        scratch_shapes=[pltpu.SemaphoreType.DMA((units,))],
        cost_estimate=cost(0, 4 * units * block * width),
        name="take_rows",
    )(first, dealt)


def spread_rows(rows, first, slots):
    units, block, width = rows.shape

    def kernel(first_ref, in_ref, out_ref):
        for i in range(slots):
            u = i // 2 if i % 2 == 0 else first_ref[0] + i // 2
            limit = first_ref[0] if i % 2 == 0 else units - first_ref[0]
            keep = i // 2 < limit

            @pl.when(keep)
            def _():
                out_ref[i] = in_ref[jnp.minimum(u, units - 1)]

            @pl.when(jnp.logical_not(keep))
            def _():
                out_ref[i] = jnp.zeros((block, width), BF)

    return pl.pallas_call(
        kernel,
        out_shape=jax.ShapeDtypeStruct((slots, block, width), BF),
        in_specs=[SMEM, VM],
        out_specs=VM,
        cost_estimate=cost(0, 4 * slots * block * width),
        name="spread_rows",
    )(first, rows)


def place_rows(values, order):
    count, block, width = values.shape

    def kernel(order_ref, in_ref, out_ref, hold, sems):
        copies = []
        for j in range(count):
            hold[j] = in_ref[j].astype(F32)
            copies.append(
                pltpu.make_async_copy(hold.at[j], out_ref.at[order_ref[j]], sems.at[j])
            )
            copies[-1].start()
        wait_all(copies)

    return pl.pallas_call(
        kernel,
        out_shape=jax.ShapeDtypeStruct(values.shape, F32),
        in_specs=[SMEM, VM],
        out_specs=ANY,
        scratch_shapes=[
            pltpu.VMEM(values.shape, F32),
            pltpu.SemaphoreType.DMA((count,)),
        ],
        cost_estimate=cost(0, 6 * values.size),
        name="place_rows",
    )(order, values)


def place_experts(places, shares, weight, lo, count, split, per, total):
    rows = shares[0].shape[0]
    width = shares[0].shape[1] // count
    half = width // 2
    used = 2 * width // 3

    def kernel(*refs):
        tab = refs[0]
        ins = refs[1 : 1 + MEMBERS]
        weight_ref = refs[1 + MEMBERS]
        out, gain, hold, w_v, sems, sem_w = refs[-6:]
        loads = []
        for k in range(MEMBERS):
            for e in range(count):
                at = k * count + e
                loads.append(
                    pltpu.make_async_copy(
                        weight_ref.at[tab[k] * per + lo + e, :, pl.ds(0, used)],
                        w_v.at[tab[k] * count + e],
                        sem_w.at[at],
                    )
                )
                loads[-1].start()
        copies = []
        for k in range(MEMBERS):
            for e in range(count):
                at = tab[k] * count + e
                for side in range(2):
                    col = (side * count + e) * half if split else e * width + side * half
                    hold[at, :, side * half : (side + 1) * half] = ins[k][
                        :, col : col + half
                    ].astype(F32)
                copies.append(
                    pltpu.make_async_copy(
                        hold.at[at], out.at[tab[k] * per + lo + e], sems.at[k * count + e]
                    )
                )
                copies[-1].start()
        wait_all(loads)
        gain[...] = jnp.zeros_like(gain)

        def add(at, carry):
            total = jnp.zeros((rows, LANE), F32)
            for c in range(used // LANE):
                cols = slice(c * LANE, (c + 1) * LANE)
                total = total + w_v[at, :, cols].astype(BF).astype(F32) * hold[at, :, cols]
            gain[...] += total
            return carry

        lax.fori_loop(0, MEMBERS * count, add, 0)
        wait_all(copies)

    before = [] if total is None else [total]
    return pl.pallas_call(
        kernel,
        out_shape=(
            jax.ShapeDtypeStruct((MEMBERS * per, rows, width), F32),
            jax.ShapeDtypeStruct((rows, LANE), F32),
        ),
        in_specs=[SMEM] + [VM] * MEMBERS + [ANY] * (1 + len(before)),
        out_specs=(ANY, VM),
        input_output_aliases={2 + MEMBERS: 0} if before else {},
        scratch_shapes=[
            pltpu.VMEM((MEMBERS * count, rows, width), F32),
            pltpu.VMEM((MEMBERS * count, rows, used), F32),
            pltpu.SemaphoreType.DMA((MEMBERS * count,)),
            pltpu.SemaphoreType.DMA((MEMBERS * count,)),
        ],
        compiler_params=params(40),
        cost_estimate=cost(0, 6 * MEMBERS * count * rows * width),
        name="place_experts",
    )(places, *shares, weight, *before)


def start_rows(refs, scratch, table, at, sems):
    copies = []
    for k in range(MEMBERS):
        place = pl.multiple_of(table[at + k] * 32, 32)
        copies.append(
            pltpu.make_async_copy(refs[k], scratch.at[:, pl.ds(place, 32), :], sems.at[k])
        )
        copies[-1].start()
    return copies


def start_weights(refs_f, refs_b, wf, wb, scratch, table, sems):
    copies = []
    n = len(refs_f)
    for s in range(n):
        rows = refs_f[s].shape[0]
        row_f = pl.multiple_of(table[s], 16)
        row_b = pl.multiple_of(table[n + s], 16)
        copies.append(
            pltpu.make_async_copy(
                refs_f[s].at[:, pl.ds(0, wf)],
                scratch.at[pl.ds(row_f, rows), pl.ds(0, wf)],
                sems.at[s],
            )
        )
        copies.append(
            pltpu.make_async_copy(
                refs_b[s].at[:, pl.ds(0, wb)],
                scratch.at[pl.ds(row_b, rows), pl.ds(wf, wb)],
                sems.at[n + s],
            )
        )
    for c in copies:
        c.start()
    return copies


def start_out(refs, scratch, table, at, sems):
    copies = []
    for k in range(MEMBERS):
        copies.append(pltpu.make_async_copy(refs[k], scratch.at[table[at + k]], sems.at[k]))
        copies[-1].start()
    return copies


def store_members(out, table, at, tiles, values, cols=None):
    per = values.shape[0] // KEYROWS
    shaped = values.reshape(per, KEYROWS, values.shape[1])
    for j in range(MEMBERS):
        piece = shaped[:, j * 32 : (j + 1) * 32]
        if cols is None:
            out[table[at + j], tiles] = piece
        else:
            out[table[at + j], tiles, :, cols] = piece


def wait_all(copies):
    for c in copies:
        c.wait()


def turn(values, cosine, sine):
    width = values.shape[1]
    lanes = lax.broadcasted_iota(jnp.int32, values.shape, 1)
    low = pltpu.roll(values, width - HEAD // 2, 1)
    high = pltpu.roll(values, HEAD // 2, 1)
    swapped = jnp.where(lanes % HEAD < HEAD // 2, low, high)
    reps = width // LANE
    return values * jnp.concatenate([cosine] * reps, 1) + swapped * jnp.concatenate([sine] * reps, 1)


def bias_for(t, extent, first_len):
    gi = lax.broadcasted_iota(jnp.int32, (KEYROWS, extent), 0) + t * KEYROWS
    gj = lax.broadcasted_iota(jnp.int32, (KEYROWS, extent), 1)
    allowed = (gj <= gi) & ((gi < first_len) | (gj >= first_len))
    return jnp.concatenate([jnp.where(allowed, 0.0, NEG)] * GROUP, 0)


def attention_forward(table, base, af, ab, rows_x, cosine, sine, width):
    n = len(af)
    tiles = PAIR_TOK // TILE
    per = TILE // KEYROWS
    nt = PAIR_TOK // KEYROWS
    chunk = af[0].shape[0]

    def kernel(*refs):
        tab = refs[0]
        f_refs = refs[1 : 1 + n]
        b_refs = refs[1 + n : 1 + 2 * n]
        x_refs = refs[1 + 2 * n : 5 + 2 * n]
        cos_ref, sin_ref = refs[5 + 2 * n : 7 + 2 * n]
        a_out, q_out, k_out, v_out, heads, small, gains = refs[7 + 2 * n : 14 + 2 * n]
        w_v, sem_x, sem_w, sem_s = refs[14 + 2 * n :]
        cs = []
        for s in range(n):
            row = pl.ds(pl.multiple_of(tab[s], 16), chunk)
            cs.append(
                pltpu.make_async_copy(
                    f_refs[s].at[:, pl.ds(Q_LOC + OUT_F, LANE)], small.at[row, :], sem_s.at[s]
                )
            )
            cs[-1].start()
        cw = start_weights(f_refs, b_refs, Q_LOC, 2 * KV_LOC, w_v, tab, sem_w)
        cx = start_rows(x_refs, a_out, tab, base, sem_x)
        wait_all(cs)
        pick = lax.broadcasted_iota(jnp.int32, (8, LANE), 1)
        pick = pick == lax.broadcasted_iota(jnp.int32, (8, LANE), 0) + GAINS_AT
        gains[...] = dot_nt(pick.astype(F32).astype(BF), small[...])
        wait_all(cw)
        wait_all(cx)
        first_len = tab[base + 8]

        def project(i, carry):
            at = pl.ds(i * per, per)
            x = a_out[at].reshape(TILE, width).astype(F32)
            scale = lax.rsqrt(jnp.mean(x * x, axis=-1, keepdims=True) + eps_norm)
            block = (x * scale * gains[0:1, :]).astype(BF)
            a_out[at] = block.reshape(per, KEYROWS, width)
            y = dot(block, w_v[...])
            rows = pl.ds(pl.multiple_of(i * TILE, TILE), TILE)
            turned = turn(y[:, : Q_LOC + KV_LOC], cos_ref[rows, :], sin_ref[rows, :])
            q = (turned[:, :Q_LOC] * 0.125).astype(BF)
            k = turned[:, Q_LOC:].astype(BF)
            v = y[:, Q_LOC + KV_LOC :].astype(BF)
            for j in range(KVH):
                k_out[j, rows, :] = k[:, j * HEAD : (j + 1) * HEAD]
                v_out[j, rows, :] = v[:, j * HEAD : (j + 1) * HEAD]
                for h in range(GROUP):
                    c = (j * GROUP + h) * HEAD
                    for r in range(per):
                        q_out[j, i * per + r, h * KEYROWS : (h + 1) * KEYROWS, :] = q[
                            r * KEYROWS : (r + 1) * KEYROWS, c : c + HEAD
                        ]
            return carry

        lax.fori_loop(0, tiles, project, 0)
        for low_t in range(0, nt, 2):
            high_t = min(low_t + 2, nt)
            extent = high_t * KEYROWS

            def attend(t, carry, extent=extent):
                bias = bias_for(t, extent, first_len)
                mixed = []
                for j in range(KVH):
                    s = dot_nt(q_out[j, t], k_out[j, :extent, :]) + bias
                    top = jnp.max(s, axis=1, keepdims=True)
                    p = jnp.exp(s - top)
                    total = jnp.sum(p, axis=1, keepdims=True)
                    o = dot(p.astype(BF), v_out[j, :extent, :]) / total
                    mixed += [o[h * KEYROWS : (h + 1) * KEYROWS] for h in range(GROUP)]
                rows = pl.ds(pl.multiple_of(t * KEYROWS, KEYROWS), KEYROWS)
                heads[rows, :] = jnp.concatenate(mixed, 1).astype(BF)
                return carry

            lax.fori_loop(low_t, high_t, attend, 0)

    return pl.pallas_call(
        kernel,
        out_shape=(
            jax.ShapeDtypeStruct((nt, KEYROWS, width), BF),
            jax.ShapeDtypeStruct((KVH, nt, GROUP * KEYROWS, HEAD), BF),
            jax.ShapeDtypeStruct((KVH, PAIR_TOK, HEAD), BF),
            jax.ShapeDtypeStruct((KVH, PAIR_TOK, HEAD), BF),
            jax.ShapeDtypeStruct((PAIR_TOK, Q_LOC), BF),
            jax.ShapeDtypeStruct((width, LANE), BF),
            jax.ShapeDtypeStruct((8, width), F32),
        ),
        in_specs=[SMEM] + [ANY] * (2 * n + 4) + [VM, VM],
        out_specs=(VM,) * 7,
        scratch_shapes=[
            pltpu.VMEM((width, QKV), BF),
            pltpu.SemaphoreType.DMA((4,)),
            pltpu.SemaphoreType.DMA((2 * n,)),
            pltpu.SemaphoreType.DMA((n,)),
        ],
        compiler_params=params(48),
        cost_estimate=cost(12 * 10**9, 14 << 20, 5 * 10**6),
        name="attention_forward",
    )(table, *af, *ab, *rows_x, cosine, sine)


def project_out(table, base, heads, wout, width):
    tiles = PAIR_TOK // TILE
    per = TILE // KEYROWS
    nt = PAIR_TOK // KEYROWS

    def kernel(tab, heads, *refs):
        o_refs, (part, o_v, sem_o) = refs[:MEMBERS], refs[MEMBERS:]
        wait_all(start_out(o_refs, o_v, tab, base + 4, sem_o))
        for i in range(tiles):
            h = heads[i * TILE : (i + 1) * TILE, :]
            for j in range(MEMBERS):
                y = dot(h, o_v[j]).astype(BF)
                store_members(
                    part, tab, base, pl.ds(i * per, per), y, pl.ds(j * Q_LOC, Q_LOC)
                )

    return pl.pallas_call(
        kernel,
        out_shape=jax.ShapeDtypeStruct((MEMBERS, nt, 32, width), BF),
        in_specs=[SMEM, VM] + [ANY] * MEMBERS,
        out_specs=VM,
        scratch_shapes=[
            pltpu.VMEM((MEMBERS, Q_LOC, Q_LOC), BF),
            pltpu.SemaphoreType.DMA((4,)),
        ],
        compiler_params=params(24),
        cost_estimate=cost(2 * 10**9, 6 << 20),
        name="project_out",
    )(table, heads, *wout)


def attention_backward(table, base, af, ab, rows_m, wout, q, k, v, cosine, sine, width):
    n = len(af)
    tiles = PAIR_TOK // TILE
    per = TILE // KEYROWS
    nt = PAIR_TOK // KEYROWS
    wide = rows_m[0].shape[2]

    def kernel(*refs):
        tab = refs[0]
        f_refs = refs[1 : 1 + n]
        b_refs = refs[1 + n : 1 + 2 * n]
        m_refs = refs[1 + 2 * n : 5 + 2 * n]
        o_refs = refs[5 + 2 * n : 9 + 2 * n]
        q_ref, k_ref, v_ref, cos_ref, sin_ref = refs[9 + 2 * n : 14 + 2 * n]
        da, dqkv = refs[14 + 2 * n : 16 + 2 * n]
        m_v, w_v, o_v, dh_s, dq_s, dk_s, dv_s, sem_m, sem_w, sem_o = refs[16 + 2 * n :]
        cm = start_rows(m_refs, m_v, tab, base, sem_m)
        co = start_out(o_refs, o_v, tab, base + 4, sem_o)
        cw = start_weights(f_refs, b_refs, Q_LOC, 2 * KV_LOC, w_v, tab, sem_w)
        dk_s[...] = jnp.zeros_like(dk_s)
        dv_s[...] = jnp.zeros_like(dv_s)
        wait_all(co)
        wait_all(cm)
        first_len = tab[base + 8]

        def heads_back(i, carry):
            total = None
            for j in range(MEMBERS):
                block = m_v[pl.ds(i * per, per), :, j * Q_LOC : (j + 1) * Q_LOC]
                y = dot_nt(block.reshape(TILE, Q_LOC), o_v[j])
                total = y if total is None else total + y
            total = total.astype(BF)
            for j in range(KVH):
                for h in range(GROUP):
                    c = (j * GROUP + h) * HEAD
                    for r in range(per):
                        dh_s[j, i * per + r, h * KEYROWS : (h + 1) * KEYROWS, :] = total[
                            r * KEYROWS : (r + 1) * KEYROWS, c : c + HEAD
                        ]
            return carry

        lax.fori_loop(0, tiles, heads_back, 0)
        for low_t in range(0, nt, 2):
            high_t = min(low_t + 2, nt)
            extent = high_t * KEYROWS

            def attend(t, carry, extent=extent):
                bias = bias_for(t, extent, first_len)
                for j in range(KVH):
                    qb = q_ref[j, t]
                    db = dh_s[j, t]
                    kb = k_ref[j, :extent, :]
                    s = dot_nt(qb, kb) + bias
                    top = jnp.max(s, axis=1, keepdims=True)
                    p = jnp.exp(s - top)
                    p = p * (1.0 / jnp.sum(p, axis=1, keepdims=True))
                    dp = dot_nt(db, v_ref[j, :extent, :])
                    prod = p * dp
                    delta = jnp.sum(prod, axis=1, keepdims=True)
                    ds = (prod - p * delta).astype(BF)
                    dq_s[j, t] = dot(ds, kb) * 0.125
                    dk_s[j, :extent, :] += dot_tn(ds, qb)
                    dv_s[j, :extent, :] += dot_tn(p.astype(BF), db)
                return carry

            lax.fori_loop(low_t, high_t, attend, 0)
        wait_all(cw)

        def inputs_back(i, carry):
            rows = pl.ds(pl.multiple_of(i * TILE, TILE), TILE)
            cols = []
            for j in range(KVH):
                for h in range(GROUP):
                    cols.append(
                        jnp.concatenate(
                            [
                                dq_s[j, i * per + r, h * KEYROWS : (h + 1) * KEYROWS, :]
                                for r in range(per)
                            ],
                            0,
                        )
                    )
            cols += [dk_s[j, rows, :] for j in range(KVH)]
            joined = jnp.concatenate(cols, 1).astype(BF).astype(F32)
            turned = turn(joined, cos_ref[rows, :], -sin_ref[rows, :])
            value = jnp.concatenate([dv_s[j, rows, :] for j in range(KVH)], 1)
            out = jnp.concatenate([turned, value], 1).astype(BF)
            dqkv[rows, :] = out
            y = dot_nt(out, w_v[...]).astype(BF)
            store_members(da, tab, base, pl.ds(i * per, per), y)
            return carry

        lax.fori_loop(0, tiles, inputs_back, 0)

    return pl.pallas_call(
        kernel,
        out_shape=(
            jax.ShapeDtypeStruct((MEMBERS, nt, 32, width), BF),
            jax.ShapeDtypeStruct((PAIR_TOK, QKV), BF),
        ),
        in_specs=[SMEM] + [ANY] * (2 * n + 8) + [VM] * 5,
        out_specs=(VM,) * 2,
        scratch_shapes=[
            pltpu.VMEM((nt, KEYROWS, wide), BF),
            pltpu.VMEM((width, QKV), BF),
            pltpu.VMEM((MEMBERS, Q_LOC, Q_LOC), BF),
            pltpu.VMEM((KVH, nt, GROUP * KEYROWS, HEAD), BF),
            pltpu.VMEM((KVH, nt, GROUP * KEYROWS, HEAD), F32),
            pltpu.VMEM((KVH, PAIR_TOK, HEAD), F32),
            pltpu.VMEM((KVH, PAIR_TOK, HEAD), F32),
            pltpu.SemaphoreType.DMA((4,)),
            pltpu.SemaphoreType.DMA((2 * n,)),
            pltpu.SemaphoreType.DMA((4,)),
        ],
        compiler_params=params(56),
        cost_estimate=cost(20 * 10**9, 16 << 20, 5 * 10**6),
        name="attention_backward",
    )(table, *af, *ab, *rows_m, *wout, q, k, v, cosine, sine)


def attention_grads(table, base, a_all, rows_b, rows_m, heads, dqkv, width, n):
    nt = PAIR_TOK // KEYROWS
    step = Q_LOC
    chunk = width // n
    owners = step // chunk
    wide = rows_m[0].shape[2]
    wide_f = Q_LOC + OUT_F
    wide_b = 2 * KV_LOC + OUT_B + LANE

    def kernel(*refs):
        tab = refs[0]
        b_refs, m_refs = refs[1:5], refs[5:9]
        a_ref, heads_ref, d_ref = refs[9:12]
        gf, gb, go = refs[12:15]
        b_v, m_v, sem_b, sem_m = refs[15:]
        j = pl.program_id(0)

        @pl.when(j == 0)
        def _():
            cb = start_rows(b_refs, b_v, tab, base, sem_b)
            cm = start_rows(m_refs, m_v, tab, base, sem_m)
            wait_all(cb)
            wait_all(cm)

        cols = pl.ds(pl.multiple_of(j * step, step), step)
        a = a_ref[...].reshape(PAIR_TOK, step)
        gq = dot_tn(a, d_ref[...]).astype(BF)
        b = b_v[:, :, cols].reshape(PAIR_TOK, step)
        gr = dot_tn(b, m_v[:, :, width:].reshape(PAIR_TOK, LANE)).astype(BF)
        for h in range(owners):
            rows = slice(h * chunk, (h + 1) * chunk)
            to_f = tab[base + 10 + j * owners + h]
            to_b = tab[base + 10 + n + j * owners + h]
            gf[to_f, :, :Q_LOC] = gq[rows, :Q_LOC]
            gb[to_b, :, : 2 * KV_LOC] = gq[rows, Q_LOC:]
            gb[to_b, :, 2 * KV_LOC + OUT_B :] = gr[rows, :]
        m = m_v[:, :, cols].reshape(PAIR_TOK, step)
        go[tab[base + 4 + j]] = dot_tn(heads_ref[...], m).astype(BF)

    return pl.pallas_call(
        kernel,
        grid=(width // step,),
        out_shape=(
            jax.ShapeDtypeStruct((n, chunk, wide_f), BF),
            jax.ShapeDtypeStruct((n, chunk, wide_b), BF),
            jax.ShapeDtypeStruct((MEMBERS, Q_LOC, Q_LOC), BF),
        ),
        in_specs=[SMEM]
        + [ANY] * 8
        + [
            pl.BlockSpec((nt, KEYROWS, step), lambda j: (0, 0, j)),
            pl.BlockSpec((PAIR_TOK, Q_LOC), lambda j: (0, 0)),
            pl.BlockSpec((PAIR_TOK, QKV), lambda j: (0, 0)),
        ],
        out_specs=(
            pl.BlockSpec((n, chunk, wide_f), lambda j: (0, 0, 0)),
            pl.BlockSpec((n, chunk, wide_b), lambda j: (0, 0, 0)),
            pl.BlockSpec((MEMBERS, Q_LOC, Q_LOC), lambda j: (0, 0, 0)),
        ),
        scratch_shapes=[
            pltpu.VMEM((nt, KEYROWS, width), BF),
            pltpu.VMEM((nt, KEYROWS, wide), BF),
            pltpu.SemaphoreType.DMA((4,)),
            pltpu.SemaphoreType.DMA((4,)),
        ],
        compiler_params=params(48),
        cost_estimate=cost(4 * 10**9, 16 << 20),
        name="attention_grads",
    )(table, *rows_b, *rows_m, a_all, heads, dqkv)


def pack_out_grads(table, base, pieces, part_f, part_b):
    n, chunk, wide_f = part_f.shape
    wide_b = part_b.shape[2]
    owners = n // MEMBERS

    def kernel(*refs):
        tab = refs[0]
        ins = refs[1 : 1 + MEMBERS]
        out_f, out_b, sems = refs[3 + MEMBERS :]
        copies = []
        for k in range(MEMBERS):
            for h in range(owners):
                owner = tab[base + 4 + k] * owners + h
                rows = pl.ds(h * chunk, chunk)
                copies.append(
                    pltpu.make_async_copy(
                        ins[k].at[rows, pl.ds(0, OUT_F)],
                        out_f.at[tab[base + 10 + owner], :, pl.ds(Q_LOC, OUT_F)],
                        sems.at[2 * (k * owners + h)],
                    )
                )
                copies.append(
                    pltpu.make_async_copy(
                        ins[k].at[rows, pl.ds(OUT_F, OUT_B)],
                        out_b.at[tab[base + 10 + n + owner], :, pl.ds(2 * KV_LOC, OUT_B)],
                        sems.at[2 * (k * owners + h) + 1],
                    )
                )
        for c in copies:
            c.start()
        wait_all(copies)

    return pl.pallas_call(
        kernel,
        out_shape=(
            jax.ShapeDtypeStruct(part_f.shape, BF),
            jax.ShapeDtypeStruct(part_b.shape, BF),
        ),
        in_specs=[SMEM] + [VM] * MEMBERS + [ANY, ANY],
        out_specs=(ANY, ANY),
        input_output_aliases={1 + MEMBERS: 0, 2 + MEMBERS: 1},
        scratch_shapes=[pltpu.SemaphoreType.DMA((2 * n,))],
        cost_estimate=cost(0, 3 << 20),
        name="pack_out_grads",
    )(table, *pieces, part_f, part_b)


def place_attention(places, shares):
    rows, width = shares[0].shape

    def kernel(*refs):
        tab = refs[0]
        ins = refs[1 : 1 + MEMBERS]
        gq, gk, gv, go, hold = refs[1 + MEMBERS :]
        for k in range(MEMBERS):
            hold[tab[k]] = ins[k][...].astype(F32)
        at = Q_LOC + OUT_F
        for j in range(MEMBERS):
            gq[:, j * Q_LOC : (j + 1) * Q_LOC] = hold[j, :, :Q_LOC]
            gk[:, j * KV_LOC : (j + 1) * KV_LOC] = hold[j, :, at : at + KV_LOC]
            gv[:, j * KV_LOC : (j + 1) * KV_LOC] = hold[j, :, at + KV_LOC : at + 2 * KV_LOC]
            go[:, j * Q_LOC : j * Q_LOC + OUT_F] = hold[j, :, Q_LOC:at]
            go[:, j * Q_LOC + OUT_F : (j + 1) * Q_LOC] = hold[j, :, at + 2 * KV_LOC :]

    return pl.pallas_call(
        kernel,
        out_shape=tuple(
            jax.ShapeDtypeStruct((rows, MEMBERS * size), F32)
            for size in (Q_LOC, KV_LOC, KV_LOC, Q_LOC)
        ),
        in_specs=[SMEM] + [VM] * MEMBERS,
        out_specs=(VM,) * 4,
        scratch_shapes=[pltpu.VMEM((MEMBERS, rows, width), F32)],
        cost_estimate=cost(0, 6 * MEMBERS * rows * width),
        name="place_attention",
    )(places, *shares)


def expert_kernel(table, base, slot, count, pieces, rows_b, rows_d, router, width, hidden, groups, ringed, offsets):
    many = len(pieces)
    n = many // 2
    half = 3 * hidden // 2
    nt = PAIR_TOK // KEYROWS
    tiles = PAIR_TOK // TILE
    per = TILE // KEYROWS
    step = TILE
    chunk = width // groups
    owners = step // chunk
    cuts = width // step
    wide = width + LANE

    def kernel(*refs):
        tab = refs[0]
        w_refs = refs[1 : 1 + many]
        b_refs = refs[1 + many : 5 + many]
        d_refs = refs[5 + many : 9 + many]
        r_ref = refs[9 + many]
        db, out = refs[10 + many : 12 + many]
        grads = refs[12 + many : 14 + many] if ringed else refs[12 + many : 13 + many]
        scratch = refs[14 + many :] if ringed else refs[13 + many :]
        w_v, b_v, d_v, dgu_v, gh_v, db_v, out_v, sem_w, sem_b, sem_d = scratch[:10]
        i = pl.program_id(0)

        def fetch(e):
            if many == 1:
                cols = pl.ds(e * 3 * hidden, 3 * hidden)
                return [pltpu.make_async_copy(w_refs[0].at[:, cols], w_v.at[e], sem_w.at[e])]
            copies = []
            for at in range(many):
                side = at // n
                rows = w_refs[at].shape[0]
                copies.append(
                    pltpu.make_async_copy(
                        w_refs[at].at[:, pl.ds(offsets[side] + e * half, half)],
                        w_v.at[
                            e,
                            pl.ds(pl.multiple_of(tab[at], 16), rows),
                            pl.ds(side * half, half),
                        ],
                        sem_w.at[e * many + at],
                    )
                )
            return copies

        @pl.when(i == 0)
        def _():
            cb = start_rows(b_refs, b_v, tab, base, sem_b)
            for e in range(count):
                for c in fetch(e):
                    c.start()
            cd = start_rows(d_refs, d_v, tab, base, sem_d)
            wait_all(cb)
            wait_all(cd)

        @pl.when(i < tiles)
        def _():
            at = pl.ds(i * per, per)
            b = b_v[at].reshape(TILE, width)
            mark = d_v[at, :, width:].reshape(TILE, LANE).astype(F32)
            lanes = lax.broadcasted_iota(jnp.int32, (TILE, LANE), 1)
            logits = jnp.where(mark > 0.0, dot(b, r_ref[...]), NEG)
            top = jnp.max(logits, axis=1, keepdims=True)
            weight = jnp.where(mark > 0.0, jnp.exp(logits - top), 0.0)
            gates = weight / jnp.sum(weight, axis=1, keepdims=True)
            rows = pl.ds(pl.multiple_of(i * TILE, TILE), TILE)

            def one(e, extra):
                for c in range(count):

                    @pl.when((i == 0) & (e == c))
                    def _(c=c):
                        wait_all(fetch(c))

                expert = tab[base + 9] + slot + e
                b = b_v[at].reshape(TILE, width)
                dy = d_v[at, :, :width].reshape(TILE, width)
                gate = jnp.sum(jnp.where(lanes == expert, gates, 0.0), axis=1, keepdims=True)
                gu = dot(b, w_v[e, :, : 2 * hidden])
                back = dot(dy, w_v[e, :, 2 * hidden :])
                g = gu[:, :hidden]
                u = gu[:, hidden:]
                sig = 1.0 / (1.0 + jnp.exp(-g))
                act = g * sig
                hb = (act * u).astype(BF)
                hf = hb.astype(F32)
                dgate = jnp.sum(hf * back, axis=1, keepdims=True)
                gh = (hf * gate).astype(BF)
                dh = back * gate
                dg = dh * u * (sig * (1.0 + g * (1.0 - sig)))
                dgu = jnp.concatenate([dg, dh * act], 1).astype(BF)
                dgu_v[e, rows, :] = dgu
                gh_v[e, rows, :] = gh
                y = dot_nt(dgu, w_v[e, :, : 2 * hidden])
                z = dot_nt(gh, w_v[e, :, 2 * hidden :])

                @pl.when(e == 0)
                def _():
                    db_v[...] = y
                    out_v[...] = z

                @pl.when(e > 0)
                def _():
                    db_v[...] += y
                    out_v[...] += z

                high = dgate.astype(BF).astype(F32)
                low = dgate - high
                return extra + jnp.where(
                    lanes == expert, high, jnp.where(lanes == expert + LANE // 2, low, 0.0)
                )

            extra = lax.fori_loop(0, count, one, jnp.zeros((TILE, LANE), F32))
            whole = slice(None)
            store_members(db, tab, base, whole, db_v[...].astype(BF), pl.ds(0, width))
            store_members(db, tab, base, whole, extra.astype(BF), pl.ds(width, LANE))
            store_members(out, tab, base, whole, out_v[...].astype(BF))

        @pl.when(i >= tiles)
        def _():
            cols = pl.ds(pl.multiple_of((i - tiles) * step, step), step)
            b = b_v[:, :, cols].reshape(PAIR_TOK, step)
            dy = d_v[:, :, cols].reshape(PAIR_TOK, step)
            if not ringed:
                grads[0][:, : 2 * hidden] = dot_tn(b, dgu_v[0]).astype(BF)
                grads[0][:, 2 * hidden :] = dot_tn(dy, gh_v[0]).astype(BF)
            else:
                g_v, sem_g = scratch[10:]
                j = i - tiles
                for e in range(count):
                    one = dot_tn(b, dgu_v[e]).astype(BF)
                    g_v[0, j, :, e * half : (e + 1) * half] = one[:, :half]
                    g_v[1, j, :, e * half : e * half + 2 * hidden - half] = one[:, half:]
                    two = dot_tn(dy, gh_v[e]).astype(BF)
                    g_v[1, j, :, e * half + 2 * hidden - half : (e + 1) * half] = two

                def send(j, h, side):
                    owner = j * owners + h
                    return pltpu.make_async_copy(
                        g_v.at[side, j, pl.ds(h * chunk, chunk)],
                        grads[side].at[tab[base + 10 + side * groups + owner]],
                        sem_g.at[side * groups + owner],
                    )

                for h in range(owners):
                    for side in range(2):
                        send(j, h, side).start()

                @pl.when(j == cuts - 1)
                def _():
                    for t in range(cuts):
                        for h in range(owners):
                            for side in range(2):
                                send(t, h, side).wait()

    if ringed:
        grad_specs = (ANY, ANY)
        grad_shapes = (jax.ShapeDtypeStruct((groups, chunk, count * half), BF),) * 2
        more = [
            pltpu.VMEM((2, cuts, step, count * half), BF),
            pltpu.SemaphoreType.DMA((2 * groups,)),
        ]
    else:
        grad_specs = (
            pl.BlockSpec((step, 3 * hidden), lambda i: (jnp.maximum(i - tiles, 0), 0)),
        )
        grad_shapes = (jax.ShapeDtypeStruct((width, 3 * hidden), BF),)
        more = []
    return pl.pallas_call(
        kernel,
        grid=(tiles + cuts,),
        out_shape=(
            jax.ShapeDtypeStruct((MEMBERS, nt, 32, wide), BF),
            jax.ShapeDtypeStruct((MEMBERS, nt, 32, width), BF),
        )
        + grad_shapes,
        in_specs=[SMEM] + [ANY] * (many + 8) + [pl.BlockSpec((width, LANE), lambda i: (0, 0))],
        out_specs=(
            pl.BlockSpec(
                (MEMBERS, per, 32, wide), lambda i: (0, jnp.minimum(i, tiles - 1), 0, 0)
            ),
            pl.BlockSpec(
                (MEMBERS, per, 32, width), lambda i: (0, jnp.minimum(i, tiles - 1), 0, 0)
            ),
        )
        + grad_specs,
        scratch_shapes=[
            pltpu.VMEM((count, width, 3 * hidden), BF),
            pltpu.VMEM((nt, KEYROWS, width), BF),
            pltpu.VMEM((nt, KEYROWS, wide), BF),
            pltpu.VMEM((count, PAIR_TOK, 2 * hidden), BF),
            pltpu.VMEM((count, PAIR_TOK, hidden), BF),
            pltpu.VMEM((TILE, width), F32),
            pltpu.VMEM((TILE, width), F32),
            pltpu.SemaphoreType.DMA((count * many,)),
            pltpu.SemaphoreType.DMA((4,)),
            pltpu.SemaphoreType.DMA((4,)),
        ]
        + more,
        compiler_params=params(58),
        cost_estimate=cost(17 * 10**9 * count, (12 + 14 * count) << 20, 10**6 * count),
        name="expert",
    )(table, *pieces, *rows_b, *rows_d, router)


def turn_out_weight(places, af, ab):
    n = len(af)
    rows = af[0].shape[0]

    def kernel(*refs):
        tab = refs[0]
        f_refs = refs[1 : 1 + n]
        b_refs = refs[1 + n : 1 + 2 * n]
        out, sems = refs[1 + 2 * n :]
        copies = []
        for s in range(n):
            at = pl.ds(pl.multiple_of(tab[n + s], 16), rows)
            copies.append(
                pltpu.make_async_copy(
                    f_refs[s].at[:, pl.ds(Q_LOC, OUT_F)],
                    out.at[tab[s], at, pl.ds(0, OUT_F)],
                    sems.at[s],
                )
            )
            at = pl.ds(pl.multiple_of(tab[3 * n + s], 16), rows)
            copies.append(
                pltpu.make_async_copy(
                    b_refs[s].at[:, pl.ds(2 * KV_LOC, OUT_B)],
                    out.at[tab[2 * n + s], at, pl.ds(OUT_F, OUT_B)],
                    sems.at[n + s],
                )
            )
        for c in copies:
            c.start()
        wait_all(copies)

    return pl.pallas_call(
        kernel,
        out_shape=jax.ShapeDtypeStruct((MEMBERS, Q_LOC, Q_LOC), BF),
        in_specs=[SMEM] + [ANY] * (2 * n),
        out_specs=VM,
        scratch_shapes=[pltpu.SemaphoreType.DMA((2 * n,))],
        cost_estimate=cost(0, 3 << 20),
        name="turn_out_weight",
    )(places, *af, *ab)


def ring_place(index, n):
    return jnp.where(index % 2 == 0, index // 2, n - 1 - index // 2)


def ring_index(place, n):
    return jnp.where(place < n // 2, 2 * place, 2 * (n - 1 - place) + 1)


def ring_pairs(n):
    ring = list(range(0, n, 2)) + list(range(n - 1, 0, -2))
    ahead = [(ring[i], ring[(i + 1) % n]) for i in range(n)]
    back = [(b, a) for a, b in ahead]
    return ahead, back


def after(value, *deps):
    return lax.optimization_barrier((value,) + deps)[0]


def swap(values, bits):
    return lax.ppermute(values, "seq", [(i, i ^ bits) for i in range(MEMBERS)])


def share_rows(values):
    across = swap(values, 2)
    return [values, swap(values, 1), across, swap(across, 1)]


def body(
    tokens,
    cotangent,
    routes,
    lengths,
    deal_order,
    attn_gain,
    query_weight,
    key_matrix,
    value_matrix,
    out_weight,
    moe_gain,
    router_weight,
    expert_weight,
):
    n = lax.axis_size("dp")
    group = lax.axis_index("dp")
    member = lax.axis_index("seq")
    slots, block, width = tokens.shape
    units = PAIR_TOK // (MEMBERS * block)
    local_rows = query_weight.shape[0]
    n_expert = router_weight.shape[1]
    hidden = expert_weight.shape[2] // 3
    per = n_expert // MEMBERS
    ahead, back = ring_pairs(n)
    natural = block == 32

    place = ring_place(group, n)
    steps = jnp.arange(n, dtype=jnp.int32)
    from_f = ring_index((place - steps) % n, n).astype(jnp.int32)
    from_b = ring_index((place + steps) % n, n).astype(jnp.int32)
    xors = jnp.bitwise_xor(jnp.arange(MEMBERS, dtype=jnp.int32), member)
    row_place = xors if natural else jnp.arange(MEMBERS, dtype=jnp.int32)
    first_seq = deal_order[2 * group]
    first_len = lengths[first_seq]
    first = (first_len // (MEMBERS * block)).reshape(1)
    base = 2 * n
    table = jnp.concatenate(
        [
            from_f * local_rows,
            from_b * local_rows,
            row_place,
            xors,
            jnp.stack([first_len, per * member]),
            (place - ring_place(steps, n)) % n,
            (ring_place(steps, n) - place) % n,
        ]
    ).astype(jnp.int32)
    share = n // MEMBERS
    out_places = jnp.concatenate(
        [
            jnp.bitwise_xor(from_f // share, member),
            from_f % share * local_rows,
            jnp.bitwise_xor(from_b // share, member),
            from_b % share * local_rows,
        ]
    ).astype(jnp.int32)

    sent_x = pick_rows(tokens, deal_order)
    dealt_x = lax.all_to_all(sent_x, "dp", split_axis=0, concat_axis=0, tiled=True)
    x_rows = take_rows(dealt_x, first, units)

    def cut(values, size):
        return lax.dynamic_slice_in_dim(values, member * size, size, axis=1).astype(BF)

    small = jnp.concatenate(
        [
            router_weight,
            jnp.zeros((local_rows, GAINS_AT - n_expert), F32),
            attn_gain[:, None],
            moe_gain[:, None],
            jnp.zeros((local_rows, LANE - GAINS_AT - 2), F32),
        ],
        1,
    ).astype(BF)
    out_cols = cut(out_weight, Q_LOC)
    attn_f = jnp.concatenate([cut(query_weight, Q_LOC), out_cols[:, :OUT_F], small], 1)
    attn_b = jnp.concatenate(
        [cut(key_matrix, KV_LOC), cut(value_matrix, KV_LOC), out_cols[:, OUT_F:]], 1
    )
    expert_first = expert_weight.transpose(1, 0, 2)
    expert_own = lax.dynamic_slice_in_dim(expert_first, per * member, per, axis=0).astype(BF)

    def rows_of(chunks):
        if natural:
            return chunks
        w = chunks[0].shape[2]
        whole = jnp.zeros((units, MEMBERS, block, w), BF)
        for k in range(MEMBERS):
            whole = lax.dynamic_update_slice(whole, chunks[k][:, None], (0, xors[k], 0, 0))
        whole = whole.reshape(PAIR_TOK // KEYROWS, MEMBERS, 32, w)
        return [whole[:, j] for j in range(MEMBERS)]

    def scatter_parts(parts):
        if natural:
            shaped = parts
        else:
            shaped = []
            for p in parts:
                rows = p.transpose(1, 0, 2, 3).reshape(units, MEMBERS, block, p.shape[3])
                shaped.append(
                    [
                        lax.dynamic_index_in_dim(rows, xors[k], axis=1, keepdims=False)
                        for k in range(MEMBERS)
                    ]
                )

        def part(k):
            total = None
            for p in shaped:
                one = p[k].astype(F32)
                total = one if total is None else total + one
            return total

        return part

    def scatter_near(part, *deps):
        far = swap(after(part(3).astype(BF), *deps), 1)
        near = swap(after(part(1).astype(BF), *deps), 1)
        hop = (part(2) + far.astype(F32)).astype(BF)
        return near, hop

    def scatter_end(part, near, cross):
        return part(0) + near.astype(F32) + cross.astype(F32)

    class Gather:
        def __init__(self, f, b):
            self.fs, self.bs = [f], [b]

        def step(self, *deps):
            if len(self.fs) < n:
                self.fs.append(lax.ppermute(after(self.fs[-1], *deps), "dp", ahead))
                self.bs.append(lax.ppermute(after(self.bs[-1], *deps), "dp", back))

        def last(self, ago=1):
            return self.fs[-ago], self.bs[-ago]

        def finish(self):
            while len(self.fs) < n:
                self.step()

    class Scatter:
        def __init__(self, part_f, part_b):
            self.parts = part_f, part_b
            self.sums = part_f(1), part_b(1)
            self.at = 1

        def step(self, *deps):
            if self.at < n:
                f = lax.ppermute(after(self.sums[0], *deps), "dp", ahead)
                b = lax.ppermute(after(self.sums[1], *deps), "dp", back)
                self.at += 1
                own = [part(self.at % n) for part in self.parts]
                self.sums = tuple(
                    (got.astype(F32) + mine.astype(F32)).astype(BF)
                    for got, mine in zip((f, b), own)
                )

        def finish(self):
            while self.at < n:
                self.step()
            return self.sums

    row = jnp.arange(PAIR_TOK, dtype=jnp.int32)
    pos = row - jnp.where(row >= first_len, first_len, 0)
    freq = rope_base ** (-(jnp.arange(HEAD // 2, dtype=F32) * 2.0 / HEAD))
    angle = pos.astype(F32)[:, None] * freq[None, :]
    cosine = jnp.concatenate([jnp.cos(angle)] * 4, 1)
    sine = jnp.sin(angle)
    sine = jnp.concatenate([-sine, sine, -sine, sine], 1)

    half = 3 * hidden // 2
    ring = Gather(
        after(jnp.concatenate([attn_f, expert_own[0, :, :half]], 1), sent_x),
        after(jnp.concatenate([attn_b, expert_own[0, :, half:]], 1), sent_x),
    )
    offsets = (attn_f.shape[1], attn_b.shape[1])
    sent_d = pick_marked(after(cotangent, sent_x), routes, deal_order)
    ring.step()
    ring.step(sent_d)
    x_across, x_near = swap(x_rows, 2), swap(x_rows, 1)
    others = per - 1
    second_f = jnp.concatenate([expert_own[e, :, :half] for e in range(1, per)], 1)
    second_b = jnp.concatenate([expert_own[e, :, half:] for e in range(1, per)], 1)
    ring.step(x_rows)
    ring.step(cosine, sine)
    ring.step(x_across, second_f, second_b)
    x_far = swap(x_across, 1)
    ring.finish()
    dealt_d = lax.all_to_all(
        after(sent_d, *ring.last()), "dp", split_axis=0, concat_axis=0, tiled=True
    )
    ring_fs, ring_bs = ring.fs, ring.bs
    second = Gather(after(second_f, *ring.last()), after(second_b, *ring.last()))
    second.step()
    turned = turn_out_weight(out_places, ring_fs, ring_bs)
    wout = [turned[0]] + [swap(turned[k], k) for k in range(1, MEMBERS)]

    rows_x = [after(x_rows, turned), x_near, x_across, x_far]
    a_all, q, k, v, heads, router, gains = attention_forward(
        table, base, ring_fs, ring_bs, rows_of(rows_x), cosine, sine, width
    )
    second.step(heads)
    d_rows = take_rows(dealt_d, first, units)
    part = project_out(table, base, after(heads, d_rows, *second.last(2)), wout, width)
    gain_a = gains[0:1]
    gain_m = gains[1:2]
    mix = scatter_parts([part])
    mix_near, mix_hop = scatter_near(mix)
    mix_cross = swap(mix_hop, 2)
    second.step(mix_hop)
    middle = after(x_rows, *second.last(2)).astype(F32) + scatter_end(mix, mix_near, mix_cross)

    inverse = lax.rsqrt(jnp.mean(middle * middle, axis=-1, keepdims=True) + eps_norm)
    b_rows = (middle * inverse * gain_m).astype(BF)
    b_across, b_near = swap(b_rows, 2), swap(b_rows, 1)
    second.step(b_rows)
    d_own_rows = after(d_rows, b_rows, *second.last(2))
    d_across, d_near = swap(d_own_rows, 2), swap(d_own_rows, 1)
    second.step(b_across)
    second.finish()
    rows_b = rows_of([b_rows, b_near, b_across, swap(b_across, 1)])
    rows_d = rows_of([d_rows, d_near, d_across, swap(d_across, 1)])

    db, out, grad = expert_kernel(
        table,
        base,
        0,
        1,
        ring_fs + ring_bs,
        rows_b,
        rows_d,
        router,
        width,
        hidden,
        n,
        False,
        offsets,
    )
    dbs, outs = [db], [out]
    first_share = lax.psum_scatter(grad, "dp", scatter_dimension=0, tiled=True)
    db, out, grad_f, grad_b = expert_kernel(
        after(table, dbs[0]),
        base,
        1,
        others,
        second.fs + second.bs,
        rows_b,
        rows_d,
        router,
        width,
        hidden,
        n,
        True,
        (0, 0),
    )
    dbs.append(db)
    outs.append(out)
    shed = Scatter(lambda s: grad_f[s], lambda s: grad_b[s])
    shed.step()

    own_b = b_rows.reshape(units * block, width)
    mark = d_rows[:, :, width:].reshape(units * block, LANE).astype(F32)
    logits = dot(own_b, router)
    gates = jax.nn.softmax(jnp.where(mark > 0.0, logits, -jnp.inf), axis=-1)

    back_part = scatter_parts(dbs)
    back_near, back_hop = scatter_near(back_part)
    back_cross = swap(back_hop, 2)
    shed.step(back_hop)
    back_sum = scatter_end(back_part, back_near, back_cross).reshape(units * block, width + LANE)
    extra = back_sum[:, width:]
    dgate = extra + jnp.roll(extra, -(LANE // 2), axis=1)
    dgate = jnp.where(mark > 0.0, dgate, 0.0)
    dlogits = (gates * (dgate - jnp.sum(gates * dgate, axis=-1, keepdims=True))).astype(BF)
    db_own = back_sum[:, :width] + dot_nt(dlogits, router)
    mid_own = middle.reshape(units * block, width)
    inv_own = inverse.reshape(units * block, 1)
    d_own = d_rows[:, :, :width].reshape(units * block, width).astype(F32)
    normed = mid_own * inv_own
    scaled = db_own * gain_m
    dmiddle = d_own + inv_own * (
        scaled - normed * jnp.mean(scaled * normed, axis=-1, keepdims=True)
    )
    dmix = jnp.concatenate([dmiddle.astype(BF), dlogits], 1).reshape(units, block, width + LANE)
    m_across, m_near = swap(dmix, 2), swap(dmix, 1)
    shed.step(dmix)
    out_part = scatter_parts(outs)
    out_near, out_hop = scatter_near(out_part, dmix)
    m_far = swap(m_across, 1)
    out_cross = swap(after(out_hop, m_across), 2)
    shed.step(m_across)
    result = middle + scatter_end(out_part, out_near, out_cross)
    sent_out = spread_rows(result.astype(BF), first, slots)
    back_out = lax.all_to_all(sent_out, "dp", split_axis=0, concat_axis=0, tiled=True)
    rows_m = rows_of([after(dmix, sent_out, first_share, *shed.sums), m_near, m_across, m_far])
    first_shares = share_rows(first_share)

    da, dqkv = attention_backward(
        table, base, ring_fs, ring_bs, rows_m, wout, q, k, v, cosine, sine, width
    )
    shed.step(da)
    half_f, half_b, gout = attention_grads(
        table, base, a_all, rows_b, rows_m, heads, dqkv, width, n
    )
    da_part = scatter_parts([da])
    da_near, da_hop = scatter_near(da_part, back_out, gout)
    da_cross = swap(da_hop, 2)
    gout = after(gout, da_cross)
    pieces = [gout[0]] + [swap(gout[kk], kk) for kk in range(1, MEMBERS)]
    full_f, full_b = pack_out_grads(table, base, pieces, half_f, half_b)
    da_own = scatter_end(da_part, da_near, da_cross).reshape(units * block, width)
    x_own = x_rows.reshape(units * block, width).astype(F32)
    inv_x = lax.rsqrt(jnp.mean(x_own * x_own, axis=-1, keepdims=True) + eps_norm)
    normed_x = x_own * inv_x
    scaled_x = da_own * gain_a
    grad_x = dmiddle + inv_x * (
        scaled_x - normed_x * jnp.mean(scaled_x * normed_x, axis=-1, keepdims=True)
    )

    sent_grad = spread_rows(grad_x.reshape(units, block, width).astype(BF), first, slots)
    back_grad = lax.all_to_all(sent_grad, "dp", split_axis=0, concat_axis=0, tiled=True)
    output = place_rows(after(back_out, sent_grad), deal_order)
    grad_tokens = place_rows(back_grad, deal_order)

    pair_f, pair_b = shed.finish()
    pair_share = jnp.concatenate([pair_f, pair_b], 1)
    pair_shares = share_rows(pair_share)
    grad_first, gain_first = place_experts(
        xors, first_shares, expert_first, 0, 1, False, per, None
    )
    grad_first, gain_rest = place_experts(
        xors, pair_shares, expert_first, 1, others, True, per, grad_first
    )
    full_f = after(full_f, pair_f, sent_grad)
    full_b = after(full_b, pair_b, sent_grad)
    final = Scatter(lambda s: full_f[s], lambda s: full_b[s])
    final.step()
    final.step(output)
    final.step()
    final.step()
    final.step(gain_rest)
    final.step(grad_tokens)
    share_f, share_b = final.finish()
    small_grad = share_b[:, full_b.shape[2] - LANE :]
    shares = share_rows(jnp.concatenate([share_f, share_b[:, : full_b.shape[2] - LANE]], 1))

    grad_query, grad_key, grad_value, grad_out = place_attention(xors, shares)
    grad_router = small_grad[:, :n_expert].astype(F32)
    grad_experts = grad_first.transpose(1, 0, 2)

    def low(values):
        return values.astype(BF).astype(F32)

    grad_attn_gain = (
        jnp.sum(low(query_weight) * grad_query, axis=1)
        + jnp.sum(low(key_matrix) * grad_key, axis=1)
        + jnp.sum(low(value_matrix) * grad_value, axis=1)
    ) / low(attn_gain)
    grad_moe_gain = (
        jnp.sum(gain_first + gain_rest, axis=1)
        + jnp.sum(low(router_weight) * grad_router, axis=1)
    ) / low(moe_gain)

    return (
        output,
        grad_tokens,
        grad_attn_gain,
        grad_query,
        grad_key,
        grad_value,
        grad_out,
        grad_moe_gain,
        grad_router,
        grad_experts,
    )


def solution(mesh):
    rows = P(None, ("dp", "seq"), None)
    placed = (
        rows,
        rows,
        rows,
        P(),
        P(),
        P("dp"),
        P("dp", None),
        P("dp", None),
        P("dp", None),
        P("dp", None),
        P("dp"),
        P("dp", None),
        P("dp", None, None),
    )
    return jax.shard_map(
        body,
        mesh=mesh,
        in_specs=placed,
        out_specs=(
            rows,
            rows,
            P("dp"),
            P("dp", None),
            P("dp", None),
            P("dp", None),
            P("dp", None),
            P("dp"),
            P("dp", None),
            P("dp", None, None),
        ),
        check_vma=False,
    )
```
